256 devices in a mesh: segment: 4 (over y), space: 64 (over z, x, core).
Axes of the slice: x: 4, y: 4, z: 8, core: 2. Of those that a mesh axis runs over, the one named last changes fastest.
Arguments:
- node_states: bfloat16 [2, 512, 29, 128], P(None, 'space'), may hold values from -6 to 6
- species: int32 [2, 512], P(None, 'space'), may hold values from 0 to 99
- species_table: bfloat16 [100, 128], replicated, may hold values from -6 to 6
- places: float32 [2, 3, 512], P(None, None, 'space'), may hold values from 0 to 2
- sources: int32 [2, 512, 8], P(None, 'space'), may hold values from 0 to 511, as said below
- radial_rate: float32 [4, 128], P('segment'), may hold values from 0.2 to 1.5
- zero_weight: bfloat16 [4, 896, 896], P('segment'), may hold values from -0.1875 to 0.1875
- one_weight: bfloat16 [4, 2, 768, 768], P('segment'), may hold values from -0.21875 to 0.21875
- two_weight: bfloat16 [4, 2, 640, 640], P('segment'), may hold values from -0.25 to 0.25
- read_weight: float32 [128], replicated, may hold values from -0.5 to 0.5
- energy_grad: float32 [2, 512], P(None, 'space'), may hold values from -6 to 6
Outputs:
- energies: float32 [2, 512], P(None, 'space')
- place_grads: float32 [2, 3, 512], P(None, None, 'space')
The draws below stay inside these ranges and needn't reach their ends.
Inputs may be any that keep to these rules, and one draw needn't show every extreme that they name: Each atom's 8 sources are distinct, differ from the atom, and lie in the atom's slab (index // 8) or in one of the two slabs beside it, the slabs forming a closed chain.
All inputs are finite; a program needn't handle non-finite values.
Results may differ from the reference program's by a relative error of at most 0.012.
The reference program's roundings to bfloat16 on the way (of `start` and `scaled`) count: a program that leaves them out, or rounds other values in their place, can miss the bound.
Values may be sent and summed in bfloat16 or wider, within the bound.
A program may use at most 128 MiB of HBM per device.

```python
import math
import jax
import jax.numpy as jnp
from jax import lax

C = 128
COEFS = 29
SPECIES = 100
NEIGH = 8
A_DEV = 8
BATCHES = 2
LAYERS = 4
ATOMS = 512
N_SPACE = 64


def draw_sources(key, part):
    slab_count = ATOMS // A_DEV
    window = 3 * A_DEV
    scores = jax.random.randint(key, (BATCHES, ATOMS, window), 0, 1 << 20, dtype=jnp.int32)
    scores = scores * window + jnp.arange(window, dtype=jnp.int32)[None, None, :]
    own_column = A_DEV + jnp.arange(ATOMS, dtype=jnp.int32) % A_DEV
    scores = jnp.where(jnp.arange(window, dtype=jnp.int32)[None, None, :] == own_column[None, :, None], jnp.int32(1 << 30), scores)
    chosen = jnp.argsort(scores, axis=-1, stable=True)[..., :NEIGH].astype(jnp.int32)
    home = jnp.arange(ATOMS, dtype=jnp.int32) // A_DEV
    source_slab = jnp.mod(home[None, :, None] - 1 + chosen // A_DEV, slab_count)
    return (source_slab * A_DEV + chosen % A_DEV).astype(jnp.int32)


def plant(entries, key, smallest, top_value):
    shape = entries.shape
    index_at = [jax.random.randint(jax.random.fold_in(key, axis), (), 0, shape[axis]) for axis in range(len(shape))]
    entries = entries.at[tuple(index_at)].set(smallest)
    longest = shape.index(max(shape))
    index_at[longest] = (index_at[longest] + 1) % shape[longest]
    return entries.at[tuple(index_at)].set(top_value)


def steps_of(key, shape, shards, least, largest):
    level, own = 1.0, jax.random.fold_in(key, 6)
    for position, parts in shards:
        draws = jnp.exp(jax.random.uniform(jax.random.fold_in(own, position), (parts,), jnp.float32, least / len(shards), largest / len(shards)))
        level = level * jnp.repeat(draws, shape[position] // parts).reshape([-1 if axis == position else 1 for axis in range(len(shape))])
    return level


def scatter_about(own_key, shape, deviation, limit, cuts=(), kind=jnp.bfloat16):
    loudness = steps_of(own_key, shape, cuts, -0.22, 0.18) if cuts else 1.0
    drawn = jax.random.normal(own_key, shape, jnp.float32) * deviation * loudness
    return jnp.minimum(jnp.maximum(drawn, -limit), limit).astype(kind)


def setup_inputs(seed: int = 0) -> dict:
    streams_of = jax.random.split(jax.random.key(seed), 12)
    node_states = scatter_about(streams_of[0], (BATCHES, ATOMS, COEFS, C), 1.0, 6.0, ((1, 64),))
    species = plant(jax.random.randint(streams_of[1], (BATCHES, ATOMS), 0, SPECIES), jax.random.fold_in(streams_of[1], 1), 0, SPECIES - 1).astype(jnp.int32)
    species_table = scatter_about(streams_of[2], (SPECIES, C), 1.0, 6.0)
    places = jnp.clip(2.0 * jax.random.uniform(streams_of[3], (BATCHES, 3, ATOMS), jnp.float32) ** steps_of(streams_of[3], (BATCHES, 3, ATOMS), ((2, 64),), -0.2, 0.2), 0.0, 2.0)
    sources = draw_sources(jax.random.fold_in(streams_of[11], 71), 0)
    radial_rate = jnp.clip(jnp.exp(math.log(1.5) - 2.014903 * jax.random.uniform(streams_of[5], (LAYERS, C), jnp.float32) ** steps_of(streams_of[5], (LAYERS, C), ((0, 4),), -0.2, 0.2)), 0.2, 1.5)
    zero_weight = scatter_about(streams_of[6], (LAYERS, 7 * C, 7 * C), (7 * C) ** -0.5, 0.1875, ((0, 4),))
    one_weight = scatter_about(streams_of[7], (LAYERS, 2, 6 * C, 6 * C), (6 * C) ** -0.5, 0.21875, ((0, 4),))
    two_weight = scatter_about(streams_of[8], (LAYERS, 2, 5 * C, 5 * C), (5 * C) ** -0.5, 0.25, ((0, 4),))
    read_weight = scatter_about(streams_of[9], (C,), C ** -0.5, 0.5, (), jnp.float32)
    energy_grad = scatter_about(streams_of[10], (BATCHES, ATOMS), 1.0, 6.0, ((1, 64),), jnp.float32)
    return {"node_states": node_states, "species": species, "species_table": species_table, "places": places, "sources": sources, "radial_rate": radial_rate, "zero_weight": zero_weight, "one_weight": one_weight, "two_weight": two_weight, "read_weight": read_weight, "energy_grad": energy_grad}


slab_depth = 2.0

def layer_core(picked, offset, own_states, decay_rate, weight_zero, weight_one, weight_two):
    per_slab = own_states.shape[0]
    channels = own_states.shape[2]
    edge_count = picked.shape[0]
    neighbours = edge_count // per_slab
    length = jnp.sqrt(lax.optimization_barrier(jnp.sum(offset * offset, axis=0)) + 1.0)
    planar = jnp.sqrt(offset[0] * offset[0] + offset[1] * offset[1] + 1.0)
    cos_one = (offset[0] / planar)[:, None]
    sin_one = (offset[1] / planar)[:, None]
    cos_two = cos_one * cos_one - sin_one * sin_one
    sin_two = 2.0 * cos_one * sin_one
    radial = jnp.exp(-decay_rate[None, :] * length[:, None])
    scaled = (picked * radial[:, None, :]).astype(jnp.bfloat16)
    zero_in = scaled[:, 0:7].reshape(edge_count, 7 * channels)
    zero_out = jnp.dot(zero_in, weight_zero, preferred_element_type=jnp.float32)
    one_re = scaled[:, 7:13].reshape(edge_count, 6 * channels)
    one_im = scaled[:, 13:19].reshape(edge_count, 6 * channels)
    first_re = jnp.dot(one_re, weight_one[0], preferred_element_type=jnp.float32) - jnp.dot(one_im, weight_one[1], preferred_element_type=jnp.float32)
    first_im = jnp.dot(one_re, weight_one[1], preferred_element_type=jnp.float32) + jnp.dot(one_im, weight_one[0], preferred_element_type=jnp.float32)
    turn_one_re = cos_one * first_re - sin_one * first_im
    turn_one_im = sin_one * first_re + cos_one * first_im
    two_re = scaled[:, 19:24].reshape(edge_count, 5 * channels)
    two_im = scaled[:, 24:29].reshape(edge_count, 5 * channels)
    second_re = jnp.dot(two_re, weight_two[0], preferred_element_type=jnp.float32) - jnp.dot(two_im, weight_two[1], preferred_element_type=jnp.float32)
    second_im = jnp.dot(two_re, weight_two[1], preferred_element_type=jnp.float32) + jnp.dot(two_im, weight_two[0], preferred_element_type=jnp.float32)
    turn_two_re = cos_two * second_re - sin_two * second_im
    turn_two_im = sin_two * second_re + cos_two * second_im
    factor = neighbours ** (-0.5)

    def pool_edges(values, rows):
        return (lax.optimization_barrier(jnp.sum(values.reshape(per_slab, neighbours, -1), axis=1)) * factor).reshape(per_slab, rows, channels)
    pooled_zero = pool_edges(zero_out, 7)
    pooled_one_re = pool_edges(turn_one_re, 6)
    pooled_one_im = pool_edges(turn_one_im, 6)
    pooled_two_re = pool_edges(turn_two_re, 5)
    pooled_two_im = pool_edges(turn_two_im, 5)
    signal = pooled_zero[:, 0] + lax.optimization_barrier(jnp.sum(pooled_one_re * pooled_one_re + pooled_one_im * pooled_one_im, axis=1)) + lax.optimization_barrier(jnp.sum(pooled_two_re * pooled_two_re + pooled_two_im * pooled_two_im, axis=1))
    gate = jax.nn.sigmoid(signal)[:, None, :]
    head = own_states[:, 0:1] + jax.nn.silu(signal)[:, None, :]
    others = jnp.concatenate([pooled_zero[:, 1:], pooled_one_re, pooled_one_im, pooled_two_re, pooled_two_im], axis=1)
    remainder = own_states[:, 1:] + gate * others
    return jnp.concatenate([head, remainder], axis=1)

def readout(updated, read_weight):
    return lax.optimization_barrier(jnp.sum(read_weight[None, :] * jax.nn.silu(updated[:, 0, :]), axis=1))

def slab_layer(states, places, sources, decay_rate, weight_zero, weight_one, weight_two):

    def block_pass(slab_index):
        block_rows = lax.dynamic_slice_in_dim(sources, slab_index * A_DEV, A_DEV, 0)
        flat_sources = block_rows.reshape(-1)
        picked = jnp.take(states, flat_sources, axis=0)
        targets = slab_index * A_DEV + jnp.arange(A_DEV, dtype=jnp.int32)
        target_flat = jnp.repeat(targets, NEIGH)
        window = (jnp.mod(flat_sources // A_DEV - slab_index + 1, N_SPACE) - 1).astype(jnp.float32)
        source_places = jnp.take(places, flat_sources, axis=1)
        elevation = jnp.stack([jnp.zeros_like(window), jnp.zeros_like(window), slab_depth * window])
        offset = source_places + elevation - jnp.take(places, target_flat, axis=1)
        own_states = lax.dynamic_slice_in_dim(states, slab_index * A_DEV, A_DEV, 0)
        return layer_core(picked, offset, own_states, decay_rate, weight_zero, weight_one, weight_two)
    blocks = lax.map(jax.checkpoint(block_pass), jnp.arange(N_SPACE, dtype=jnp.int32))
    return blocks.reshape(ATOMS, COEFS, C)

def reference(node_states, species, species_table, places, sources, radial_rate, zero_weight, one_weight, two_weight, read_weight, energy_grad):
    onehot = (species[..., None] == jnp.arange(SPECIES, dtype=jnp.int32)[None, None, :]).astype(jnp.float32)
    embed = jnp.einsum('bak,kc->bac', onehot, species_table.astype(jnp.float32))
    start = jnp.concatenate([node_states[:, :, 0:1].astype(jnp.float32) + embed[:, :, None, :], node_states[:, :, 1:].astype(jnp.float32)], axis=2).astype(jnp.bfloat16)

    def weighted(all_places):
        energy_list = []
        for batch_now in range(BATCHES):
            state = start[batch_now]
            updated = None
            for layer in range(LAYERS):
                updated = slab_layer(state.astype(jnp.float32), all_places[batch_now], sources[batch_now], radial_rate[layer], zero_weight[layer], one_weight[layer], two_weight[layer])
                if layer + 1 < LAYERS:
                    state = updated.astype(jnp.bfloat16)
            energy_list.append(readout(updated, read_weight))
        stacked = jnp.stack(energy_list)
        return (jnp.sum(stacked * energy_grad), stacked)
    output, pullback, energies = jax.vjp(weighted, places, has_aux=True)
    gradient = pullback(jnp.ones_like(output))[0]
    return (energies, gradient)
```

```python
import functools
import jax
import jax.numpy as jnp
from jax import lax
from jax.experimental import pallas as pl
from jax.experimental.pallas import tpu as pltpu
from jax.sharding import PartitionSpec as P

A = 8
NEIGH = 8
C = 128
BATCHES = 2
SLAB_DEPTH = 2.0
MESH = pl.DeviceIdType.MESH
F32 = jnp.float32
BF16 = jnp.bfloat16

CHUNKS = ((0, 512), (512, 768), (1280, 640))
WIDTH = 1920
UPPER = (0, 1, 2, 3, 7, 8, 9, 10, 11, 12, 19, 20, 21, 22, 23)
LOWER = (4, 5, 6, None, 13, 14, 15, 16, 17, 18, 24, 25, 26, 27, 28)
RAD, C1, S1, C2, S2, LX, LY, LZ, PLANAR = range(9)


def dot(x, y):
    return lax.dot_general(x, y, (((1,), (0,)), ((), ())), preferred_element_type=F32)


def dot_t(x, y):
    return lax.dot_general(x, y, (((1,), (1,)), ((), ())), preferred_element_type=F32)


def halves(x):
    high = x.astype(BF16).astype(F32)
    return jnp.concatenate([high, x - high], axis=0).astype(BF16)


def kernel(
    node, species, table, places, sources, rate, wz_hbm, w1_hbm, w2_hbm, read, egrad,
    out_e, out_p,
    wz, w1, w2, staging, ext, yout, scaled, pooled, signal, last_top, gmat, gtr, mask, geo, ct, du, uv, dmat,
    ownsum, hsend, hrecv, ysend, ptile, precv, ftile, frecv, grecv,
    wsem, psem_s, psem_r, fh_s, fh_r, fy_s, fy_r, bh_s, bh_r, by_s, by_r, eh_s, eh_r, ey_s, ey_r,
):
    seg = lax.axis_index("segment")
    slab = lax.axis_index("space")
    segments = lax.axis_size("segment")
    slabs = lax.axis_size("space")
    left = lax.rem(slab + slabs - 1, slabs)
    right = lax.rem(slab + 1, slabs)
    last = segments - 1
    up = lax.rem(seg + 1, segments)
    down = lax.rem(seg + segments - 1, segments)
    beside = ({"space": left}, {"space": right})
    factor = NEIGH ** (-0.5)
    lane = lax.broadcasted_iota(jnp.int32, (A, C), 1)
    row = lax.broadcasted_iota(jnp.int32, (A, C), 0)
    ownmask = jnp.where(lane == row + A, 1.0, 0.0).astype(F32)

    loads = (
        pltpu.make_async_copy(wz_hbm.at[0], wz, wsem.at[0]),
        pltpu.make_async_copy(w1_hbm.at[0], w1, wsem.at[1]),
        pltpu.make_async_copy(w2_hbm.at[0], w2, wsem.at[2]),
    )
    for load in loads:
        load.start()

    barrier = pltpu.get_barrier_semaphore()
    for target in beside:
        pl.semaphore_signal(barrier, inc=1, device_id=target, device_id_type=MESH)
    for step in range(1, segments):
        pl.semaphore_signal(
            barrier, inc=1, device_id={"segment": lax.rem(seg + step, segments)}, device_id_type=MESH
        )

    def remote(src, dst, send, recv, target):
        return pltpu.make_async_remote_copy(
            src_ref=src, dst_ref=dst, send_sem=send, recv_sem=recv, device_id=target, device_id_type=MESH
        )

    def cols(k):
        return pl.ds(CHUNKS[k][0], CHUNKS[k][1])

    def place_copy(side):
        return remote(ptile.at[side], precv.at[1 - side], psem_s.at[side], psem_r.at[side], beside[side])

    def halo_copy(b, k, side):
        return remote(
            ext.at[b, pl.ds(16, 16), cols(k)], ext.at[b, pl.ds(32 * (1 - side), 16), cols(k)],
            fh_s.at[b, k, side], fh_r.at[b, k, side], beside[side],
        )

    def up_copy(b, k):
        return remote(
            yout.at[b, :, cols(k)], ext.at[b, pl.ds(16, 16), cols(k)], fy_s.at[b, k], fy_r.at[b, k], {"segment": up}
        )

    def back_copy(b, k, side):
        return remote(
            hsend.at[b, side, :, cols(k)], hrecv.at[b, 1 - side, :, cols(k)],
            bh_s.at[b, k, side], bh_r.at[b, k, side], beside[side],
        )

    def down_copy(b, k):
        return remote(
            ysend.at[b, :, cols(k)], ct.at[b, :, cols(k)], by_s.at[b, k], by_r.at[b, k], {"segment": down}
        )

    def end_copy(side):
        return remote(ftile, frecv.at[1 - side], eh_s.at[side], eh_r.at[side], beside[side])

    def gather_copy(step):
        return remote(
            grecv.at[seg], grecv.at[seg], ey_s.at[step - 1], ey_r.at[step - 1],
            {"segment": lax.rem(seg + step, segments)},
        )

    ptile[1] = jnp.zeros((A, C), F32)
    ptile[1, 0:3, 0:A] = places[0]
    ptile[1, 3:6, 0:A] = places[1]
    ptile[1, 6:8, 0:A] = egrad[...]
    base = ptile[1]
    ptile[0] = pltpu.roll(base, 16, 1)
    own_tile = pltpu.roll(base, A, 1)

    def make_start(b):
        for atom in range(A):
            staging[atom * 32 : atom * 32 + 29, :] = node[b, atom].astype(F32)
        kind = jnp.sum(
            jnp.where(lane == row, jnp.broadcast_to(spec_tile[b : b + 1], (A, C)), 0.0), axis=1, keepdims=True
        )
        onehot = jnp.where(lane.astype(F32) == kind, 1.0, 0.0).astype(BF16)
        embed = dot(onehot[:, : table.shape[0]], table[...])
        for t in range(15):
            upper = staging[pl.ds(UPPER[t], A, stride=32), :]
            if t == 0:
                upper = upper + embed
            if LOWER[t] is None:
                lower = jnp.zeros((A, C), F32)
            else:
                lower = staging[pl.ds(LOWER[t], A, stride=32), :]
            ext[b, 16:32, t * C : (t + 1) * C] = jnp.concatenate([upper, lower], axis=0).astype(BF16)

    spec_tile = jnp.concatenate(
        [species[...].astype(F32), jnp.zeros((BATCHES, C - A), F32)], axis=1
    )

    @pl.when(seg == 0)
    def _():
        for b in range(BATCHES):
            make_start(b)

    pl.semaphore_wait(barrier, segments + 1)

    for side in range(2):
        place_copy(side).start()

    @pl.when(seg == 0)
    def _():
        for b in range(BATCHES):
            for k in range(3):
                for side in range(2):
                    halo_copy(b, k, side).start()

    lane3 = lax.broadcasted_iota(jnp.int32, (NEIGH, A, C), 2)
    lane_local = (lane3 >> 4) * A + (lane3 & 7)
    lane_part = (lane3 >> 3) & 1

    def make_index(b):
        index = sources[b]
        window = (index >> 3) - slab + 1
        window = jnp.where(window < 0, window + slabs, window)
        window = jnp.where(window >= slabs, window - slabs, window)
        local = window * A + (index & 7)
        local = jnp.concatenate([jnp.broadcast_to(local[:, j : j + 1], (A, C))[None] for j in range(NEIGH)], axis=0)
        mask[b] = jnp.where(local == lane3, 1.0, 0.0).astype(F32)
        same = local == lane_local
        picks = jnp.concatenate(
            [
                jnp.where(same & (lane_part == 0), 1.0, 0.0).astype(F32),
                jnp.where(same & (lane_part == 1), 1.0, 0.0).astype(F32),
            ],
            axis=1,
        ).reshape(2 * NEIGH * A, C)
        gmat[b] = picks[:, :48].astype(BF16)
        gtr[b] = picks.T[:48].astype(BF16)

    for b in range(BATCHES):
        make_index(b)

    for side in range(2):
        place_copy(side).wait_recv()
    around = precv[0] + own_tile + precv[1]
    elevation = jnp.where(lane < A, -SLAB_DEPTH, jnp.where(lane < 2 * A, 0.0, SLAB_DEPTH)).astype(F32)[0:1]
    rate_row = rate[...]

    def make_geometry(b):
        picks = mask[b]
        offsets = []
        for axis in range(3):
            line = around[b * 3 + axis : b * 3 + axis + 1]
            raised = line + elevation if axis == 2 else line
            there = jnp.sum(picks * raised[None], axis=2, keepdims=True)
            here = jnp.sum(ownmask * line, axis=1, keepdims=True)
            offsets.append(jnp.broadcast_to(there - here[None], (NEIGH, A, C)))
        ox, oy, oz = offsets
        length = jnp.sqrt(ox * ox + oy * oy + oz * oz + 1.0)
        planar = jnp.sqrt(ox * ox + oy * oy + 1.0)
        c1 = ox / planar
        s1 = oy / planar
        geo[b, RAD] = jnp.exp(-rate_row[None] * length)
        geo[b, C1] = c1
        geo[b, S1] = s1
        geo[b, C2] = c1 * c1 - s1 * s1
        geo[b, S2] = 2.0 * c1 * s1
        geo[b, LX] = ox / length
        geo[b, LY] = oy / length
        geo[b, LZ] = oz / length
        geo[b, PLANAR] = planar

    for b in range(BATCHES):
        make_geometry(b)

    weights = (None, w1, w2)

    def relay(b):
        @pl.when(seg > 0)
        def _():
            for k in range(3):
                up_copy(b, k).wait_recv()
                for side in range(2):
                    halo_copy(b, k, side).start()

    def forward_chunk(b, k):
        c0, n = CHUNKS[k]
        for side in range(2):
            halo_copy(b, k, side).wait_recv()
        picked = dot(gmat[b], ext[b, :, c0 : c0 + n])
        radial = geo[b, RAD]
        radial = jnp.concatenate([radial, radial], axis=1)
        if k:
            cos, sin = geo[b, (C1, C2)[k - 1]], geo[b, (S1, S2)[k - 1]]
        sums = []
        for t in range(n // C):
            part = picked[:, t * C : (t + 1) * C].reshape(NEIGH, 16, C)
            rounded = (part * radial).astype(BF16)
            scaled[b, :, c0 + t * C : c0 + (t + 1) * C] = rounded.reshape(NEIGH * 16, C)
            part = rounded.astype(F32)
            if k:
                re, im = part[:, :A], part[:, A:]
                sums.append(
                    jnp.concatenate(
                        [jnp.sum(cos * re - sin * im, axis=0), jnp.sum(sin * re + cos * im, axis=0)], axis=0
                    )
                )
            else:
                sums.append(jnp.sum(part, axis=0))
        if b == 0:
            loads[k].wait()
        if k:
            both = halves(jnp.concatenate(sums, axis=1))
            p = dot(both, weights[k][0])
            q = dot(both, weights[k][1])
            p = p[:16] + p[16:]
            q = q[:16] + q[16:]
            pooled[b, 0:8, c0 : c0 + n] = (p[:8] - q[8:]) * factor
            pooled[b, 8:16, c0 : c0 + n] = (p[8:] + q[:8]) * factor
        else:
            whole = jnp.concatenate([x[:8] for x in sums] + [x[8:] for x in sums[:3]], axis=1)
            z = dot(halves(whole), wz[...])
            z = (z[:8] + z[8:]) * factor
            pooled[b, 0:8, 0:512] = z[:, :512]
            pooled[b, 8:16, 0:384] = z[:, 512:]
            pooled[b, 8:16, 384:512] = jnp.zeros((A, C), F32)

    def forward_end(b):
        total = jnp.zeros((16, C), F32)
        for t in range(4, 15):
            value = pooled[b, :, t * C : (t + 1) * C]
            total = total + value * value
        sig = pooled[b, 0:8, 0:C] + total[:8] + total[8:]
        signal[b] = sig
        gate = jax.nn.sigmoid(sig)
        silu = sig * gate
        gate2 = jnp.concatenate([gate, gate], axis=0)
        for t in range(15):
            own = ext[b, 16:32, t * C : (t + 1) * C].astype(F32)
            added = gate2 * pooled[b, :, t * C : (t + 1) * C]
            if t == 0:
                added = jnp.concatenate([silu, added[8:]], axis=0)
            new = own + added
            if t == 0:
                last_top[b] = new[:8]
            yout[b, :, t * C : (t + 1) * C] = new.astype(BF16)

        @pl.when(seg < last)
        def _():
            for k in range(3):
                up_copy(b, k).start()

    relay(0)
    forward_chunk(0, 0)
    forward_chunk(0, 1)
    forward_chunk(0, 2)
    forward_end(0)
    relay(1)
    forward_chunk(1, 0)
    forward_chunk(1, 1)
    forward_chunk(1, 2)
    forward_end(1)

    read_row = read[...]

    def backward_head(b):
        @pl.when(seg == last)
        def _():
            top = last_top[b]
            gate = jax.nn.sigmoid(top)
            energy = jnp.sum(read_row * (top * gate), axis=1, keepdims=True)
            seed = jnp.sum(ownmask * own_tile[6 + b : 7 + b], axis=1, keepdims=True)
            ftile[6 + b : 7 + b, :] = jnp.sum(ownmask * energy, axis=0, keepdims=True)
            du[b] = jnp.zeros((16, WIDTH), F32)
            du[b, 0:8, 0:C] = seed * read_row * (gate * (1.0 + top * (1.0 - gate)))

        @pl.when(seg < last)
        def _():
            ftile[6 + b : 7 + b, :] = jnp.zeros((1, C), F32)
            for k in range(3):
                down_copy(b, k).wait_recv()
            du[b] = ct[b].astype(F32)

        sig = signal[b]
        gate = jax.nn.sigmoid(sig)
        total = jnp.zeros((16, C), F32)
        for t in range(15):
            value = du[b, :, t * C : (t + 1) * C] * pooled[b, :, t * C : (t + 1) * C]
            if t == 0:
                value = jnp.concatenate([jnp.zeros((A, C), F32), value[8:]], axis=0)
            total = total + value
        dgate = total[:8] + total[8:]
        dsig = du[b, 0:8, 0:C] * (gate * (1.0 + sig * (1.0 - gate))) + dgate * (gate * (1.0 - gate))
        return dsig, gate

    def backward_chunk(b, k, dsig, gate):
        c0, n = CHUNKS[k]
        gate2 = jnp.concatenate([gate, gate], axis=0)
        dsig2 = jnp.concatenate([dsig, dsig], axis=0)
        parts = []
        for t in range(n // C):
            at = slice(c0 + t * C, c0 + (t + 1) * C)
            part = gate2 * du[b, :, at]
            if k:
                part = part + 2.0 * pooled[b, :, at] * dsig2
            elif t == 0:
                part = jnp.concatenate([dsig, part[8:]], axis=0)
            parts.append(part * factor)
        if k:
            both = halves(jnp.concatenate(parts, axis=1))
            p = dot_t(both, weights[k][0])
            q = dot_t(both, weights[k][1])
            p = p[:16] + p[16:]
            q = q[:16] + q[16:]
            uv[b, 0:8, c0 : c0 + n] = p[:8] + q[8:]
            uv[b, 8:16, c0 : c0 + n] = p[8:] - q[:8]
        else:
            whole = jnp.concatenate([x[:8] for x in parts] + [x[8:] for x in parts[:3]], axis=1)
            z = dot_t(halves(whole), wz[...])
            z = z[:8] + z[8:]
            uv[b, 0:8, 0:512] = z[:, :512]
            uv[b, 8:16, 0:384] = z[:, 512:]
            uv[b, 8:16, 384:512] = jnp.zeros((A, C), F32)

        @pl.when(seg > 0)
        def _():
            radial = geo[b, RAD]
            if k:
                rc, rs = radial * geo[b, (C1, C2)[k - 1]], radial * geo[b, (S1, S2)[k - 1]]
            for t in range(n // C):
                at = slice(c0 + t * C, c0 + (t + 1) * C)
                u, v = uv[b, 0:8, at], uv[b, 8:16, at]
                if k:
                    upper, lower = rc * u + rs * v, rc * v - rs * u
                else:
                    upper, lower = radial * u, radial * v
                dmat[:, at] = jnp.concatenate([upper, lower], axis=1).reshape(NEIGH * 16, C).astype(BF16)
            spread = dot(gtr[b], dmat[:, c0 : c0 + n])
            hsend[b, 0, :, c0 : c0 + n] = spread[0:16].astype(BF16)
            hsend[b, 1, :, c0 : c0 + n] = spread[32:48].astype(BF16)
            for side in range(2):
                back_copy(b, k, side).start()
            ownsum[b, :, c0 : c0 + n] = spread[16:32] + du[b, :, c0 : c0 + n]

    def combine(b):
        @pl.when(seg > 0)
        def _():
            for k in range(3):
                for side in range(2):
                    back_copy(b, k, side).wait_recv()
                ysend[b, :, cols(k)] = (
                    ownsum[b, :, cols(k)]
                    + hrecv[b, 0, :, cols(k)].astype(F32)
                    + hrecv[b, 1, :, cols(k)].astype(F32)
                ).astype(BF16)
                down_copy(b, k).start()

    def coordinates(b):
        edge = [jnp.zeros((NEIGH, A, C), F32) for _ in range(3)]
        turn = [None, jnp.zeros((NEIGH, A, C), F32), jnp.zeros((NEIGH, A, C), F32)]
        for k in range(3):
            c0, n = CHUNKS[k]
            for t in range(n // C):
                at = slice(c0 + t * C, c0 + (t + 1) * C)
                part = scaled[b, :, at].astype(F32).reshape(NEIGH, 16, C)
                re, im = part[:, :A], part[:, A:]
                u, v = uv[b, 0:8, at], uv[b, 8:16, at]
                edge[k] = edge[k] + (re * u + im * v)
                if k:
                    turn[k] = turn[k] + (re * v - im * u)
        c1, s1, c2, s2 = geo[b, C1], geo[b, S1], geo[b, C2], geo[b, S2]
        weighted = edge[0] + c1 * edge[1] + s1 * turn[1] + c2 * edge[2] + s2 * turn[2]
        dlength = -jnp.sum(rate_row[None] * weighted, axis=2, keepdims=True)
        dc2 = jnp.sum(edge[2], axis=2, keepdims=True)
        ds2 = jnp.sum(turn[2], axis=2, keepdims=True)
        dc1 = jnp.sum(edge[1], axis=2, keepdims=True) + 2.0 * (c1 * dc2 + s1 * ds2)
        ds1 = jnp.sum(turn[1], axis=2, keepdims=True) + 2.0 * (c1 * ds2 - s1 * dc2)
        along = dc1 * c1 + ds1 * s1
        planar = geo[b, PLANAR]
        grads = (
            (dc1 - along * c1) / planar + dlength * geo[b, LX],
            (ds1 - along * s1) / planar + dlength * geo[b, LY],
            dlength * geo[b, LZ],
        )
        where = mask[b] - ownmask[None]
        for axis in range(3):
            ftile[b * 3 + axis : b * 3 + axis + 1, :] = jnp.sum(
                jnp.sum(where * grads[axis], axis=0), axis=0, keepdims=True
            )

    for b in range(BATCHES):
        dsig, gate = backward_head(b)
        for k in range(3):
            backward_chunk(b, k, dsig, gate)
        coordinates(b)
        combine(b)

    for side in range(2):
        end_copy(side).start()
    for side in range(2):
        end_copy(side).wait_recv()
    share = ftile[...] + jnp.where(row < 6, pltpu.roll(frecv[0], C - A, 1) + pltpu.roll(frecv[1], A, 1), 0.0)
    grecv[seg] = pltpu.roll(share, C - A, 1)
    for step in range(1, segments):
        gather_copy(step).start()
    for step in range(1, segments):
        gather_copy(step).wait_recv()
    result = grecv[0]
    for other in range(1, segments):
        result = result + grecv[other]
    out_p[0] = result[0:3, 0:A]
    out_p[1] = result[3:6, 0:A]
    out_e[...] = result[6:8, 0:A]

    for side in range(2):
        place_copy(side).wait_send()
        end_copy(side).wait_send()
        for b in range(BATCHES):
            for k in range(3):
                halo_copy(b, k, side).wait_send()
    for step in range(1, segments):
        gather_copy(step).wait_send()

    @pl.when(seg < last)
    def _():
        for b in range(BATCHES):
            for k in range(3):
                up_copy(b, k).wait_send()

    @pl.when(seg > 0)
    def _():
        for b in range(BATCHES):
            for k in range(3):
                down_copy(b, k).wait_send()
                for side in range(2):
                    back_copy(b, k, side).wait_send()


def solution(mesh):
    segments = mesh.shape["segment"]
    vmem = pl.BlockSpec(memory_space=pltpu.VMEM)
    anywhere = pl.BlockSpec(memory_space=pl.ANY)
    dma = pltpu.SemaphoreType.DMA
    B = BATCHES

    def on_device(
        node_states, species, species_table, places, sources, radial_rate, zero_weight, one_weight, two_weight,
        read_weight, energy_grad,
    ):
        return pl.pallas_call(
            kernel,
            out_shape=(
                jax.ShapeDtypeStruct((B, A), F32),
                jax.ShapeDtypeStruct((B, 3, A), F32),
            ),
            in_specs=[vmem] * 6 + [anywhere] * 3 + [vmem] * 2,
            out_specs=(vmem, vmem),
            scratch_shapes=[
                pltpu.VMEM((7 * C, 7 * C), BF16),
                pltpu.VMEM((2, 6 * C, 6 * C), BF16),
                pltpu.VMEM((2, 5 * C, 5 * C), BF16),
                pltpu.VMEM((A * 32, C), F32),
                pltpu.VMEM((B, 48, WIDTH), BF16),
                pltpu.VMEM((B, 16, WIDTH), BF16),
                pltpu.VMEM((B, NEIGH * 16, WIDTH), BF16),
                pltpu.VMEM((B, 16, WIDTH), F32),
                pltpu.VMEM((B, A, C), F32),
                pltpu.VMEM((B, A, C), F32),
                pltpu.VMEM((B, NEIGH * 16, 48), BF16),
                pltpu.VMEM((B, 48, NEIGH * 16), BF16),
                pltpu.VMEM((B, NEIGH, A, C), F32),
                pltpu.VMEM((B, 9, NEIGH, A, C), F32),
                pltpu.VMEM((B, 16, WIDTH), BF16),
                pltpu.VMEM((B, 16, WIDTH), F32),
                pltpu.VMEM((B, 16, WIDTH), F32),
                pltpu.VMEM((NEIGH * 16, WIDTH), BF16),
                pltpu.VMEM((B, 16, WIDTH), F32),
                pltpu.VMEM((B, 2, 16, WIDTH), BF16),
                pltpu.VMEM((B, 2, 16, WIDTH), BF16),
                pltpu.VMEM((B, 16, WIDTH), BF16),
                pltpu.VMEM((2, A, C), F32),
                pltpu.VMEM((2, A, C), F32),
                pltpu.VMEM((A, C), F32),
                pltpu.VMEM((2, A, C), F32),
                pltpu.VMEM((segments, A, C), F32),
                dma((3,)),
                dma((2,)),
                dma((2,)),
                dma((B, 3, 2)),
                dma((B, 3, 2)),
                dma((B, 3)),
                dma((B, 3)),
                dma((B, 3, 2)),
                dma((B, 3, 2)),
                dma((B, 3)),
                dma((B, 3)),
                dma((2,)),
                dma((2,)),
                dma((segments - 1,)),
                dma((segments - 1,)),
            ],
            compiler_params=pltpu.CompilerParams(
                collective_id=0, has_side_effects=True, vmem_limit_bytes=48 * 1024 * 1024
            ),
        )(
            node_states, species, species_table, places, sources, radial_rate, zero_weight, one_weight, two_weight,
            read_weight.reshape(1, C), energy_grad,
        )

    in_specs = (
        P(None, "space", None, None),
        P(None, "space"),
        P(),
        P(None, None, "space"),
        P(None, "space", None),
        P("segment", None),
        P("segment", None, None),
        P("segment", None, None, None),
        P("segment", None, None, None),
        P(),
        P(None, "space"),
    )
    out_specs = (P(None, "space"), P(None, None, "space"))
    return jax.shard_map(on_device, mesh=mesh, in_specs=in_specs, out_specs=out_specs, check_vma=False)
```

```python
import contextlib
import jax
import jax.numpy as jnp
from jax import lax
from jax.experimental import pallas as pl
from jax.experimental.pallas import tpu as pltpu
from jax.sharding import PartitionSpec as P

A = 8
NEIGH = 8
C = 128
BATCHES = 2
SLAB_DEPTH = 2.0
MESH = pl.DeviceIdType.MESH
F32 = jnp.float32
BF16 = jnp.bfloat16

CHUNKS = ((0, 512), (512, 768), (1280, 640))
WIDTH = 1920
UPPER = (0, 1, 2, 3, 7, 8, 9, 10, 11, 12, 19, 20, 21, 22, 23)
LOWER = (4, 5, 6, None, 13, 14, 15, 16, 17, 18, 24, 25, 26, 27, 28)
SCOPES = False
RAD, C1, S1, C2, S2, LX, LY, LZ, PLANAR = range(9)


def dot(x, y):
    return lax.dot_general(x, y, (((1,), (0,)), ((), ())), preferred_element_type=F32)


def dot_t(x, y):
    return lax.dot_general(x, y, (((1,), (1,)), ((), ())), preferred_element_type=F32)


def scope(name):
    return jax.named_scope(name) if SCOPES else contextlib.nullcontext()


def halves(x):
    high = x.astype(BF16).astype(F32)
    return jnp.concatenate([high, x - high], axis=0).astype(BF16)


def kernel(
    places_hbm, egrad_hbm, node_hbm, species_hbm, table_hbm, sources_hbm, rate_hbm, read_hbm, wz_hbm, w1_hbm, w2_hbm,
    out_e, out_p,
    places, egrad, node, species, table, sources, rate, read, wz, w1, w2, ext, yout, scaled, pooled, signal, last_top, gmat, gtr, mask, geo, ct, du, uv, dmat,
    ownsum, hsend, hrecv, ysend, ptile, precv, ftile, frecv, grecv,
    isem, psem_s, psem_r, fh_s, fh_r, fy_s, fy_r, bh_s, bh_r, by_s, by_r, eh_s, eh_r, ey_s, ey_r,
):
    seg = lax.axis_index("segment")
    slab = lax.axis_index("space")
    segments = lax.axis_size("segment")
    slabs = lax.axis_size("space")
    left = lax.rem(slab + slabs - 1, slabs)
    right = lax.rem(slab + 1, slabs)
    last = segments - 1
    up = lax.rem(seg + 1, segments)
    down = lax.rem(seg + segments - 1, segments)
    beside = ({"space": left}, {"space": right})
    factor = NEIGH ** (-0.5)
    lane = lax.broadcasted_iota(jnp.int32, (A, C), 1)
    row = lax.broadcasted_iota(jnp.int32, (A, C), 0)
    ownmask = jnp.where(lane == row + A, 1.0, 0.0).astype(F32)

    inputs = (
        (places_hbm, places), (egrad_hbm, egrad), (node_hbm, node), (species_hbm, species), (table_hbm, table),
        (sources_hbm, sources), (rate_hbm, rate), (read_hbm, read), (wz_hbm.at[0], wz), (w1_hbm.at[0], w1),
        (w2_hbm.at[0], w2),
    )
    inputs = [pltpu.make_async_copy(src, dst, isem.at[i]) for i, (src, dst) in enumerate(inputs)]
    loads = inputs[8:]
    for load in inputs:
        load.start()

    barrier = pltpu.get_barrier_semaphore()
    for target in beside:
        pl.semaphore_signal(barrier, inc=1, device_id=target, device_id_type=MESH)
    for step in range(1, segments):
        pl.semaphore_signal(
            barrier, inc=1, device_id={"segment": lax.rem(seg + step, segments)}, device_id_type=MESH
        )

    def remote(src, dst, send, recv, target):
        return pltpu.make_async_remote_copy(
            src_ref=src, dst_ref=dst, send_sem=send, recv_sem=recv, device_id=target, device_id_type=MESH
        )

    def cols(k):
        return pl.ds(CHUNKS[k][0], CHUNKS[k][1])

    def place_copy(side):
        return remote(ptile.at[side], precv.at[1 - side], psem_s.at[side], psem_r.at[side], beside[side])

    def halo_copy(b, k, side):
        return remote(
            ext.at[b, pl.ds(16, 16), cols(k)], ext.at[b, pl.ds(32 * (1 - side), 16), cols(k)],
            fh_s.at[b, k, side], fh_r.at[b, k, side], beside[side],
        )

    def up_copy(b, k):
        return remote(
            yout.at[b, :, cols(k)], ext.at[b, pl.ds(16, 16), cols(k)], fy_s.at[b, k], fy_r.at[b, k], {"segment": up}
        )

    def back_copy(b, k, side):
        return remote(
            hsend.at[b, side, :, cols(k)], hrecv.at[b, 1 - side, :, cols(k)],
            bh_s.at[b, k, side], bh_r.at[b, k, side], beside[side],
        )

    def down_copy(b, k):
        return remote(
            ysend.at[b, :, cols(k)], ct.at[b, :, cols(k)], by_s.at[b, k], by_r.at[b, k], {"segment": down}
        )

    def end_copy(side):
        return remote(ftile, frecv.at[1 - side], eh_s.at[side], eh_r.at[side], beside[side])

    def gather_copy(step):
        return remote(
            grecv.at[seg], grecv.at[seg], ey_s.at[step - 1], ey_r.at[step - 1],
            {"segment": lax.rem(seg + step, segments)},
        )

    ptile[1] = jnp.zeros((A, C), F32)
    for load in inputs[:8]:
        load.wait()
    for axis in range(3):
        for b in range(BATCHES):
            ptile[1, b * 3 + axis : b * 3 + axis + 1, 0:A] = places[axis, b : b + 1]
    ptile[1, 6:8, 0:A] = egrad[...]
    base = ptile[1]
    ptile[0] = pltpu.roll(base, 16, 1)
    own_tile = pltpu.roll(base, A, 1)

    def make_start(b):
        kind = jnp.sum(
            jnp.where(lane == row, jnp.broadcast_to(spec_tile[b : b + 1], (A, C)), 0.0), axis=1, keepdims=True
        )
        onehot = jnp.where(lane.astype(F32) == kind, 1.0, 0.0).astype(BF16)
        embed = dot(onehot[:, : table.shape[0]], table[...])
        for t in range(15):
            upper = node[b, UPPER[t]].astype(F32)
            if t == 0:
                upper = upper + embed
            if LOWER[t] is None:
                lower = jnp.zeros((A, C), F32)
            else:
                lower = node[b, LOWER[t]].astype(F32)
            ext[b, 16:32, t * C : (t + 1) * C] = jnp.concatenate([upper, lower], axis=0).astype(BF16)

    spec_tile = jnp.concatenate(
        [species[...].astype(F32), jnp.zeros((BATCHES, C - A), F32)], axis=1
    )

    @pl.when(seg == 0)
    def _():
        for b in range(BATCHES):
            make_start(b)

    pl.semaphore_wait(barrier, segments + 1)

    for side in range(2):
        place_copy(side).start()

    @pl.when(seg == 0)
    def _():
        for b in range(BATCHES):
            for k in range(3):
                for side in range(2):
                    halo_copy(b, k, side).start()

    lane3 = lax.broadcasted_iota(jnp.int32, (NEIGH, A, C), 2)
    lane_local = (lane3 >> 4) * A + (lane3 & 7)
    lane_part = (lane3 >> 3) & 1

    def make_index(b):
        index = sources[b]
        window = (index >> 3) - slab + 1
        window = jnp.where(window < 0, window + slabs, window)
        window = jnp.where(window >= slabs, window - slabs, window)
        local = window * A + (index & 7)
        local = jnp.concatenate([jnp.broadcast_to(local[:, j : j + 1], (A, C))[None] for j in range(NEIGH)], axis=0)
        mask[b] = jnp.where(local == lane3, 1.0, 0.0).astype(F32)
        same = local == lane_local
        picks = jnp.concatenate(
            [
                jnp.where(same & (lane_part == 0), 1.0, 0.0).astype(F32),
                jnp.where(same & (lane_part == 1), 1.0, 0.0).astype(F32),
            ],
            axis=1,
        ).reshape(2 * NEIGH * A, C)
        gmat[b] = picks[:, :48].astype(BF16)
        gtr[b] = picks.T[:48].astype(BF16)

    for b in range(BATCHES):
        make_index(b)

    for side in range(2):
        place_copy(side).wait_recv()
    around = precv[0] + own_tile + precv[1]
    elevation = jnp.where(lane < A, -SLAB_DEPTH, jnp.where(lane < 2 * A, 0.0, SLAB_DEPTH)).astype(F32)[0:1]
    rate_row = rate[...]

    def make_geometry(b):
        picks = mask[b]
        offsets = []
        for axis in range(3):
            line = around[b * 3 + axis : b * 3 + axis + 1]
            raised = line + elevation if axis == 2 else line
            there = jnp.sum(picks * raised[None], axis=2, keepdims=True)
            here = jnp.sum(ownmask * line, axis=1, keepdims=True)
            offsets.append(jnp.broadcast_to(there - here[None], (NEIGH, A, C)))
        ox, oy, oz = offsets
        length = jnp.sqrt(ox * ox + oy * oy + oz * oz + 1.0)
        planar = jnp.sqrt(ox * ox + oy * oy + 1.0)
        c1 = ox / planar
        s1 = oy / planar
        geo[b, RAD] = jnp.exp(-rate_row[None] * length)
        geo[b, C1] = c1
        geo[b, S1] = s1
        geo[b, C2] = c1 * c1 - s1 * s1
        geo[b, S2] = 2.0 * c1 * s1
        geo[b, LX] = ox / length
        geo[b, LY] = oy / length
        geo[b, LZ] = oz / length
        geo[b, PLANAR] = planar

    for b in range(BATCHES):
        make_geometry(b)

    weights = (None, w1, w2)

    def relay(b):
        @pl.when(seg > 0)
        def _():
            for k in range(3):
                up_copy(b, k).wait_recv()
                for side in range(2):
                    halo_copy(b, k, side).start()

    def forward_chunk(b, k):
        c0, n = CHUNKS[k]
        with scope(f"fwait{b}{k}"):
            for side in range(2):
                halo_copy(b, k, side).wait_recv()
        picked = dot(gmat[b], ext[b, :, c0 : c0 + n])
        radial = geo[b, RAD]
        radial = jnp.concatenate([radial, radial], axis=1)
        if k:
            cos, sin = geo[b, (C1, C2)[k - 1]], geo[b, (S1, S2)[k - 1]]
        sums = []
        for t in range(n // C):
            part = picked[:, t * C : (t + 1) * C].reshape(NEIGH, 16, C)
            rounded = (part * radial).astype(BF16)
            scaled[b, :, c0 + t * C : c0 + (t + 1) * C] = rounded.reshape(NEIGH * 16, C)
            part = rounded.astype(F32)
            if k:
                re, im = part[:, :A], part[:, A:]
                sums.append(
                    jnp.concatenate(
                        [jnp.sum(cos * re - sin * im, axis=0), jnp.sum(sin * re + cos * im, axis=0)], axis=0
                    )
                )
            else:
                sums.append(jnp.sum(part, axis=0))
        if b == 0:
            loads[k].wait()
        if k:
            both = halves(jnp.concatenate(sums, axis=1))
            p = dot(both, weights[k][0])
            q = dot(both, weights[k][1])
            p = p[:16] + p[16:]
            q = q[:16] + q[16:]
            pooled[b, 0:8, c0 : c0 + n] = (p[:8] - q[8:]) * factor
            pooled[b, 8:16, c0 : c0 + n] = (p[8:] + q[:8]) * factor
        else:
            whole = jnp.concatenate([x[:8] for x in sums] + [x[8:] for x in sums[:3]], axis=1)
            z = dot(halves(whole), wz[...])
            z = (z[:8] + z[8:]) * factor
            pooled[b, 0:8, 0:512] = z[:, :512]
            pooled[b, 8:16, 0:384] = z[:, 512:]
            pooled[b, 8:16, 384:512] = jnp.zeros((A, C), F32)

    def forward_end(b):
        total = jnp.zeros((16, C), F32)
        for t in range(4, 15):
            value = pooled[b, :, t * C : (t + 1) * C]
            total = total + value * value
        sig = pooled[b, 0:8, 0:C] + total[:8] + total[8:]
        signal[b] = sig
        gate = jax.nn.sigmoid(sig)
        silu = sig * gate
        gate2 = jnp.concatenate([gate, gate], axis=0)
        for t in range(15):
            own = ext[b, 16:32, t * C : (t + 1) * C].astype(F32)
            added = gate2 * pooled[b, :, t * C : (t + 1) * C]
            if t == 0:
                added = jnp.concatenate([silu, added[8:]], axis=0)
            new = own + added
            if t == 0:
                last_top[b] = new[:8]
            yout[b, :, t * C : (t + 1) * C] = new.astype(BF16)

        @pl.when(seg < last)
        def _():
            for k in range(3):
                up_copy(b, k).start()

    for b in range(BATCHES):
        with scope(f"relay{b}"):
            relay(b)
        for k in range(3):
            with scope(f"f{b}{k}"):
                forward_chunk(b, k)
        with scope(f"fend{b}"):
            forward_end(b)

    read_row = read[...]

    def backward_head(b):
        @pl.when(seg == last)
        def _():
            top = last_top[b]
            gate = jax.nn.sigmoid(top)
            energy = jnp.sum(read_row * (top * gate), axis=1, keepdims=True)
            seed = jnp.sum(ownmask * own_tile[6 + b : 7 + b], axis=1, keepdims=True)
            ftile[6 + b : 7 + b, :] = jnp.sum(ownmask * energy, axis=0, keepdims=True)
            du[b] = jnp.zeros((16, WIDTH), F32)
            du[b, 0:8, 0:C] = seed * read_row * (gate * (1.0 + top * (1.0 - gate)))

        @pl.when(seg < last)
        def _():
            ftile[6 + b : 7 + b, :] = jnp.zeros((1, C), F32)
            for k in range(3):
                down_copy(b, k).wait_recv()
            du[b] = ct[b].astype(F32)

        sig = signal[b]
        gate = jax.nn.sigmoid(sig)
        total = jnp.zeros((16, C), F32)
        for t in range(15):
            value = du[b, :, t * C : (t + 1) * C] * pooled[b, :, t * C : (t + 1) * C]
            if t == 0:
                value = jnp.concatenate([jnp.zeros((A, C), F32), value[8:]], axis=0)
            total = total + value
        dgate = total[:8] + total[8:]
        dsig = du[b, 0:8, 0:C] * (gate * (1.0 + sig * (1.0 - gate))) + dgate * (gate * (1.0 - gate))
        return dsig, gate

    def backward_chunk(b, k, dsig, gate):
        c0, n = CHUNKS[k]
        gate2 = jnp.concatenate([gate, gate], axis=0)
        dsig2 = jnp.concatenate([dsig, dsig], axis=0)
        parts = []
        for t in range(n // C):
            at = slice(c0 + t * C, c0 + (t + 1) * C)
            part = gate2 * du[b, :, at]
            if k:
                part = part + 2.0 * pooled[b, :, at] * dsig2
            elif t == 0:
                part = jnp.concatenate([dsig, part[8:]], axis=0)
            parts.append(part * factor)
        if k:
            both = halves(jnp.concatenate(parts, axis=1))
            p = dot_t(both, weights[k][0])
            q = dot_t(both, weights[k][1])
            p = p[:16] + p[16:]
            q = q[:16] + q[16:]
            uv[b, 0:8, c0 : c0 + n] = p[:8] + q[8:]
            uv[b, 8:16, c0 : c0 + n] = p[8:] - q[:8]
        else:
            whole = jnp.concatenate([x[:8] for x in parts] + [x[8:] for x in parts[:3]], axis=1)
            z = dot_t(halves(whole), wz[...])
            z = z[:8] + z[8:]
            uv[b, 0:8, 0:512] = z[:, :512]
            uv[b, 8:16, 0:384] = z[:, 512:]
            uv[b, 8:16, 384:512] = jnp.zeros((A, C), F32)

        @pl.when(seg > 0)
        def _():
            radial = geo[b, RAD]
            if k:
                rc, rs = radial * geo[b, (C1, C2)[k - 1]], radial * geo[b, (S1, S2)[k - 1]]
            for t in range(n // C):
                at = slice(c0 + t * C, c0 + (t + 1) * C)
                u, v = uv[b, 0:8, at], uv[b, 8:16, at]
                if k:
                    upper, lower = rc * u + rs * v, rc * v - rs * u
                else:
                    upper, lower = radial * u, radial * v
                dmat[:, at] = jnp.concatenate([upper, lower], axis=1).reshape(NEIGH * 16, C).astype(BF16)
            spread = dot(gtr[b], dmat[:, c0 : c0 + n])
            hsend[b, 0, :, c0 : c0 + n] = spread[0:16].astype(BF16)
            hsend[b, 1, :, c0 : c0 + n] = spread[32:48].astype(BF16)
            for side in range(2):
                back_copy(b, k, side).start()
            ownsum[b, :, c0 : c0 + n] = spread[16:32] + du[b, :, c0 : c0 + n]

    def combine(b):
        @pl.when(seg > 0)
        def _():
            for k in range(3):
                for side in range(2):
                    back_copy(b, k, side).wait_recv()
                ysend[b, :, cols(k)] = (
                    ownsum[b, :, cols(k)]
                    + hrecv[b, 0, :, cols(k)].astype(F32)
                    + hrecv[b, 1, :, cols(k)].astype(F32)
                ).astype(BF16)
                down_copy(b, k).start()

    def coordinates(b):
        edge = [jnp.zeros((NEIGH, A, C), F32) for _ in range(3)]
        turn = [None, jnp.zeros((NEIGH, A, C), F32), jnp.zeros((NEIGH, A, C), F32)]
        for k in range(3):
            c0, n = CHUNKS[k]
            for t in range(n // C):
                at = slice(c0 + t * C, c0 + (t + 1) * C)
                part = scaled[b, :, at].astype(F32).reshape(NEIGH, 16, C)
                re, im = part[:, :A], part[:, A:]
                u, v = uv[b, 0:8, at], uv[b, 8:16, at]
                edge[k] = edge[k] + (re * u + im * v)
                if k:
                    turn[k] = turn[k] + (re * v - im * u)
        c1, s1, c2, s2 = geo[b, C1], geo[b, S1], geo[b, C2], geo[b, S2]
        weighted = edge[0] + c1 * edge[1] + s1 * turn[1] + c2 * edge[2] + s2 * turn[2]
        dlength = -jnp.sum(rate_row[None] * weighted, axis=2, keepdims=True)
        dc2 = jnp.sum(edge[2], axis=2, keepdims=True)
        ds2 = jnp.sum(turn[2], axis=2, keepdims=True)
        dc1 = jnp.sum(edge[1], axis=2, keepdims=True) + 2.0 * (c1 * dc2 + s1 * ds2)
        ds1 = jnp.sum(turn[1], axis=2, keepdims=True) + 2.0 * (c1 * ds2 - s1 * dc2)
        along = dc1 * c1 + ds1 * s1
        planar = geo[b, PLANAR]
        grads = (
            (dc1 - along * c1) / planar + dlength * geo[b, LX],
            (ds1 - along * s1) / planar + dlength * geo[b, LY],
            dlength * geo[b, LZ],
        )
        where = mask[b] - ownmask[None]
        for axis in range(3):
            ftile[b * 3 + axis : b * 3 + axis + 1, :] = jnp.sum(
                jnp.sum(where * grads[axis], axis=0), axis=0, keepdims=True
            )

    for b in range(BATCHES):
        with scope(f"bhead{b}"):
            dsig, gate = backward_head(b)
        for k in range(3):
            with scope(f"b{b}{k}"):
                backward_chunk(b, k, dsig, gate)
        with scope(f"coord{b}"):
            coordinates(b)
        with scope(f"comb{b}"):
            combine(b)

    for side in range(2):
        end_copy(side).start()
    for side in range(2):
        end_copy(side).wait_recv()
    share = ftile[...] + jnp.where(row < 6, pltpu.roll(frecv[0], C - A, 1) + pltpu.roll(frecv[1], A, 1), 0.0)
    grecv[seg] = pltpu.roll(share, C - A, 1)
    for step in range(1, segments):
        gather_copy(step).start()
    for step in range(1, segments):
        gather_copy(step).wait_recv()
    result = grecv[0]
    for other in range(1, segments):
        result = result + grecv[other]
    for axis in range(3):
        for b in range(BATCHES):
            out_p[axis, b : b + 1] = result[b * 3 + axis : b * 3 + axis + 1, 0:A]
    out_e[...] = result[6:8, 0:A]

    for side in range(2):
        place_copy(side).wait_send()
        end_copy(side).wait_send()
        for b in range(BATCHES):
            for k in range(3):
                halo_copy(b, k, side).wait_send()
    for step in range(1, segments):
        gather_copy(step).wait_send()

    @pl.when(seg < last)
    def _():
        for b in range(BATCHES):
            for k in range(3):
                up_copy(b, k).wait_send()

    @pl.when(seg > 0)
    def _():
        for b in range(BATCHES):
            for k in range(3):
                down_copy(b, k).wait_send()
                for side in range(2):
                    back_copy(b, k, side).wait_send()


def solution(mesh):
    segments = mesh.shape["segment"]
    vmem = pl.BlockSpec(memory_space=pltpu.VMEM)
    hbm = pl.BlockSpec(memory_space=pltpu.HBM)
    dma = pltpu.SemaphoreType.DMA
    B = BATCHES

    def on_device(
        node_states, species, species_table, places, sources, radial_rate, zero_weight, one_weight, two_weight,
        read_weight, energy_grad,
    ):
        energies, grads = pl.pallas_call(
            kernel,
            out_shape=(
                jax.ShapeDtypeStruct((B, A), F32),
                jax.ShapeDtypeStruct((3, B, A), F32),
            ),
            in_specs=[hbm] * 11,
            out_specs=(vmem, vmem),
            scratch_shapes=[
                pltpu.VMEM((3, B, A), F32),
                pltpu.VMEM((B, A), F32),
                pltpu.VMEM((B, 29, A, C), BF16),
                pltpu.VMEM((B, A), jnp.int32),
                pltpu.VMEM(species_table.shape, BF16),
                pltpu.VMEM((B, A, NEIGH), jnp.int32),
                pltpu.VMEM((1, C), F32),
                pltpu.VMEM((1, C), F32),
                pltpu.VMEM((7 * C, 7 * C), BF16),
                pltpu.VMEM((2, 6 * C, 6 * C), BF16),
                pltpu.VMEM((2, 5 * C, 5 * C), BF16),
                pltpu.VMEM((B, 48, WIDTH), BF16),
                pltpu.VMEM((B, 16, WIDTH), BF16),
                pltpu.VMEM((B, NEIGH * 16, WIDTH), BF16),
                pltpu.VMEM((B, 16, WIDTH), F32),
                pltpu.VMEM((B, A, C), F32),
                pltpu.VMEM((B, A, C), F32),
                pltpu.VMEM((B, NEIGH * 16, 48), BF16),
                pltpu.VMEM((B, 48, NEIGH * 16), BF16),
                pltpu.VMEM((B, NEIGH, A, C), F32),
                pltpu.VMEM((B, 9, NEIGH, A, C), F32),
                pltpu.VMEM((B, 16, WIDTH), BF16),
                pltpu.VMEM((B, 16, WIDTH), F32),
                pltpu.VMEM((B, 16, WIDTH), F32),
                pltpu.VMEM((NEIGH * 16, WIDTH), BF16),
                pltpu.VMEM((B, 16, WIDTH), F32),
                pltpu.VMEM((B, 2, 16, WIDTH), BF16),
                pltpu.VMEM((B, 2, 16, WIDTH), BF16),
                pltpu.VMEM((B, 16, WIDTH), BF16),
                pltpu.VMEM((2, A, C), F32),
                pltpu.VMEM((2, A, C), F32),
                pltpu.VMEM((A, C), F32),
                pltpu.VMEM((2, A, C), F32),
                pltpu.VMEM((segments, A, C), F32),
                dma((11,)),
                dma((2,)),
                dma((2,)),
                dma((B, 3, 2)),
                dma((B, 3, 2)),
                dma((B, 3)),
                dma((B, 3)),
                dma((B, 3, 2)),
                dma((B, 3, 2)),
                dma((B, 3)),
                dma((B, 3)),
                dma((2,)),
                dma((2,)),
                dma((segments - 1,)),
                dma((segments - 1,)),
            ],
            compiler_params=pltpu.CompilerParams(
                collective_id=0, has_side_effects=True, vmem_limit_bytes=67043328
            ),
        )(
            places.transpose(1, 0, 2), energy_grad, node_states.transpose(0, 2, 1, 3), species, species_table, sources,
            radial_rate, read_weight.reshape(1, C), zero_weight, one_weight, two_weight,
        )
        return energies, grads.transpose(1, 0, 2)

    in_specs = (
        P(None, "space", None, None),
        P(None, "space"),
        P(),
        P(None, None, "space"),
        P(None, "space", None),
        P("segment", None),
        P("segment", None, None),
        P("segment", None, None, None),
        P("segment", None, None, None),
        P(),
        P(None, "space"),
    )
    out_specs = (P(None, "space"), P(None, None, "space"))
    return jax.shard_map(on_device, mesh=mesh, in_specs=in_specs, out_specs=out_specs, check_vma=False)
```

```python
import contextlib
import jax
import jax.numpy as jnp
from jax import lax
from jax.experimental import pallas as pl
from jax.experimental.pallas import tpu as pltpu
from jax.sharding import PartitionSpec as P

A = 8
NEIGH = 8
C = 128
BATCHES = 2
SLAB_DEPTH = 2.0
MESH = pl.DeviceIdType.MESH
F32 = jnp.float32
BF16 = jnp.bfloat16

CHUNKS = ((0, 512), (512, 768), (1280, 640))
WIDTH = 1920
UPPER = (0, 1, 2, 3, 7, 8, 9, 10, 11, 12, 19, 20, 21, 22, 23)
LOWER = (4, 5, 6, None, 13, 14, 15, 16, 17, 18, 24, 25, 26, 27, 28)
SCOPES = False
RAD, C1, S1, C2, S2, LX, LY, LZ, PLANAR = range(9)


def dot(x, y):
    return lax.dot_general(x, y, (((1,), (0,)), ((), ())), preferred_element_type=F32)


def dot_t(x, y):
    return lax.dot_general(x, y, (((1,), (1,)), ((), ())), preferred_element_type=F32)


def scope(name):
    return jax.named_scope(name) if SCOPES else contextlib.nullcontext()


def halves(x):
    high = x.astype(BF16).astype(F32)
    return jnp.concatenate([high, x - high], axis=0).astype(BF16)


def kernel(
    places_hbm, egrad_hbm, node_hbm, species_hbm, table_hbm, sources_hbm, rate_hbm, read_hbm, wz_hbm, w1_hbm, w2_hbm,
    out_e, out_p,
    places, egrad, node, species, table, sources, rate, read, wz, w1, w2, ext, yout, scaled, pooled, signal, last_top, gmat, gtr, mask, geo, ct, du, uv, dmat,
    ownsum, hsend, hrecv, ctfar, ysend, ptile, precv, ftile, grecv,
    isem, psem_s, psem_r, f0_s, fn_s, fn_r, ff_s, ff_r, fy_s, fy_r, bn_s, bn_r, bf_s, bf_r, by_s, by_r, e_s, e_r,
):
    seg = lax.axis_index("segment")
    slab = lax.axis_index("space")
    segments = lax.axis_size("segment")
    slabs = lax.axis_size("space")
    core = lax.rem(slab, 2)
    near = slab + 1 - 2 * core
    far = lax.rem(slab + slabs + 2 * core - 1, slabs)
    near_slot = 2 * core
    far_slot = 2 - 2 * core
    last = segments - 1
    up = lax.rem(seg + 1, segments)
    down = lax.rem(seg + segments - 1, segments)
    factor = NEIGH ** (-0.5)
    lane = lax.broadcasted_iota(jnp.int32, (A, C), 1)
    row = lax.broadcasted_iota(jnp.int32, (A, C), 0)
    ownmask = jnp.where(lane == row + A, 1.0, 0.0).astype(F32)

    inputs = (
        (places_hbm, places), (egrad_hbm, egrad), (node_hbm, node), (species_hbm, species), (table_hbm, table),
        (sources_hbm, sources), (rate_hbm, rate), (read_hbm, read), (wz_hbm.at[0], wz), (w1_hbm.at[0], w1),
        (w2_hbm.at[0], w2),
    )
    inputs = [pltpu.make_async_copy(src, dst, isem.at[i]) for i, (src, dst) in enumerate(inputs)]
    loads = inputs[8:]
    for load in inputs:
        load.start()

    barrier = pltpu.get_barrier_semaphore()
    for target in (near, far):
        pl.semaphore_signal(barrier, inc=1, device_id={"space": target}, device_id_type=MESH)

    @pl.when(seg > 0)
    def _():
        pl.semaphore_signal(barrier, inc=1, device_id={"segment": down}, device_id_type=MESH)

    @pl.when(seg < last)
    def _():
        pl.semaphore_signal(barrier, inc=1, device_id={"segment": up}, device_id_type=MESH)

    greeted = 2 + jnp.minimum(seg, 1) + jnp.minimum(last - seg, 1)

    def remote(src, dst, send, recv, target):
        return pltpu.make_async_remote_copy(
            src_ref=src, dst_ref=dst, send_sem=send, recv_sem=recv, device_id=target, device_id_type=MESH
        )

    def cols(k):
        return pl.ds(CHUNKS[k][0], CHUNKS[k][1])

    def place_copy(kind):
        return remote(
            ptile.at[(far_slot, near_slot)[kind]], precv.at[(far_slot, near_slot)[kind]],
            psem_s.at[kind], psem_r.at[kind], {"space": (far, near)[kind]},
        )

    def near_copy(b, k):
        return remote(
            ext.at[b, 1, :, cols(k)], ext.at[b, near_slot, :, cols(k)], fn_s.at[b, k], fn_r.at[b, k], {"space": near}
        )

    def first_copy(b, k):
        return remote(
            ext.at[b, 1, :, cols(k)], ext.at[b, far_slot, :, cols(k)], f0_s.at[b, k], ff_r.at[b, k], {"space": far}
        )

    def far_copy(b, k):
        return remote(
            yout.at[b, :, cols(k)], ext.at[b, far_slot, :, cols(k)], ff_s.at[b, k], ff_r.at[b, k],
            {"segment": up, "space": far},
        )

    def up_copy(b, k):
        return remote(
            yout.at[b, :, cols(k)], ext.at[b, 1, :, cols(k)], fy_s.at[b, k], fy_r.at[b, k], {"segment": up}
        )

    def back_near_copy(b, k):
        return remote(
            hsend.at[b, 0, :, cols(k)], hrecv.at[b, :, cols(k)], bn_s.at[b, k], bn_r.at[b, k], {"space": near}
        )

    def back_far_copy(b, k):
        return remote(
            hsend.at[b, 1, :, cols(k)], ctfar.at[b, :, cols(k)], bf_s.at[b, k], bf_r.at[b, k],
            {"segment": down, "space": far},
        )

    def down_copy(b, k):
        return remote(
            ysend.at[b, :, cols(k)], ct.at[b, :, cols(k)], by_s.at[b, k], by_r.at[b, k], {"segment": down}
        )

    def end_copy(step, kind):
        return remote(
            ftile, grecv.at[seg, (far_slot, near_slot, 1)[kind]], e_s.at[step, kind], e_r.at[step, kind],
            {"segment": lax.rem(seg + step, segments), "space": (far, near, slab)[kind]},
        )

    ends = [(step, kind) for step in range(segments) for kind in range(3) if step or kind < 2]

    ptile[1] = jnp.zeros((A, C), F32)
    with scope("input"):
        for load in inputs[:8]:
            load.wait()
    for axis in range(3):
        for b in range(BATCHES):
            ptile[1, b * 3 + axis : b * 3 + axis + 1, 0:A] = places[axis, b : b + 1]
    ptile[1, 6:8, 0:A] = egrad[...]
    base = ptile[1]
    ptile[0] = base
    ptile[2] = pltpu.roll(base, 16, 1)
    own_tile = pltpu.roll(base, A, 1)

    def make_start(b):
        kind = jnp.sum(
            jnp.where(lane == row, jnp.broadcast_to(spec_tile[b : b + 1], (A, C)), 0.0), axis=1, keepdims=True
        )
        onehot = jnp.where(lane.astype(F32) == kind, 1.0, 0.0).astype(BF16)
        embed = dot(onehot[:, : table.shape[0]], table[...])
        for t in range(15):
            upper = node[b, UPPER[t]].astype(F32)
            if t == 0:
                upper = upper + embed
            if LOWER[t] is None:
                lower = jnp.zeros((A, C), F32)
            else:
                lower = node[b, LOWER[t]].astype(F32)
            ext[b, 1, :, t * C : (t + 1) * C] = jnp.concatenate([upper, lower], axis=0).astype(BF16)

    spec_tile = jnp.concatenate(
        [species[...].astype(F32), jnp.zeros((BATCHES, C - A), F32)], axis=1
    )

    with scope("start"):

        @pl.when(seg == 0)
        def _():
            for b in range(BATCHES):
                make_start(b)

    with scope("barrier"):
        pl.semaphore_wait(barrier, greeted)

    for kind in range(2):
        place_copy(kind).start()

    @pl.when(seg == 0)
    def _():
        for b in range(BATCHES):
            for k in range(3):
                first_copy(b, k).start()
                near_copy(b, k).start()

    lane3 = lax.broadcasted_iota(jnp.int32, (NEIGH, A, C), 2)
    lane_local = (lane3 >> 4) * A + (lane3 & 7)
    lane_part = (lane3 >> 3) & 1

    def make_index(b):
        index = sources[b]
        window = (index >> 3) - slab + 1
        window = jnp.where(window < 0, window + slabs, window)
        window = jnp.where(window >= slabs, window - slabs, window)
        local = window * A + (index & 7)
        local = jnp.concatenate([jnp.broadcast_to(local[:, j : j + 1], (A, C))[None] for j in range(NEIGH)], axis=0)
        mask[b] = jnp.where(local == lane3, 1.0, 0.0).astype(F32)
        same = local == lane_local
        picks = jnp.concatenate(
            [
                jnp.where(same & (lane_part == 0), 1.0, 0.0).astype(F32),
                jnp.where(same & (lane_part == 1), 1.0, 0.0).astype(F32),
            ],
            axis=1,
        ).reshape(2 * NEIGH * A, C)
        gmat[b] = picks[:, :48].astype(BF16)
        gtr[b] = picks.T[:48].astype(BF16)

    with scope("index"):
        for b in range(BATCHES):
            make_index(b)

    with scope("places"):
        for kind in range(2):
            place_copy(kind).wait_recv()
    around = precv[0] + own_tile + precv[2]
    elevation = jnp.where(lane < A, -SLAB_DEPTH, jnp.where(lane < 2 * A, 0.0, SLAB_DEPTH)).astype(F32)[0:1]
    rate_row = rate[...]

    def make_geometry(b):
        picks = mask[b]
        offsets = []
        for axis in range(3):
            line = around[b * 3 + axis : b * 3 + axis + 1]
            raised = line + elevation if axis == 2 else line
            there = jnp.sum(picks * raised[None], axis=2, keepdims=True)
            here = jnp.sum(ownmask * line, axis=1, keepdims=True)
            offsets.append(jnp.broadcast_to(there - here[None], (NEIGH, A, C)))
        ox, oy, oz = offsets
        length = jnp.sqrt(ox * ox + oy * oy + oz * oz + 1.0)
        planar = jnp.sqrt(ox * ox + oy * oy + 1.0)
        c1 = ox / planar
        s1 = oy / planar
        geo[b, RAD] = jnp.exp(-rate_row[None] * length)
        geo[b, C1] = c1
        geo[b, S1] = s1
        geo[b, C2] = c1 * c1 - s1 * s1
        geo[b, S2] = 2.0 * c1 * s1
        geo[b, LX] = ox / length
        geo[b, LY] = oy / length
        geo[b, LZ] = oz / length
        geo[b, PLANAR] = planar

    with scope("geometry"):
        for b in range(BATCHES):
            make_geometry(b)

    weights = (None, w1, w2)

    def relay(b):
        @pl.when(seg > 0)
        def _():
            for k in range(3):
                up_copy(b, k).wait_recv()
                near_copy(b, k).start()

    def forward_chunk(b, k):
        c0, n = CHUNKS[k]
        with scope(f"fwait{b}{k}"):
            near_copy(b, k).wait_recv()
            far_copy(b, k).wait_recv()
        picked = dot(gmat[b], ext[b, :, :, c0 : c0 + n].reshape(48, n))
        radial = geo[b, RAD]
        radial = jnp.concatenate([radial, radial], axis=1)
        if k:
            cos, sin = geo[b, (C1, C2)[k - 1]], geo[b, (S1, S2)[k - 1]]
        sums = []
        for t in range(n // C):
            part = picked[:, t * C : (t + 1) * C].reshape(NEIGH, 16, C)
            rounded = (part * radial).astype(BF16)
            scaled[b, :, c0 + t * C : c0 + (t + 1) * C] = rounded.reshape(NEIGH * 16, C)
            part = rounded.astype(F32)
            if k:
                re, im = part[:, :A], part[:, A:]
                sums.append(
                    jnp.concatenate(
                        [jnp.sum(cos * re - sin * im, axis=0), jnp.sum(sin * re + cos * im, axis=0)], axis=0
                    )
                )
            else:
                sums.append(jnp.sum(part, axis=0))
        if b == 0:
            loads[k].wait()
        if k:
            both = halves(jnp.concatenate(sums, axis=1))
            p = dot(both, weights[k][0])
            q = dot(both, weights[k][1])
            p = p[:16] + p[16:]
            q = q[:16] + q[16:]
            pooled[b, 0:8, c0 : c0 + n] = (p[:8] - q[8:]) * factor
            pooled[b, 8:16, c0 : c0 + n] = (p[8:] + q[:8]) * factor
        else:
            whole = jnp.concatenate([x[:8] for x in sums] + [x[8:] for x in sums[:3]], axis=1)
            z = dot(halves(whole), wz[...])
            z = (z[:8] + z[8:]) * factor
            pooled[b, 0:8, 0:512] = z[:, :512]
            pooled[b, 8:16, 0:384] = z[:, 512:]
            pooled[b, 8:16, 384:512] = jnp.zeros((A, C), F32)

    def forward_end(b):
        total = jnp.zeros((16, C), F32)
        for t in range(4, 15):
            value = pooled[b, :, t * C : (t + 1) * C]
            total = total + value * value
        sig = pooled[b, 0:8, 0:C] + total[:8] + total[8:]
        signal[b] = sig
        gate = jax.nn.sigmoid(sig)
        silu = sig * gate
        gate2 = jnp.concatenate([gate, gate], axis=0)
        for t in range(15):
            own = ext[b, 1, :, t * C : (t + 1) * C].astype(F32)
            added = gate2 * pooled[b, :, t * C : (t + 1) * C]
            if t == 0:
                added = jnp.concatenate([silu, added[8:]], axis=0)
            new = own + added
            if t == 0:
                last_top[b] = new[:8]
            yout[b, :, t * C : (t + 1) * C] = new.astype(BF16)

        @pl.when(seg < last)
        def _():
            for k in range(3):
                up_copy(b, k).start()
                far_copy(b, k).start()

    for b in range(BATCHES):
        with scope(f"relay{b}"):
            relay(b)
        for k in range(3):
            with scope(f"f{b}{k}"):
                forward_chunk(b, k)
        with scope(f"fend{b}"):
            forward_end(b)

    read_row = read[...]

    def backward_head(b):
        @pl.when(seg == last)
        def _():
            top = last_top[b]
            gate = jax.nn.sigmoid(top)
            energy = jnp.sum(read_row * (top * gate), axis=1, keepdims=True)
            seed = jnp.sum(ownmask * own_tile[6 + b : 7 + b], axis=1, keepdims=True)
            ftile[6 + b : 7 + b, :] = jnp.sum(ownmask * energy, axis=0, keepdims=True)
            du[b] = jnp.zeros((16, WIDTH), F32)
            du[b, 0:8, 0:C] = seed * read_row * (gate * (1.0 + top * (1.0 - gate)))

        @pl.when(seg < last)
        def _():
            ftile[6 + b : 7 + b, :] = jnp.zeros((1, C), F32)
            for k in range(3):
                down_copy(b, k).wait_recv()
                back_far_copy(b, k).wait_recv()
            du[b] = ct[b].astype(F32) + ctfar[b].astype(F32)

        sig = signal[b]
        gate = jax.nn.sigmoid(sig)
        total = jnp.zeros((16, C), F32)
        for t in range(15):
            value = du[b, :, t * C : (t + 1) * C] * pooled[b, :, t * C : (t + 1) * C]
            if t == 0:
                value = jnp.concatenate([jnp.zeros((A, C), F32), value[8:]], axis=0)
            total = total + value
        dgate = total[:8] + total[8:]
        dsig = du[b, 0:8, 0:C] * (gate * (1.0 + sig * (1.0 - gate))) + dgate * (gate * (1.0 - gate))
        return dsig, gate

    def backward_chunk(b, k, dsig, gate):
        c0, n = CHUNKS[k]
        gate2 = jnp.concatenate([gate, gate], axis=0)
        dsig2 = jnp.concatenate([dsig, dsig], axis=0)
        parts = []
        for t in range(n // C):
            at = slice(c0 + t * C, c0 + (t + 1) * C)
            part = gate2 * du[b, :, at]
            if k:
                part = part + 2.0 * pooled[b, :, at] * dsig2
            elif t == 0:
                part = jnp.concatenate([dsig, part[8:]], axis=0)
            parts.append(part * factor)
        if k:
            both = halves(jnp.concatenate(parts, axis=1))
            p = dot_t(both, weights[k][0])
            q = dot_t(both, weights[k][1])
            p = p[:16] + p[16:]
            q = q[:16] + q[16:]
            uv[b, 0:8, c0 : c0 + n] = p[:8] + q[8:]
            uv[b, 8:16, c0 : c0 + n] = p[8:] - q[:8]
        else:
            whole = jnp.concatenate([x[:8] for x in parts] + [x[8:] for x in parts[:3]], axis=1)
            z = dot_t(halves(whole), wz[...])
            z = z[:8] + z[8:]
            uv[b, 0:8, 0:512] = z[:, :512]
            uv[b, 8:16, 0:384] = z[:, 512:]
            uv[b, 8:16, 384:512] = jnp.zeros((A, C), F32)

        @pl.when(seg > 0)
        def _():
            radial = geo[b, RAD]
            if k:
                rc, rs = radial * geo[b, (C1, C2)[k - 1]], radial * geo[b, (S1, S2)[k - 1]]
            for t in range(n // C):
                at = slice(c0 + t * C, c0 + (t + 1) * C)
                u, v = uv[b, 0:8, at], uv[b, 8:16, at]
                if k:
                    upper, lower = rc * u + rs * v, rc * v - rs * u
                else:
                    upper, lower = radial * u, radial * v
                dmat[:, at] = jnp.concatenate([upper, lower], axis=1).reshape(NEIGH * 16, C).astype(BF16)
            spread = dot(gtr[b], dmat[:, c0 : c0 + n])
            hsend[b, 1 - core, :, c0 : c0 + n] = spread[0:16].astype(BF16)
            hsend[b, core, :, c0 : c0 + n] = spread[32:48].astype(BF16)
            back_near_copy(b, k).start()
            back_far_copy(b, k).start()
            ownsum[b, :, c0 : c0 + n] = spread[16:32] + du[b, :, c0 : c0 + n]

    def combine(b, where):
        @pl.when(where)
        def _():
            for k in range(3):
                back_near_copy(b, k).wait_recv()
                ysend[b, :, cols(k)] = (ownsum[b, :, cols(k)] + hrecv[b, :, cols(k)].astype(F32)).astype(BF16)
                down_copy(b, k).start()

    def coordinates(b):
        edge = [jnp.zeros((NEIGH, A, C), F32) for _ in range(3)]
        turn = [None, jnp.zeros((NEIGH, A, C), F32), jnp.zeros((NEIGH, A, C), F32)]
        for k in range(3):
            c0, n = CHUNKS[k]
            for t in range(n // C):
                at = slice(c0 + t * C, c0 + (t + 1) * C)
                part = scaled[b, :, at].astype(F32).reshape(NEIGH, 16, C)
                re, im = part[:, :A], part[:, A:]
                u, v = uv[b, 0:8, at], uv[b, 8:16, at]
                edge[k] = edge[k] + (re * u + im * v)
                if k:
                    turn[k] = turn[k] + (re * v - im * u)
        c1, s1, c2, s2 = geo[b, C1], geo[b, S1], geo[b, C2], geo[b, S2]
        weighted = edge[0] + c1 * edge[1] + s1 * turn[1] + c2 * edge[2] + s2 * turn[2]
        dlength = -jnp.sum(rate_row[None] * weighted, axis=2, keepdims=True)
        dc2 = jnp.sum(edge[2], axis=2, keepdims=True)
        ds2 = jnp.sum(turn[2], axis=2, keepdims=True)
        dc1 = jnp.sum(edge[1], axis=2, keepdims=True) + 2.0 * (c1 * dc2 + s1 * ds2)
        ds1 = jnp.sum(turn[1], axis=2, keepdims=True) + 2.0 * (c1 * ds2 - s1 * dc2)
        along = dc1 * c1 + ds1 * s1
        planar = geo[b, PLANAR]
        grads = (
            (dc1 - along * c1) / planar + dlength * geo[b, LX],
            (ds1 - along * s1) / planar + dlength * geo[b, LY],
            dlength * geo[b, LZ],
        )
        where = mask[b] - ownmask[None]
        for axis in range(3):
            ftile[b * 3 + axis : b * 3 + axis + 1, :] = jnp.sum(
                jnp.sum(where * grads[axis], axis=0), axis=0, keepdims=True
            )

    for b in range(BATCHES):
        with scope(f"bhead{b}"):
            dsig, gate = backward_head(b)
        for k in range(3):
            with scope(f"b{b}{k}"):
                backward_chunk(b, k, dsig, gate)
            if b == 1 and k == 0:
                with scope("comb0l"):
                    combine(0, seg == last)
        with scope(f"coord{b}"):
            coordinates(b)
        with scope(f"comb{b}"):
            combine(b, (seg > 0) & (seg < last) if b == 0 else seg > 0)

    with scope("final"):
        for step, kind in ends:
            end_copy(step, kind).start()
        grecv[seg, 1] = ftile[...]
        for step, kind in ends:
            end_copy(step, kind).wait_recv()
    totals = []
    for slot in range(3):
        total = grecv[0, slot]
        for other in range(1, segments):
            total = total + grecv[other, slot]
        totals.append(total)
    result = totals[1] + jnp.where(row < 6, pltpu.roll(totals[0], C - A, 1) + pltpu.roll(totals[2], A, 1), 0.0)
    result = pltpu.roll(result, C - A, 1)
    for axis in range(3):
        for b in range(BATCHES):
            out_p[axis, b : b + 1] = result[b * 3 + axis : b * 3 + axis + 1, 0:A]
    out_e[...] = result[6:8, 0:A]

    with scope("drain"):
        for kind in range(2):
            place_copy(kind).wait_send()
        for step, kind in ends:
            end_copy(step, kind).wait_send()
        for b in range(BATCHES):
            for k in range(3):
                near_copy(b, k).wait_send()

        @pl.when(seg == 0)
        def _():
            for b in range(BATCHES):
                for k in range(3):
                    first_copy(b, k).wait_send()

        @pl.when(seg < last)
        def _():
            for b in range(BATCHES):
                for k in range(3):
                    up_copy(b, k).wait_send()
                    far_copy(b, k).wait_send()

        @pl.when(seg > 0)
        def _():
            for b in range(BATCHES):
                for k in range(3):
                    down_copy(b, k).wait_send()
                    back_near_copy(b, k).wait_send()
                    back_far_copy(b, k).wait_send()


def solution(mesh):
    segments = mesh.shape["segment"]
    vmem = pl.BlockSpec(memory_space=pltpu.VMEM)
    hbm = pl.BlockSpec(memory_space=pltpu.HBM)
    dma = pltpu.SemaphoreType.DMA
    B = BATCHES

    def on_device(
        node_states, species, species_table, places, sources, radial_rate, zero_weight, one_weight, two_weight,
        read_weight, energy_grad,
    ):
        energies, grads = pl.pallas_call(
            kernel,
            out_shape=(
                jax.ShapeDtypeStruct((B, A), F32),
                jax.ShapeDtypeStruct((3, B, A), F32),
            ),
            in_specs=[hbm] * 11,
            out_specs=(vmem, vmem),
            scratch_shapes=[
                pltpu.VMEM((3, B, A), F32),
                pltpu.VMEM((B, A), F32),
                pltpu.VMEM((B, 29, A, C), BF16),
                pltpu.VMEM((B, A), jnp.int32),
                pltpu.VMEM(species_table.shape, BF16),
                pltpu.VMEM((B, A, NEIGH), jnp.int32),
                pltpu.VMEM((1, C), F32),
                pltpu.VMEM((1, C), F32),
                pltpu.VMEM((7 * C, 7 * C), BF16),
                pltpu.VMEM((2, 6 * C, 6 * C), BF16),
                pltpu.VMEM((2, 5 * C, 5 * C), BF16),
                pltpu.VMEM((B, 3, 16, WIDTH), BF16),
                pltpu.VMEM((B, 16, WIDTH), BF16),
                pltpu.VMEM((B, NEIGH * 16, WIDTH), BF16),
                pltpu.VMEM((B, 16, WIDTH), F32),
                pltpu.VMEM((B, A, C), F32),
                pltpu.VMEM((B, A, C), F32),
                pltpu.VMEM((B, NEIGH * 16, 48), BF16),
                pltpu.VMEM((B, 48, NEIGH * 16), BF16),
                pltpu.VMEM((B, NEIGH, A, C), F32),
                pltpu.VMEM((B, 9, NEIGH, A, C), F32),
                pltpu.VMEM((B, 16, WIDTH), BF16),
                pltpu.VMEM((B, 16, WIDTH), F32),
                pltpu.VMEM((B, 16, WIDTH), F32),
                pltpu.VMEM((NEIGH * 16, WIDTH), BF16),
                pltpu.VMEM((B, 16, WIDTH), F32),
                pltpu.VMEM((B, 2, 16, WIDTH), BF16),
                pltpu.VMEM((B, 16, WIDTH), BF16),
                pltpu.VMEM((B, 16, WIDTH), BF16),
                pltpu.VMEM((B, 16, WIDTH), BF16),
                pltpu.VMEM((3, A, C), F32),
                pltpu.VMEM((3, A, C), F32),
                pltpu.VMEM((A, C), F32),
                pltpu.VMEM((segments, 3, A, C), F32),
                dma((11,)),
                dma((2,)),
                dma((2,)),
                *[dma((B, 3))] * 13,
                dma((segments, 3)),
                dma((segments, 3)),
            ],
            compiler_params=pltpu.CompilerParams(
                collective_id=0, has_side_effects=True, vmem_limit_bytes=67043328
            ),
        )(
            places.transpose(1, 0, 2), energy_grad, node_states.transpose(0, 2, 1, 3), species, species_table, sources,
            radial_rate, read_weight.reshape(1, C), zero_weight, one_weight, two_weight,
        )
        return energies, grads.transpose(1, 0, 2)

    in_specs = (
        P(None, "space", None, None),
        P(None, "space"),
        P(),
        P(None, None, "space"),
        P(None, "space", None),
        P("segment", None),
        P("segment", None, None),
        P("segment", None, None, None),
        P("segment", None, None, None),
        P(),
        P(None, "space"),
    )
    out_specs = (P(None, "space"), P(None, None, "space"))
    return jax.shard_map(on_device, mesh=mesh, in_specs=in_specs, out_specs=out_specs, check_vma=False)
```

```python
import contextlib
import jax
import jax.numpy as jnp
from jax import lax
from jax.experimental import pallas as pl
from jax.experimental.pallas import tpu as pltpu
from jax.sharding import PartitionSpec as P

A = 8
NEIGH = 8
C = 128
BATCHES = 2
SLAB_DEPTH = 2.0
ROW = 8
MESH = pl.DeviceIdType.MESH
F32 = jnp.float32
BF16 = jnp.bfloat16

CHUNKS = ((0, 512), (512, 768), (1280, 640))
WIDTH = 1920
UPPER = (0, 1, 2, 3, 7, 8, 9, 10, 11, 12, 19, 20, 21, 22, 23)
LOWER = (4, 5, 6, None, 13, 14, 15, 16, 17, 18, 24, 25, 26, 27, 28)
SCOPES = False
DIRECT = 1
RAD, C1, S1, C2, S2, LX, LY, LZ, PLANAR = range(9)


def dot(x, y):
    return lax.dot_general(x, y, (((1,), (0,)), ((), ())), preferred_element_type=F32)


def dot_t(x, y):
    return lax.dot_general(x, y, (((1,), (1,)), ((), ())), preferred_element_type=F32)


def scope(name):
    return jax.named_scope(name) if SCOPES else contextlib.nullcontext()


def halves(x):
    high = x.astype(BF16).astype(F32)
    return jnp.concatenate([high, x - high], axis=0).astype(BF16)


def kernel(
    places_hbm, egrad_hbm, node_hbm, species_hbm, table_hbm, sources_hbm, rate_hbm, read_hbm, wz_hbm, w1_hbm, w2_hbm,
    out_e, out_p,
    places, egrad, node, species, table, sources, rate, read, wz, w1, w2, ext, yout, scaled, pooled, signal, last_top, gmat, gtr, mask, geo, ct, du, uv, dmat,
    ownsum, hsend, hrecv, hfar, ctfar, ysend, ptile, precv, ftile, grecv,
    isem, psem_s, psem_r, f0_s, fn_s, fn_r, ff_s, ff_r, fy_s, fy_r, bn_s, bn_r, bf_s, bf_r, bs_r, by_s, by_r, e_s, e_r,
):
    seg = lax.axis_index("segment")
    slab = lax.axis_index("space")
    segments = lax.axis_size("segment")
    slabs = lax.axis_size("space")
    core = lax.rem(slab, 2)
    near = slab + 1 - 2 * core
    far = lax.rem(slab + slabs + 2 * core - 1, slabs)
    near_slot = 2 * core
    far_slot = 2 - 2 * core
    row_of_slabs = min(ROW, slabs)
    place_in_row = lax.rem(slab, row_of_slabs)
    cross = (place_in_row == 0) | (place_in_row == row_of_slabs - 1)
    inner = jnp.logical_not(cross)
    last = segments - 1
    up = lax.rem(seg + 1, segments)
    down = lax.rem(seg + segments - 1, segments)
    factor = NEIGH ** (-0.5)
    lane = lax.broadcasted_iota(jnp.int32, (A, C), 1)
    row = lax.broadcasted_iota(jnp.int32, (A, C), 0)
    ownmask = jnp.where(lane == row + A, 1.0, 0.0).astype(F32)

    inputs = (
        (places_hbm, places), (egrad_hbm, egrad), (node_hbm, node), (species_hbm, species), (table_hbm, table),
        (sources_hbm, sources), (rate_hbm, rate), (read_hbm, read), (wz_hbm.at[0], wz), (w1_hbm.at[0], w1),
        (w2_hbm.at[0], w2),
    )
    inputs = [pltpu.make_async_copy(src, dst, isem.at[i]) for i, (src, dst) in enumerate(inputs)]
    loads = inputs[8:]
    for load in inputs:
        load.start()

    barrier = pltpu.get_barrier_semaphore()
    for target in (near, far):
        pl.semaphore_signal(barrier, inc=1, device_id={"space": target}, device_id_type=MESH)

    @pl.when(seg > 0)
    def _():
        pl.semaphore_signal(barrier, inc=1, device_id={"segment": down}, device_id_type=MESH)

    @pl.when(seg < last)
    def _():
        pl.semaphore_signal(barrier, inc=1, device_id={"segment": up}, device_id_type=MESH)

    greeted = 2 + jnp.minimum(seg, 1) + jnp.minimum(last - seg, 1)

    def remote(src, dst, send, recv, target):
        return pltpu.make_async_remote_copy(
            src_ref=src, dst_ref=dst, send_sem=send, recv_sem=recv, device_id=target, device_id_type=MESH
        )

    def cols(k):
        return pl.ds(CHUNKS[k][0], CHUNKS[k][1])

    def place_copy(kind):
        return remote(
            ptile.at[(far_slot, near_slot)[kind]], precv.at[(far_slot, near_slot)[kind]],
            psem_s.at[kind], psem_r.at[kind], {"space": (far, near)[kind]},
        )

    def near_copy(b, k):
        return remote(
            ext.at[b, 1, :, cols(k)], ext.at[b, near_slot, :, cols(k)], fn_s.at[b, k], fn_r.at[b, k], {"space": near}
        )

    def first_copy(b, k):
        return remote(
            ext.at[b, 1, :, cols(k)], ext.at[b, far_slot, :, cols(k)], f0_s.at[b, k], ff_r.at[b, k], {"space": far}
        )

    def far_copy(b, k):
        return remote(
            yout.at[b, :, cols(k)], ext.at[b, far_slot, :, cols(k)], ff_s.at[b, k], ff_r.at[b, k],
            {"segment": up, "space": far},
        )

    def up_copy(b, k):
        return remote(
            yout.at[b, :, cols(k)], ext.at[b, 1, :, cols(k)], fy_s.at[b, k], fy_r.at[b, k], {"segment": up}
        )

    def back_near_copy(b, k):
        return remote(
            hsend.at[b, 0, :, cols(k)], hrecv.at[b, :, cols(k)], bn_s.at[b, k], bn_r.at[b, k], {"space": near}
        )

    def back_far_copy(b, k):
        return remote(
            hsend.at[b, 1, :, cols(k)], ctfar.at[b, :, cols(k)], bf_s.at[b, k], bf_r.at[b, k],
            {"segment": down, "space": far},
        )

    def back_side_copy(b, k):
        return remote(
            hsend.at[b, 1, :, cols(k)], hfar.at[b, :, cols(k)], bf_s.at[b, k], bs_r.at[b, k], {"space": far}
        )

    def down_copy(b, k):
        return remote(
            ysend.at[b, :, cols(k)], ct.at[b, :, cols(k)], by_s.at[b, k], by_r.at[b, k], {"segment": down}
        )

    def end_copy(step, kind):
        return remote(
            ftile, grecv.at[seg, (far_slot, near_slot, 1)[kind]], e_s.at[step, kind], e_r.at[step, kind],
            {"segment": lax.rem(seg + step, segments), "space": (far, near, slab)[kind]},
        )

    ends = [(step, kind) for step in range(segments) for kind in range(3) if step or kind < 2]

    ptile[1] = jnp.zeros((A, C), F32)
    with scope("input"):
        for load in inputs[:8]:
            load.wait()
    for axis in range(3):
        for b in range(BATCHES):
            ptile[1, b * 3 + axis : b * 3 + axis + 1, 0:A] = places[axis, b : b + 1]
    ptile[1, 6:8, 0:A] = egrad[...]
    base = ptile[1]
    ptile[0] = base
    ptile[2] = pltpu.roll(base, 16, 1)
    own_tile = pltpu.roll(base, A, 1)

    def make_start(b):
        kind = jnp.sum(
            jnp.where(lane == row, jnp.broadcast_to(spec_tile[b : b + 1], (A, C)), 0.0), axis=1, keepdims=True
        )
        onehot = jnp.where(lane.astype(F32) == kind, 1.0, 0.0).astype(BF16)
        embed = dot(onehot[:, : table.shape[0]], table[...])
        for t in range(15):
            upper = node[b, UPPER[t]].astype(F32)
            if t == 0:
                upper = upper + embed
            if LOWER[t] is None:
                lower = jnp.zeros((A, C), F32)
            else:
                lower = node[b, LOWER[t]].astype(F32)
            ext[b, 1, :, t * C : (t + 1) * C] = jnp.concatenate([upper, lower], axis=0).astype(BF16)

    spec_tile = jnp.concatenate(
        [species[...].astype(F32), jnp.zeros((BATCHES, C - A), F32)], axis=1
    )

    with scope("start"):

        @pl.when(seg == 0)
        def _():
            for b in range(BATCHES):
                make_start(b)

    with scope("barrier"):
        pl.semaphore_wait(barrier, greeted)

    for kind in range(2):
        place_copy(kind).start()

    @pl.when(seg == 0)
    def _():
        for b in range(BATCHES):
            for k in range(3):
                first_copy(b, k).start()
                near_copy(b, k).start()

    lane3 = lax.broadcasted_iota(jnp.int32, (NEIGH, A, C), 2)
    lane_local = (lane3 >> 4) * A + (lane3 & 7)
    lane_part = (lane3 >> 3) & 1

    def make_index(b):
        index = sources[b]
        window = (index >> 3) - slab + 1
        window = jnp.where(window < 0, window + slabs, window)
        window = jnp.where(window >= slabs, window - slabs, window)
        local = window * A + (index & 7)
        local = jnp.concatenate([jnp.broadcast_to(local[:, j : j + 1], (A, C))[None] for j in range(NEIGH)], axis=0)
        mask[b] = jnp.where(local == lane3, 1.0, 0.0).astype(F32)
        same = local == lane_local
        picks = jnp.concatenate(
            [
                jnp.where(same & (lane_part == 0), 1.0, 0.0).astype(F32),
                jnp.where(same & (lane_part == 1), 1.0, 0.0).astype(F32),
            ],
            axis=1,
        ).reshape(2 * NEIGH * A, C)
        gmat[b] = picks[:, :48].astype(BF16)
        gtr[b] = picks.T[:48].astype(BF16)

    with scope("index"):
        for b in range(BATCHES):
            make_index(b)

    with scope("places"):
        for kind in range(2):
            place_copy(kind).wait_recv()
    around = precv[0] + own_tile + precv[2]
    elevation = jnp.where(lane < A, -SLAB_DEPTH, jnp.where(lane < 2 * A, 0.0, SLAB_DEPTH)).astype(F32)[0:1]
    rate_row = rate[...]

    def make_geometry(b):
        picks = mask[b]
        offsets = []
        for axis in range(3):
            line = around[b * 3 + axis : b * 3 + axis + 1]
            raised = line + elevation if axis == 2 else line
            there = jnp.sum(picks * raised[None], axis=2, keepdims=True)
            here = jnp.sum(ownmask * line, axis=1, keepdims=True)
            offsets.append(jnp.broadcast_to(there - here[None], (NEIGH, A, C)))
        ox, oy, oz = offsets
        length = jnp.sqrt(ox * ox + oy * oy + oz * oz + 1.0)
        planar = jnp.sqrt(ox * ox + oy * oy + 1.0)
        c1 = ox / planar
        s1 = oy / planar
        geo[b, RAD] = jnp.exp(-rate_row[None] * length)
        geo[b, C1] = c1
        geo[b, S1] = s1
        geo[b, C2] = c1 * c1 - s1 * s1
        geo[b, S2] = 2.0 * c1 * s1
        geo[b, LX] = ox / length
        geo[b, LY] = oy / length
        geo[b, LZ] = oz / length
        geo[b, PLANAR] = planar

    with scope("geometry"):
        for b in range(BATCHES):
            make_geometry(b)

    weights = (None, w1, w2)

    def relay(b):
        @pl.when(seg > 0)
        def _():
            for k in range(3):
                up_copy(b, k).wait_recv()
                near_copy(b, k).start()
                pl.when(inner)(first_copy(b, k).start)

    def gather(b, k):
        c0, n = CHUNKS[k]
        with scope(f"fwait{b}{k}"):
            near_copy(b, k).wait_recv()
            far_copy(b, k).wait_recv()
        picked = dot(gmat[b], ext[b, :, :, c0 : c0 + n].reshape(48, n))
        radial = geo[b, RAD]
        radial = jnp.concatenate([radial, radial], axis=1)
        if k:
            cos, sin = geo[b, (C1, C2)[k - 1]], geo[b, (S1, S2)[k - 1]]
        sums = []
        for t in range(n // C):
            part = picked[:, t * C : (t + 1) * C].reshape(NEIGH, 16, C)
            rounded = (part * radial).astype(BF16)
            scaled[b, :, c0 + t * C : c0 + (t + 1) * C] = rounded.reshape(NEIGH * 16, C)
            part = rounded.astype(F32)
            if k:
                re, im = part[:, :A], part[:, A:]
                sums.append(
                    jnp.concatenate(
                        [jnp.sum(cos * re - sin * im, axis=0), jnp.sum(sin * re + cos * im, axis=0)], axis=0
                    )
                )
            else:
                sums.append(jnp.sum(part, axis=0))
        return sums

    def mix(b, k, sums):
        c0, n = CHUNKS[k]
        if k:
            both = halves(jnp.concatenate(sums, axis=1))
            p = dot(both, weights[k][0])
            q = dot(both, weights[k][1])
            p = p[:16] + p[16:]
            q = q[:16] + q[16:]
            pooled[b, 0:8, c0 : c0 + n] = (p[:8] - q[8:]) * factor
            pooled[b, 8:16, c0 : c0 + n] = (p[8:] + q[:8]) * factor
        else:
            whole = jnp.concatenate([x[:8] for x in sums] + [x[8:] for x in sums[:3]], axis=1)
            z = dot(halves(whole), wz[...])
            z = (z[:8] + z[8:]) * factor
            pooled[b, 0:8, 0:512] = z[:, :512]
            pooled[b, 8:16, 0:384] = z[:, 512:]
            pooled[b, 8:16, 384:512] = jnp.zeros((A, C), F32)

    def forward_end(b):
        total = jnp.zeros((16, C), F32)
        for t in range(4, 15):
            value = pooled[b, :, t * C : (t + 1) * C]
            total = total + value * value
        sig = pooled[b, 0:8, 0:C] + total[:8] + total[8:]
        signal[b] = sig
        gate = jax.nn.sigmoid(sig)
        silu = sig * gate
        gate2 = jnp.concatenate([gate, gate], axis=0)
        for t in range(15):
            own = ext[b, 1, :, t * C : (t + 1) * C].astype(F32)
            added = gate2 * pooled[b, :, t * C : (t + 1) * C]
            if t == 0:
                added = jnp.concatenate([silu, added[8:]], axis=0)
            new = own + added
            if t == 0:
                last_top[b] = new[:8]
            yout[b, :, t * C : (t + 1) * C] = new.astype(BF16)

        @pl.when(seg < last)
        def _():
            for k in range(3):
                up_copy(b, k).start()
                pl.when(cross)(far_copy(b, k).start)

    def forward(b):
        if b == 0:
            for load in loads:
                load.wait()
        with scope(f"f{b}0"):
            mix(b, 0, gather(b, 0))
        if b == 0:
            with scope("relay1"):
                relay(1)
        with scope(f"f{b}1"):
            sums = gather(b, 1)
        with scope(f"f{b}2"):
            more = gather(b, 2)
            mix(b, 1, sums)
            mix(b, 2, more)
        with scope(f"fend{b}"):
            forward_end(b)

    read_row = read[...]

    def backward_head(b):
        @pl.when(seg == last)
        def _():
            top = last_top[b]
            gate = jax.nn.sigmoid(top)
            energy = jnp.sum(read_row * (top * gate), axis=1, keepdims=True)
            seed = jnp.sum(ownmask * own_tile[6 + b : 7 + b], axis=1, keepdims=True)
            ftile[6 + b : 7 + b, :] = jnp.sum(ownmask * energy, axis=0, keepdims=True)
            du[b] = jnp.zeros((16, WIDTH), F32)
            du[b, 0:8, 0:C] = seed * read_row * (gate * (1.0 + top * (1.0 - gate)))

        @pl.when(seg < last)
        def _():
            ftile[6 + b : 7 + b, :] = jnp.zeros((1, C), F32)
            for k in range(3):
                down_copy(b, k).wait_recv()
            split = CHUNKS[DIRECT][0]

            @pl.when(cross)
            def _():
                for k in range(DIRECT):
                    back_far_copy(b, k).wait_recv()
                du[b, :, :split] = ct[b, :, :split].astype(F32) + ctfar[b, :, :split].astype(F32)

            @pl.when(inner)
            def _():
                du[b, :, :split] = ct[b, :, :split].astype(F32)

            for k in range(DIRECT, 3):
                back_far_copy(b, k).wait_recv()
            du[b, :, split:] = ct[b, :, split:].astype(F32) + ctfar[b, :, split:].astype(F32)

        sig = signal[b]
        gate = jax.nn.sigmoid(sig)
        total = jnp.zeros((16, C), F32)
        for t in range(15):
            value = du[b, :, t * C : (t + 1) * C] * pooled[b, :, t * C : (t + 1) * C]
            if t == 0:
                value = jnp.concatenate([jnp.zeros((A, C), F32), value[8:]], axis=0)
            total = total + value
        dgate = total[:8] + total[8:]
        dsig = du[b, 0:8, 0:C] * (gate * (1.0 + sig * (1.0 - gate))) + dgate * (gate * (1.0 - gate))
        return dsig, gate

    def mix_back(b, k, dsig, gate):
        c0, n = CHUNKS[k]
        gate2 = jnp.concatenate([gate, gate], axis=0)
        dsig2 = jnp.concatenate([dsig, dsig], axis=0)
        parts = []
        for t in range(n // C):
            at = slice(c0 + t * C, c0 + (t + 1) * C)
            part = gate2 * du[b, :, at]
            if k:
                part = part + 2.0 * pooled[b, :, at] * dsig2
            elif t == 0:
                part = jnp.concatenate([dsig, part[8:]], axis=0)
            parts.append(part * factor)
        if k:
            both = halves(jnp.concatenate(parts, axis=1))
            p = dot_t(both, weights[k][0])
            q = dot_t(both, weights[k][1])
            p = p[:16] + p[16:]
            q = q[:16] + q[16:]
            uv[b, 0:8, c0 : c0 + n] = p[:8] + q[8:]
            uv[b, 8:16, c0 : c0 + n] = p[8:] - q[:8]
        else:
            whole = jnp.concatenate([x[:8] for x in parts] + [x[8:] for x in parts[:3]], axis=1)
            z = dot_t(halves(whole), wz[...])
            z = z[:8] + z[8:]
            uv[b, 0:8, 0:512] = z[:, :512]
            uv[b, 8:16, 0:384] = z[:, 512:]
            uv[b, 8:16, 384:512] = jnp.zeros((A, C), F32)

    def spread_back(b, k):
        c0, n = CHUNKS[k]
        radial = geo[b, RAD]
        if k:
            rc, rs = radial * geo[b, (C1, C2)[k - 1]], radial * geo[b, (S1, S2)[k - 1]]
        for t in range(n // C):
            at = slice(c0 + t * C, c0 + (t + 1) * C)
            u, v = uv[b, 0:8, at], uv[b, 8:16, at]
            if k:
                upper, lower = rc * u + rs * v, rc * v - rs * u
            else:
                upper, lower = radial * u, radial * v
            dmat[:, at] = jnp.concatenate([upper, lower], axis=1).reshape(NEIGH * 16, C).astype(BF16)
        spread = dot(gtr[b], dmat[:, c0 : c0 + n])
        hsend[b, 1 - core, :, c0 : c0 + n] = spread[0:16].astype(BF16)
        hsend[b, core, :, c0 : c0 + n] = spread[32:48].astype(BF16)
        ownsum[b, :, c0 : c0 + n] = spread[16:32] + du[b, :, c0 : c0 + n]
    def send_back(b, k):
        back_near_copy(b, k).start()
        if k < DIRECT:
            pl.when(cross)(back_far_copy(b, k).start)
            pl.when(inner)(back_side_copy(b, k).start)
        else:
            back_far_copy(b, k).start()

    def combine(b):
        for k in range(3):
            back_near_copy(b, k).wait_recv()
            total = ownsum.at[b, :, cols(k)]
            total[...] += hrecv[b, :, cols(k)].astype(F32)
            if k < DIRECT:

                @pl.when(inner)
                def _():
                    back_side_copy(b, k).wait_recv()
                    total[...] += hfar[b, :, cols(k)].astype(F32)

            ysend[b, :, cols(k)] = total[...].astype(BF16)
            down_copy(b, k).start()

    def coordinates(b):
        edge = [jnp.zeros((NEIGH, A, C), F32) for _ in range(3)]
        turn = [None, jnp.zeros((NEIGH, A, C), F32), jnp.zeros((NEIGH, A, C), F32)]
        for k in range(3):
            c0, n = CHUNKS[k]
            for t in range(n // C):
                at = slice(c0 + t * C, c0 + (t + 1) * C)
                part = scaled[b, :, at].astype(F32).reshape(NEIGH, 16, C)
                re, im = part[:, :A], part[:, A:]
                u, v = uv[b, 0:8, at], uv[b, 8:16, at]
                edge[k] = edge[k] + (re * u + im * v)
                if k:
                    turn[k] = turn[k] + (re * v - im * u)
        c1, s1, c2, s2 = geo[b, C1], geo[b, S1], geo[b, C2], geo[b, S2]
        weighted = edge[0] + c1 * edge[1] + s1 * turn[1] + c2 * edge[2] + s2 * turn[2]
        dlength = -jnp.sum(rate_row[None] * weighted, axis=2, keepdims=True)
        dc2 = jnp.sum(edge[2], axis=2, keepdims=True)
        ds2 = jnp.sum(turn[2], axis=2, keepdims=True)
        dc1 = jnp.sum(edge[1], axis=2, keepdims=True) + 2.0 * (c1 * dc2 + s1 * ds2)
        ds1 = jnp.sum(turn[1], axis=2, keepdims=True) + 2.0 * (c1 * ds2 - s1 * dc2)
        along = dc1 * c1 + ds1 * s1
        planar = geo[b, PLANAR]
        grads = (
            (dc1 - along * c1) / planar + dlength * geo[b, LX],
            (ds1 - along * s1) / planar + dlength * geo[b, LY],
            dlength * geo[b, LZ],
        )
        where = mask[b] - ownmask[None]
        for axis in range(3):
            ftile[b * 3 + axis : b * 3 + axis + 1, :] = jnp.sum(
                jnp.sum(where * grads[axis], axis=0), axis=0, keepdims=True
            )

    def backward(b, spreads):
        with scope(f"bhead{b}"):
            dsig, gate = backward_head(b)
        if spreads:
            with scope(f"b{b}0"):
                mix_back(b, 0, dsig, gate)
                mix_back(b, 1, dsig, gate)
                spread_back(b, 0)
            send_back(b, 0)
            with scope(f"b{b}1"):
                mix_back(b, 2, dsig, gate)
                spread_back(b, 1)
            send_back(b, 1)
            with scope(f"b{b}2"):
                spread_back(b, 2)
            send_back(b, 2)
        else:
            with scope(f"b{b}first"):
                for k in range(3):
                    mix_back(b, k, dsig, gate)
        with scope(f"coord{b}"):
            coordinates(b)
        if spreads:
            with scope(f"comb{b}"):
                combine(b)

    with scope("relay0"):
        relay(0)
    forward(0)

    @pl.when(seg == last)
    def _():
        backward(0, True)

    forward(1)

    @pl.when((seg > 0) & (seg < last))
    def _():
        backward(0, True)

    @pl.when(seg == 0)
    def _():
        backward(0, False)
        backward(1, False)

    @pl.when(seg > 0)
    def _():
        backward(1, True)

    with scope("final"):
        for step, kind in ends:
            end_copy(step, kind).start()
        grecv[seg, 1] = ftile[...]
        for step, kind in ends:
            end_copy(step, kind).wait_recv()
    totals = []
    for slot in range(3):
        total = grecv[0, slot]
        for other in range(1, segments):
            total = total + grecv[other, slot]
        totals.append(total)
    result = totals[1] + jnp.where(row < 6, pltpu.roll(totals[0], C - A, 1) + pltpu.roll(totals[2], A, 1), 0.0)
    result = pltpu.roll(result, C - A, 1)
    for axis in range(3):
        for b in range(BATCHES):
            out_p[axis, b : b + 1] = result[b * 3 + axis : b * 3 + axis + 1, 0:A]
    out_e[...] = result[6:8, 0:A]

    with scope("drain"):
        for kind in range(2):
            place_copy(kind).wait_send()
        for step, kind in ends:
            end_copy(step, kind).wait_send()
        for b in range(BATCHES):
            for k in range(3):
                near_copy(b, k).wait_send()

        @pl.when((seg == 0) | inner)
        def _():
            for b in range(BATCHES):
                for k in range(3):
                    first_copy(b, k).wait_send()

        @pl.when(seg < last)
        def _():
            for b in range(BATCHES):
                for k in range(3):
                    up_copy(b, k).wait_send()
                    pl.when(cross)(far_copy(b, k).wait_send)

        @pl.when(seg > 0)
        def _():
            for b in range(BATCHES):
                for k in range(3):
                    down_copy(b, k).wait_send()
                    back_near_copy(b, k).wait_send()
                    back_far_copy(b, k).wait_send()


def solution(mesh):
    segments = mesh.shape["segment"]
    vmem = pl.BlockSpec(memory_space=pltpu.VMEM)
    hbm = pl.BlockSpec(memory_space=pltpu.HBM)
    dma = pltpu.SemaphoreType.DMA
    B = BATCHES

    def on_device(
        node_states, species, species_table, places, sources, radial_rate, zero_weight, one_weight, two_weight,
        read_weight, energy_grad,
    ):
        energies, grads = pl.pallas_call(
            kernel,
            out_shape=(
                jax.ShapeDtypeStruct((B, A), F32),
                jax.ShapeDtypeStruct((3, B, A), F32),
            ),
            in_specs=[hbm] * 11,
            out_specs=(vmem, vmem),
            scratch_shapes=[
                pltpu.VMEM((3, B, A), F32),
                pltpu.VMEM((B, A), F32),
                pltpu.VMEM((B, 29, A, C), BF16),
                pltpu.VMEM((B, A), jnp.int32),
                pltpu.VMEM(species_table.shape, BF16),
                pltpu.VMEM((B, A, NEIGH), jnp.int32),
                pltpu.VMEM((1, C), F32),
                pltpu.VMEM((1, C), F32),
                pltpu.VMEM((7 * C, 7 * C), BF16),
                pltpu.VMEM((2, 6 * C, 6 * C), BF16),
                pltpu.VMEM((2, 5 * C, 5 * C), BF16),
                pltpu.VMEM((B, 3, 16, WIDTH), BF16),
                pltpu.VMEM((B, 16, WIDTH), BF16),
                pltpu.VMEM((B, NEIGH * 16, WIDTH), BF16),
                pltpu.VMEM((B, 16, WIDTH), F32),
                pltpu.VMEM((B, A, C), F32),
                pltpu.VMEM((B, A, C), F32),
                pltpu.VMEM((B, NEIGH * 16, 48), BF16),
                pltpu.VMEM((B, 48, NEIGH * 16), BF16),
                pltpu.VMEM((B, NEIGH, A, C), F32),
                pltpu.VMEM((B, 9, NEIGH, A, C), F32),
                pltpu.VMEM((B, 16, WIDTH), BF16),
                pltpu.VMEM((B, 16, WIDTH), F32),
                pltpu.VMEM((B, 16, WIDTH), F32),
                pltpu.VMEM((NEIGH * 16, WIDTH), BF16),
                pltpu.VMEM((B, 16, WIDTH), F32),
                pltpu.VMEM((B, 2, 16, WIDTH), BF16),
                pltpu.VMEM((B, 16, WIDTH), BF16),
                pltpu.VMEM((B, 16, WIDTH), BF16),
                pltpu.VMEM((B, 16, WIDTH), BF16),
                pltpu.VMEM((B, 16, WIDTH), BF16),
                pltpu.VMEM((3, A, C), F32),
                pltpu.VMEM((3, A, C), F32),
                pltpu.VMEM((A, C), F32),
                pltpu.VMEM((segments, 3, A, C), F32),
                dma((11,)),
                dma((2,)),
                dma((2,)),
                *[dma((B, 3))] * 14,
                dma((segments, 3)),
                dma((segments, 3)),
            ],
            compiler_params=pltpu.CompilerParams(
                collective_id=0, has_side_effects=True, vmem_limit_bytes=67043328
            ),
        )(
            places.transpose(1, 0, 2), energy_grad, node_states.transpose(0, 2, 1, 3), species, species_table, sources,
            radial_rate, read_weight.reshape(1, C), zero_weight, one_weight, two_weight,
        )
        return energies, grads.transpose(1, 0, 2)

    in_specs = (
        P(None, "space", None, None),
        P(None, "space"),
        P(),
        P(None, None, "space"),
        P(None, "space", None),
        P("segment", None),
        P("segment", None, None),
        P("segment", None, None, None),
        P("segment", None, None, None),
        P(),
        P(None, "space"),
    )
    out_specs = (P(None, "space"), P(None, None, "space"))
    return jax.shard_map(on_device, mesh=mesh, in_specs=in_specs, out_specs=out_specs, check_vma=False)
```

```python
import contextlib
import jax
import jax.numpy as jnp
from jax import lax
from jax.experimental import pallas as pl
from jax.experimental.pallas import tpu as pltpu
from jax.sharding import PartitionSpec as P

A = 8
NEIGH = 8
C = 128
BATCHES = 2
SLAB_DEPTH = 2.0
ROW = 8
MESH = pl.DeviceIdType.MESH
F32 = jnp.float32
BF16 = jnp.bfloat16

CHUNKS = ((0, 512), (512, 768), (1280, 640))
WIDTH = 1920
UPPER = (0, 1, 2, 3, 7, 8, 9, 10, 11, 12, 19, 20, 21, 22, 23)
LOWER = (4, 5, 6, None, 13, 14, 15, 16, 17, 18, 24, 25, 26, 27, 28)
SCOPES = False
DIRECT_MIDDLE = 0
DIRECT_END = 0
RAD, C1, S1, C2, S2, LX, LY, LZ, PLANAR = range(9)


def dot(x, y):
    return lax.dot_general(x, y, (((1,), (0,)), ((), ())), preferred_element_type=F32)


def dot_t(x, y):
    return lax.dot_general(x, y, (((1,), (1,)), ((), ())), preferred_element_type=F32)


def scope(name):
    return jax.named_scope(name) if SCOPES else contextlib.nullcontext()


def halves(x):
    high = x.astype(BF16).astype(F32)
    return jnp.concatenate([high, x - high], axis=0).astype(BF16)


def kernel(
    places_hbm, egrad_hbm, node_hbm, species_hbm, table_hbm, sources_hbm, rate_hbm, read_hbm, wz_hbm, w1_hbm, w2_hbm,
    out_e, out_p,
    places, egrad, node, species, table, sources, rate, read, wz, w1, w2, ext, yout, scaled, pooled, signal, last_top, gmat, gtr, mask, geo, ct, du, uv, dmat,
    ownsum, hsend, hrecv, ctfar, ysend, ptile, precv, ftile, grecv,
    isem, psem_s, psem_r, f0_s, fn_s, fn_r, ff_s, ff_r, fy_s, fy_r, bn_s, bn_r, bf_s, bf_r, by_s, by_r, e_s, e_r,
):
    seg = lax.axis_index("segment")
    slab = lax.axis_index("space")
    segments = lax.axis_size("segment")
    slabs = lax.axis_size("space")
    core = lax.rem(slab, 2)
    near = slab + 1 - 2 * core
    far = lax.rem(slab + slabs + 2 * core - 1, slabs)
    near_slot = 2 * core
    far_slot = 2 - 2 * core
    row_of_slabs = min(ROW, slabs)
    place_in_row = lax.rem(slab, row_of_slabs)
    cross = (place_in_row == 0) | (place_in_row == row_of_slabs - 1)
    inner = jnp.logical_not(cross)
    last = segments - 1
    up = lax.rem(seg + 1, segments)
    down = lax.rem(seg + segments - 1, segments)
    factor = NEIGH ** (-0.5)
    lane = lax.broadcasted_iota(jnp.int32, (A, C), 1)
    row = lax.broadcasted_iota(jnp.int32, (A, C), 0)
    ownmask = jnp.where(lane == row + A, 1.0, 0.0).astype(F32)

    inputs = (
        (places_hbm, places), (egrad_hbm, egrad), (node_hbm, node), (species_hbm, species), (table_hbm, table),
        (sources_hbm, sources), (rate_hbm, rate), (read_hbm, read), (wz_hbm.at[0], wz), (w1_hbm.at[0], w1),
        (w2_hbm.at[0], w2),
    )
    inputs = [pltpu.make_async_copy(src, dst, isem.at[i]) for i, (src, dst) in enumerate(inputs)]
    loads = inputs[8:]
    for load in inputs:
        load.start()

    barrier = pltpu.get_barrier_semaphore()
    for target in (near, far):
        pl.semaphore_signal(barrier, inc=1, device_id={"space": target}, device_id_type=MESH)

    @pl.when(seg > 0)
    def _():
        pl.semaphore_signal(barrier, inc=1, device_id={"segment": down}, device_id_type=MESH)

    @pl.when(seg < last)
    def _():
        pl.semaphore_signal(barrier, inc=1, device_id={"segment": up}, device_id_type=MESH)

    greeted = 2 + jnp.minimum(seg, 1) + jnp.minimum(last - seg, 1)

    def remote(src, dst, send, recv, target):
        return pltpu.make_async_remote_copy(
            src_ref=src, dst_ref=dst, send_sem=send, recv_sem=recv, device_id=target, device_id_type=MESH
        )

    def cols(k):
        return pl.ds(CHUNKS[k][0], CHUNKS[k][1])

    def place_copy(kind):
        return remote(
            ptile.at[(far_slot, near_slot)[kind]], precv.at[(far_slot, near_slot)[kind]],
            psem_s.at[kind], psem_r.at[kind], {"space": (far, near)[kind]},
        )

    def near_copy(b, k):
        return remote(
            ext.at[b, 1, :, cols(k)], ext.at[b, near_slot, :, cols(k)], fn_s.at[b, k], fn_r.at[b, k], {"space": near}
        )

    def first_copy(b, k):
        return remote(
            ext.at[b, 1, :, cols(k)], ext.at[b, far_slot, :, cols(k)], f0_s.at[b, k], ff_r.at[b, k], {"space": far}
        )

    def far_copy(b, k):
        return remote(
            yout.at[b, :, cols(k)], ext.at[b, far_slot, :, cols(k)], ff_s.at[b, k], ff_r.at[b, k],
            {"segment": up, "space": far},
        )

    def up_copy(b, k):
        return remote(
            yout.at[b, :, cols(k)], ext.at[b, 1, :, cols(k)], fy_s.at[b, k], fy_r.at[b, k], {"segment": up}
        )

    def back_near_copy(b, k):
        return remote(
            hsend.at[b, 0, :, cols(k)], hrecv.at[b, :, cols(k)], bn_s.at[b, k], bn_r.at[b, k], {"space": near}
        )

    middle = (place_in_row == row_of_slabs // 2) | (place_in_row == row_of_slabs // 2 - 1)
    bound = jnp.where(cross, 0, jnp.where(middle, DIRECT_MIDDLE, DIRECT_END))

    def straight(k):
        return k >= bound

    def back_far_copy(b, k):
        return remote(
            hsend.at[b, 1, :, cols(k)], ctfar.at[b, :, cols(k)], bf_s.at[b, k], bf_r.at[b, k],
            {"segment": jnp.where(straight(k), down, seg), "space": far},
        )

    def down_copy(b, k):
        return remote(
            ysend.at[b, :, cols(k)], ct.at[b, :, cols(k)], by_s.at[b, k], by_r.at[b, k], {"segment": down}
        )

    def end_copy(step, kind):
        return remote(
            ftile, grecv.at[seg, (far_slot, near_slot, 1)[kind]], e_s.at[step, kind], e_r.at[step, kind],
            {"segment": lax.rem(seg + step, segments), "space": (far, near, slab)[kind]},
        )

    ends = [(step, kind) for step in range(segments) for kind in range(3) if step or kind < 2]

    ptile[1] = jnp.zeros((A, C), F32)
    with scope("input"):
        for load in inputs[:8]:
            load.wait()
    for axis in range(3):
        for b in range(BATCHES):
            ptile[1, b * 3 + axis : b * 3 + axis + 1, 0:A] = places[axis, b : b + 1]
    ptile[1, 6:8, 0:A] = egrad[...]
    base = ptile[1]
    ptile[0] = base
    ptile[2] = pltpu.roll(base, 16, 1)
    own_tile = pltpu.roll(base, A, 1)

    def make_start(b):
        kind = jnp.sum(
            jnp.where(lane == row, jnp.broadcast_to(spec_tile[b : b + 1], (A, C)), 0.0), axis=1, keepdims=True
        )
        onehot = jnp.where(lane.astype(F32) == kind, 1.0, 0.0).astype(BF16)
        embed = dot(onehot[:, : table.shape[0]], table[...])
        for t in range(15):
            upper = node[b, UPPER[t]].astype(F32)
            if t == 0:
                upper = upper + embed
            if LOWER[t] is None:
                lower = jnp.zeros((A, C), F32)
            else:
                lower = node[b, LOWER[t]].astype(F32)
            ext[b, 1, :, t * C : (t + 1) * C] = jnp.concatenate([upper, lower], axis=0).astype(BF16)

    spec_tile = jnp.concatenate(
        [species[...].astype(F32), jnp.zeros((BATCHES, C - A), F32)], axis=1
    )

    with scope("start"):

        @pl.when(seg == 0)
        def _():
            for b in range(BATCHES):
                make_start(b)

    with scope("barrier"):
        pl.semaphore_wait(barrier, greeted)

    for kind in range(2):
        place_copy(kind).start()

    @pl.when(seg == 0)
    def _():
        for b in range(BATCHES):
            for k in range(3):
                first_copy(b, k).start()
                near_copy(b, k).start()

    lane3 = lax.broadcasted_iota(jnp.int32, (NEIGH, A, C), 2)
    lane_local = (lane3 >> 4) * A + (lane3 & 7)
    lane_part = (lane3 >> 3) & 1

    def make_index(b):
        index = sources[b]
        window = (index >> 3) - slab + 1
        window = jnp.where(window < 0, window + slabs, window)
        window = jnp.where(window >= slabs, window - slabs, window)
        local = window * A + (index & 7)
        local = jnp.concatenate([jnp.broadcast_to(local[:, j : j + 1], (A, C))[None] for j in range(NEIGH)], axis=0)
        mask[b] = jnp.where(local == lane3, 1.0, 0.0).astype(F32)
        same = local == lane_local
        picks = jnp.concatenate(
            [
                jnp.where(same & (lane_part == 0), 1.0, 0.0).astype(F32),
                jnp.where(same & (lane_part == 1), 1.0, 0.0).astype(F32),
            ],
            axis=1,
        ).reshape(2 * NEIGH * A, C)
        gmat[b] = picks[:, :48].astype(BF16)
        gtr[b] = picks.T[:48].astype(BF16)

    with scope("index"):
        for b in range(BATCHES):
            make_index(b)

    with scope("places"):
        for kind in range(2):
            place_copy(kind).wait_recv()
    around = precv[0] + own_tile + precv[2]
    elevation = jnp.where(lane < A, -SLAB_DEPTH, jnp.where(lane < 2 * A, 0.0, SLAB_DEPTH)).astype(F32)[0:1]
    rate_row = rate[...]

    def make_geometry(b):
        picks = mask[b]
        offsets = []
        for axis in range(3):
            line = around[b * 3 + axis : b * 3 + axis + 1]
            raised = line + elevation if axis == 2 else line
            there = jnp.sum(picks * raised[None], axis=2, keepdims=True)
            here = jnp.sum(ownmask * line, axis=1, keepdims=True)
            offsets.append(jnp.broadcast_to(there - here[None], (NEIGH, A, C)))
        ox, oy, oz = offsets
        length = jnp.sqrt(ox * ox + oy * oy + oz * oz + 1.0)
        planar = jnp.sqrt(ox * ox + oy * oy + 1.0)
        c1 = ox / planar
        s1 = oy / planar
        geo[b, RAD] = jnp.exp(-rate_row[None] * length)
        geo[b, C1] = c1
        geo[b, S1] = s1
        geo[b, C2] = c1 * c1 - s1 * s1
        geo[b, S2] = 2.0 * c1 * s1
        geo[b, LX] = ox / length
        geo[b, LY] = oy / length
        geo[b, LZ] = oz / length
        geo[b, PLANAR] = planar

    with scope("geometry"):
        for b in range(BATCHES):
            make_geometry(b)

    weights = (None, w1, w2)

    def relay(b, where):
        @pl.when(where)
        def _():
            for k in range(3):
                up_copy(b, k).wait_recv()
                near_copy(b, k).start()
                pl.when(inner)(first_copy(b, k).start)

    def gather(b, k):
        c0, n = CHUNKS[k]
        with scope(f"fwait{b}{k}"):
            near_copy(b, k).wait_recv()
            far_copy(b, k).wait_recv()
        picked = dot(gmat[b], ext[b, :, :, c0 : c0 + n].reshape(48, n))
        radial = geo[b, RAD]
        radial = jnp.concatenate([radial, radial], axis=1)
        if k:
            cos, sin = geo[b, (C1, C2)[k - 1]], geo[b, (S1, S2)[k - 1]]
        sums = []
        for t in range(n // C):
            part = picked[:, t * C : (t + 1) * C].reshape(NEIGH, 16, C)
            rounded = (part * radial).astype(BF16)
            scaled[b, :, c0 + t * C : c0 + (t + 1) * C] = rounded.reshape(NEIGH * 16, C)
            part = rounded.astype(F32)
            if k:
                re, im = part[:, :A], part[:, A:]
                sums.append(
                    jnp.concatenate(
                        [jnp.sum(cos * re - sin * im, axis=0), jnp.sum(sin * re + cos * im, axis=0)], axis=0
                    )
                )
            else:
                sums.append(jnp.sum(part, axis=0))
        return sums

    def mix(b, k, sums):
        c0, n = CHUNKS[k]
        if k:
            both = halves(jnp.concatenate(sums, axis=1))
            p = dot(both, weights[k][0])
            q = dot(both, weights[k][1])
            p = p[:16] + p[16:]
            q = q[:16] + q[16:]
            pooled[b, 0:8, c0 : c0 + n] = (p[:8] - q[8:]) * factor
            pooled[b, 8:16, c0 : c0 + n] = (p[8:] + q[:8]) * factor
        else:
            whole = jnp.concatenate([x[:8] for x in sums] + [x[8:] for x in sums[:3]], axis=1)
            z = dot(halves(whole), wz[...])
            z = (z[:8] + z[8:]) * factor
            pooled[b, 0:8, 0:512] = z[:, :512]
            pooled[b, 8:16, 0:384] = z[:, 512:]
            pooled[b, 8:16, 384:512] = jnp.zeros((A, C), F32)

    def forward_end(b):
        total = jnp.zeros((16, C), F32)
        for t in range(4, 15):
            value = pooled[b, :, t * C : (t + 1) * C]
            total = total + value * value
        sig = pooled[b, 0:8, 0:C] + total[:8] + total[8:]
        signal[b] = sig
        gate = jax.nn.sigmoid(sig)
        silu = sig * gate
        gate2 = jnp.concatenate([gate, gate], axis=0)
        for t in range(15):
            own = ext[b, 1, :, t * C : (t + 1) * C].astype(F32)
            added = gate2 * pooled[b, :, t * C : (t + 1) * C]
            if t == 0:
                added = jnp.concatenate([silu, added[8:]], axis=0)
            new = own + added
            if t == 0:
                last_top[b] = new[:8]
            yout[b, :, t * C : (t + 1) * C] = new.astype(BF16)

        @pl.when(seg < last)
        def _():
            for k in range(3):
                up_copy(b, k).start()
                pl.when(cross)(far_copy(b, k).start)

    def forward(b):
        if b == 0:
            for load in loads:
                load.wait()
        with scope(f"f{b}0"):
            mix(b, 0, gather(b, 0))
        with scope(f"f{b}1"):
            sums = gather(b, 1)
        if b == 0:
            with scope("relay1"):
                relay(1, seg == 1)
        else:
            with scope("comb0"):

                @pl.when(seg == last)
                def _():
                    combine(0)

        with scope(f"f{b}2"):
            more = gather(b, 2)
            mix(b, 1, sums)
            mix(b, 2, more)
        with scope(f"fend{b}"):
            forward_end(b)

    read_row = read[...]

    def backward_head(b):
        @pl.when(seg == last)
        def _():
            top = last_top[b]
            gate = jax.nn.sigmoid(top)
            energy = jnp.sum(read_row * (top * gate), axis=1, keepdims=True)
            seed = jnp.sum(ownmask * own_tile[6 + b : 7 + b], axis=1, keepdims=True)
            ftile[6 + b : 7 + b, :] = jnp.sum(ownmask * energy, axis=0, keepdims=True)
            du[b] = jnp.zeros((16, WIDTH), F32)
            du[b, 0:8, 0:C] = seed * read_row * (gate * (1.0 + top * (1.0 - gate)))

        @pl.when(seg < last)
        def _():
            ftile[6 + b : 7 + b, :] = jnp.zeros((1, C), F32)
            for k in range(3):
                down_copy(b, k).wait_recv()
                du[b, :, cols(k)] = ct[b, :, cols(k)].astype(F32)

            for k in range(3):

                @pl.when(straight(k))
                def _():
                    back_far_copy(b, k).wait_recv()
                    du[b, :, cols(k)] += ctfar[b, :, cols(k)].astype(F32)

        sig = signal[b]
        gate = jax.nn.sigmoid(sig)
        total = jnp.zeros((16, C), F32)
        for t in range(15):
            value = du[b, :, t * C : (t + 1) * C] * pooled[b, :, t * C : (t + 1) * C]
            if t == 0:
                value = jnp.concatenate([jnp.zeros((A, C), F32), value[8:]], axis=0)
            total = total + value
        dgate = total[:8] + total[8:]
        dsig = du[b, 0:8, 0:C] * (gate * (1.0 + sig * (1.0 - gate))) + dgate * (gate * (1.0 - gate))
        return dsig, gate

    def mix_back(b, k, dsig, gate):
        c0, n = CHUNKS[k]
        gate2 = jnp.concatenate([gate, gate], axis=0)
        dsig2 = jnp.concatenate([dsig, dsig], axis=0)
        parts = []
        for t in range(n // C):
            at = slice(c0 + t * C, c0 + (t + 1) * C)
            part = gate2 * du[b, :, at]
            if k:
                part = part + 2.0 * pooled[b, :, at] * dsig2
            elif t == 0:
                part = jnp.concatenate([dsig, part[8:]], axis=0)
            parts.append(part * factor)
        if k:
            both = halves(jnp.concatenate(parts, axis=1))
            p = dot_t(both, weights[k][0])
            q = dot_t(both, weights[k][1])
            p = p[:16] + p[16:]
            q = q[:16] + q[16:]
            uv[b, 0:8, c0 : c0 + n] = p[:8] + q[8:]
            uv[b, 8:16, c0 : c0 + n] = p[8:] - q[:8]
        else:
            whole = jnp.concatenate([x[:8] for x in parts] + [x[8:] for x in parts[:3]], axis=1)
            z = dot_t(halves(whole), wz[...])
            z = z[:8] + z[8:]
            uv[b, 0:8, 0:512] = z[:, :512]
            uv[b, 8:16, 0:384] = z[:, 512:]
            uv[b, 8:16, 384:512] = jnp.zeros((A, C), F32)

    def spread_back(b, k):
        c0, n = CHUNKS[k]
        radial = geo[b, RAD]
        if k:
            rc, rs = radial * geo[b, (C1, C2)[k - 1]], radial * geo[b, (S1, S2)[k - 1]]
        for t in range(n // C):
            at = slice(c0 + t * C, c0 + (t + 1) * C)
            u, v = uv[b, 0:8, at], uv[b, 8:16, at]
            if k:
                upper, lower = rc * u + rs * v, rc * v - rs * u
            else:
                upper, lower = radial * u, radial * v
            dmat[:, at] = jnp.concatenate([upper, lower], axis=1).reshape(NEIGH * 16, C).astype(BF16)
        spread = dot(gtr[b], dmat[:, c0 : c0 + n])
        hsend[b, 1 - core, :, c0 : c0 + n] = spread[0:16].astype(BF16)
        hsend[b, core, :, c0 : c0 + n] = spread[32:48].astype(BF16)
        ownsum[b, :, c0 : c0 + n] = spread[16:32] + du[b, :, c0 : c0 + n]
    def send_back(b, k):
        back_near_copy(b, k).start()
        back_far_copy(b, k).start()

    def combine(b):
        for k in range(3):
            back_near_copy(b, k).wait_recv()
            total = ownsum.at[b, :, cols(k)]
            total[...] += hrecv[b, :, cols(k)].astype(F32)
            if k < max(DIRECT_MIDDLE, DIRECT_END):

                @pl.when(jnp.logical_not(straight(k)))
                def _():
                    back_far_copy(b, k).wait_recv()
                    total[...] += ctfar[b, :, cols(k)].astype(F32)

            ysend[b, :, cols(k)] = total[...].astype(BF16)
            down_copy(b, k).start()

    def coordinates(b):
        edge = [jnp.zeros((NEIGH, A, C), F32) for _ in range(3)]
        turn = [None, jnp.zeros((NEIGH, A, C), F32), jnp.zeros((NEIGH, A, C), F32)]
        for k in range(3):
            c0, n = CHUNKS[k]
            for t in range(n // C):
                at = slice(c0 + t * C, c0 + (t + 1) * C)
                part = scaled[b, :, at].astype(F32).reshape(NEIGH, 16, C)
                re, im = part[:, :A], part[:, A:]
                u, v = uv[b, 0:8, at], uv[b, 8:16, at]
                edge[k] = edge[k] + (re * u + im * v)
                if k:
                    turn[k] = turn[k] + (re * v - im * u)
        c1, s1, c2, s2 = geo[b, C1], geo[b, S1], geo[b, C2], geo[b, S2]
        weighted = edge[0] + c1 * edge[1] + s1 * turn[1] + c2 * edge[2] + s2 * turn[2]
        dlength = -jnp.sum(rate_row[None] * weighted, axis=2, keepdims=True)
        dc2 = jnp.sum(edge[2], axis=2, keepdims=True)
        ds2 = jnp.sum(turn[2], axis=2, keepdims=True)
        dc1 = jnp.sum(edge[1], axis=2, keepdims=True) + 2.0 * (c1 * dc2 + s1 * ds2)
        ds1 = jnp.sum(turn[1], axis=2, keepdims=True) + 2.0 * (c1 * ds2 - s1 * dc2)
        along = dc1 * c1 + ds1 * s1
        planar = geo[b, PLANAR]
        grads = (
            (dc1 - along * c1) / planar + dlength * geo[b, LX],
            (ds1 - along * s1) / planar + dlength * geo[b, LY],
            dlength * geo[b, LZ],
        )
        where = mask[b] - ownmask[None]
        for axis in range(3):
            ftile[b * 3 + axis : b * 3 + axis + 1, :] = jnp.sum(
                jnp.sum(where * grads[axis], axis=0), axis=0, keepdims=True
            )

    def backward(b, spreads, ends=True):
        with scope(f"bhead{b}"):
            dsig, gate = backward_head(b)
        if spreads:
            with scope(f"b{b}0"):
                mix_back(b, 0, dsig, gate)
                mix_back(b, 1, dsig, gate)
                spread_back(b, 0)
            send_back(b, 0)
            if not ends:
                with scope("relay1m"):
                    relay(1, seg == last)
            with scope(f"b{b}1"):
                mix_back(b, 2, dsig, gate)
                spread_back(b, 1)
            send_back(b, 1)
            with scope(f"b{b}2"):
                spread_back(b, 2)
            send_back(b, 2)
        else:
            with scope(f"b{b}first"):
                for k in range(3):
                    mix_back(b, k, dsig, gate)
        with scope(f"coord{b}"):
            coordinates(b)
        if spreads and ends:
            with scope(f"comb{b}"):
                combine(b)

    with scope("relay0"):
        relay(0, seg > 0)
    forward(0)

    with scope("relay1l"):
        relay(1, (seg > 1) & (seg < last))

    @pl.when(seg == last)
    def _():
        backward(0, True, False)

    forward(1)

    @pl.when((seg > 0) & (seg < last))
    def _():
        backward(0, True)

    @pl.when(seg == 0)
    def _():
        backward(0, False)
        backward(1, False)

    @pl.when(seg > 0)
    def _():
        backward(1, True)

    with scope("final"):
        for step, kind in ends:
            end_copy(step, kind).start()
        grecv[seg, 1] = ftile[...]
        for step, kind in ends:
            end_copy(step, kind).wait_recv()
    totals = []
    for slot in range(3):
        total = grecv[0, slot]
        for other in range(1, segments):
            total = total + grecv[other, slot]
        totals.append(total)
    result = totals[1] + jnp.where(row < 6, pltpu.roll(totals[0], C - A, 1) + pltpu.roll(totals[2], A, 1), 0.0)
    result = pltpu.roll(result, C - A, 1)
    for axis in range(3):
        for b in range(BATCHES):
            out_p[axis, b : b + 1] = result[b * 3 + axis : b * 3 + axis + 1, 0:A]
    out_e[...] = result[6:8, 0:A]

    with scope("drain"):
        for kind in range(2):
            place_copy(kind).wait_send()
        for step, kind in ends:
            end_copy(step, kind).wait_send()
        for b in range(BATCHES):
            for k in range(3):
                near_copy(b, k).wait_send()

        @pl.when((seg == 0) | inner)
        def _():
            for b in range(BATCHES):
                for k in range(3):
                    first_copy(b, k).wait_send()

        @pl.when(seg < last)
        def _():
            for b in range(BATCHES):
                for k in range(3):
                    up_copy(b, k).wait_send()
                    pl.when(cross)(far_copy(b, k).wait_send)

        @pl.when(seg > 0)
        def _():
            for b in range(BATCHES):
                for k in range(3):
                    down_copy(b, k).wait_send()
                    back_near_copy(b, k).wait_send()
                    back_far_copy(b, k).wait_send()


def solution(mesh):
    segments = mesh.shape["segment"]
    vmem = pl.BlockSpec(memory_space=pltpu.VMEM)
    hbm = pl.BlockSpec(memory_space=pltpu.HBM)
    dma = pltpu.SemaphoreType.DMA
    B = BATCHES

    def on_device(
        node_states, species, species_table, places, sources, radial_rate, zero_weight, one_weight, two_weight,
        read_weight, energy_grad,
    ):
        energies, grads = pl.pallas_call(
            kernel,
            out_shape=(
                jax.ShapeDtypeStruct((B, A), F32),
                jax.ShapeDtypeStruct((3, B, A), F32),
            ),
            in_specs=[hbm] * 11,
            out_specs=(vmem, vmem),
            scratch_shapes=[
                pltpu.VMEM((3, B, A), F32),
                pltpu.VMEM((B, A), F32),
                pltpu.VMEM((B, 29, A, C), BF16),
                pltpu.VMEM((B, A), jnp.int32),
                pltpu.VMEM(species_table.shape, BF16),
                pltpu.VMEM((B, A, NEIGH), jnp.int32),
                pltpu.VMEM((1, C), F32),
                pltpu.VMEM((1, C), F32),
                pltpu.VMEM((7 * C, 7 * C), BF16),
                pltpu.VMEM((2, 6 * C, 6 * C), BF16),
                pltpu.VMEM((2, 5 * C, 5 * C), BF16),
                pltpu.VMEM((B, 3, 16, WIDTH), BF16),
                pltpu.VMEM((B, 16, WIDTH), BF16),
                pltpu.VMEM((B, NEIGH * 16, WIDTH), BF16),
                pltpu.VMEM((B, 16, WIDTH), F32),
                pltpu.VMEM((B, A, C), F32),
                pltpu.VMEM((B, A, C), F32),
                pltpu.VMEM((B, NEIGH * 16, 48), BF16),
                pltpu.VMEM((B, 48, NEIGH * 16), BF16),
                pltpu.VMEM((B, NEIGH, A, C), F32),
                pltpu.VMEM((B, 9, NEIGH, A, C), F32),
                pltpu.VMEM((B, 16, WIDTH), BF16),
                pltpu.VMEM((B, 16, WIDTH), F32),
                pltpu.VMEM((B, 16, WIDTH), F32),
                pltpu.VMEM((NEIGH * 16, WIDTH), BF16),
                pltpu.VMEM((B, 16, WIDTH), F32),
                pltpu.VMEM((B, 2, 16, WIDTH), BF16),
                pltpu.VMEM((B, 16, WIDTH), BF16),
                pltpu.VMEM((B, 16, WIDTH), BF16),
                pltpu.VMEM((B, 16, WIDTH), BF16),
                pltpu.VMEM((3, A, C), F32),
                pltpu.VMEM((3, A, C), F32),
                pltpu.VMEM((A, C), F32),
                pltpu.VMEM((segments, 3, A, C), F32),
                dma((11,)),
                dma((2,)),
                dma((2,)),
                *[dma((B, 3))] * 13,
                dma((segments, 3)),
                dma((segments, 3)),
            ],
            compiler_params=pltpu.CompilerParams(
                collective_id=0, has_side_effects=True, vmem_limit_bytes=67043328
            ),
        )(
            places.transpose(1, 0, 2), energy_grad, node_states.transpose(0, 2, 1, 3), species, species_table, sources,
            radial_rate, read_weight.reshape(1, C), zero_weight, one_weight, two_weight,
        )
        return energies, grads.transpose(1, 0, 2)

    in_specs = (
        P(None, "space", None, None),
        P(None, "space"),
        P(),
        P(None, None, "space"),
        P(None, "space", None),
        P("segment", None),
        P("segment", None, None),
        P("segment", None, None, None),
        P("segment", None, None, None),
        P(),
        P(None, "space"),
    )
    out_specs = (P(None, "space"), P(None, None, "space"))
    return jax.shard_map(on_device, mesh=mesh, in_specs=in_specs, out_specs=out_specs, check_vma=False)
```

```python
import contextlib
import jax
import jax.numpy as jnp
from jax import lax
from jax.experimental import pallas as pl
from jax.experimental.pallas import tpu as pltpu
from jax.sharding import PartitionSpec as P

A = 8
NEIGH = 8
C = 128
BATCHES = 2
SLAB_DEPTH = 2.0
ROW = 8
MESH = pl.DeviceIdType.MESH
F32 = jnp.float32
BF16 = jnp.bfloat16

CHUNKS = ((0, 512), (512, 768), (1280, 640))
WIDTH = 1920
UPPER = (0, 1, 2, 3, 7, 8, 9, 10, 11, 12, 19, 20, 21, 22, 23)
LOWER = (4, 5, 6, None, 13, 14, 15, 16, 17, 18, 24, 25, 26, 27, 28)
SCOPES = False
DIRECT_MIDDLE = 0
DIRECT_END = 0
EARLY, LATE = (0, 1), (2,)
RAD, C1, S1, C2, S2, LX, LY, LZ, PLANAR = range(9)


def dot(x, y):
    return lax.dot_general(x, y, (((1,), (0,)), ((), ())), preferred_element_type=F32)


def dot_t(x, y):
    return lax.dot_general(x, y, (((1,), (1,)), ((), ())), preferred_element_type=F32)


def scope(name):
    return jax.named_scope(name) if SCOPES else contextlib.nullcontext()


def halves(x):
    high = x.astype(BF16).astype(F32)
    return jnp.concatenate([high, x - high], axis=0).astype(BF16)


def kernel(
    places_hbm, egrad_hbm, node_hbm, species_hbm, table_hbm, sources_hbm, rate_hbm, read_hbm, wz_hbm, w1_hbm, w2_hbm,
    out_e, out_p,
    places, egrad, node, species, table, sources, rate, read, wz, w1, w2, ext, yout, scaled, pooled, signal, last_top, gmat, gtr, mask, geo, ct, du, uv, dmat,
    ownsum, hsend, hrecv, ctfar, ysend, ptile, precv, ftile, grecv,
    isem, psem_s, psem_r, f0_s, fn_s, fn_r, ff_s, ff_r, fy_s, fy_r, bn_s, bn_r, bf_s, bf_r, by_s, by_r, e_s, e_r,
):
    seg = lax.axis_index("segment")
    slab = lax.axis_index("space")
    segments = lax.axis_size("segment")
    slabs = lax.axis_size("space")
    core = lax.rem(slab, 2)
    near = slab + 1 - 2 * core
    far = lax.rem(slab + slabs + 2 * core - 1, slabs)
    near_slot = 2 * core
    far_slot = 2 - 2 * core
    row_of_slabs = min(ROW, slabs)
    place_in_row = lax.rem(slab, row_of_slabs)
    cross = (place_in_row == 0) | (place_in_row == row_of_slabs - 1)
    inner = jnp.logical_not(cross)
    last = segments - 1
    up = lax.rem(seg + 1, segments)
    down = lax.rem(seg + segments - 1, segments)
    factor = NEIGH ** (-0.5)
    lane = lax.broadcasted_iota(jnp.int32, (A, C), 1)
    row = lax.broadcasted_iota(jnp.int32, (A, C), 0)
    ownmask = jnp.where(lane == row + A, 1.0, 0.0).astype(F32)

    inputs = (
        (places_hbm, places), (egrad_hbm, egrad), (node_hbm, node), (species_hbm, species), (table_hbm, table),
        (sources_hbm, sources), (rate_hbm, rate), (read_hbm, read), (wz_hbm.at[0], wz), (w1_hbm.at[0], w1),
        (w2_hbm.at[0], w2),
    )
    inputs = [pltpu.make_async_copy(src, dst, isem.at[i]) for i, (src, dst) in enumerate(inputs)]
    loads = inputs[8:]
    for load in inputs:
        load.start()

    barrier = pltpu.get_barrier_semaphore()
    for target in (near, far):
        pl.semaphore_signal(barrier, inc=1, device_id={"space": target}, device_id_type=MESH)

    @pl.when(seg > 0)
    def _():
        pl.semaphore_signal(barrier, inc=1, device_id={"segment": down}, device_id_type=MESH)

    @pl.when(seg < last)
    def _():
        pl.semaphore_signal(barrier, inc=1, device_id={"segment": up}, device_id_type=MESH)

    greeted = 2 + jnp.minimum(seg, 1) + jnp.minimum(last - seg, 1)

    def remote(src, dst, send, recv, target):
        return pltpu.make_async_remote_copy(
            src_ref=src, dst_ref=dst, send_sem=send, recv_sem=recv, device_id=target, device_id_type=MESH
        )

    def cols(k):
        return pl.ds(CHUNKS[k][0], CHUNKS[k][1])

    def place_copy(kind):
        return remote(
            ptile.at[(far_slot, near_slot)[kind]], precv.at[(far_slot, near_slot)[kind]],
            psem_s.at[kind], psem_r.at[kind], {"space": (far, near)[kind]},
        )

    def near_copy(b, k):
        return remote(
            ext.at[b, 1, :, cols(k)], ext.at[b, near_slot, :, cols(k)], fn_s.at[b, k], fn_r.at[b, k], {"space": near}
        )

    def first_copy(b, k):
        return remote(
            ext.at[b, 1, :, cols(k)], ext.at[b, far_slot, :, cols(k)], f0_s.at[b, k], ff_r.at[b, k], {"space": far}
        )

    def far_copy(b, k):
        return remote(
            yout.at[b, :, cols(k)], ext.at[b, far_slot, :, cols(k)], ff_s.at[b, k], ff_r.at[b, k],
            {"segment": up, "space": far},
        )

    def up_copy(b, k):
        return remote(
            yout.at[b, :, cols(k)], ext.at[b, 1, :, cols(k)], fy_s.at[b, k], fy_r.at[b, k], {"segment": up}
        )

    def back_near_copy(b, k):
        return remote(
            hsend.at[b, 0, :, cols(k)], hrecv.at[b, :, cols(k)], bn_s.at[b, k], bn_r.at[b, k], {"space": near}
        )

    middle = (place_in_row == row_of_slabs // 2) | (place_in_row == row_of_slabs // 2 - 1)
    bound = jnp.where(cross, 0, jnp.where(middle, DIRECT_MIDDLE, DIRECT_END))

    def straight(k):
        return k >= bound

    def back_far_copy(b, k):
        return remote(
            hsend.at[b, 1, :, cols(k)], ctfar.at[b, :, cols(k)], bf_s.at[b, k], bf_r.at[b, k],
            {"segment": jnp.where(straight(k), down, seg), "space": far},
        )

    def down_copy(b, k):
        return remote(
            ysend.at[b, :, cols(k)], ct.at[b, :, cols(k)], by_s.at[b, k], by_r.at[b, k], {"segment": down}
        )

    def end_copy(step, kind):
        return remote(
            ftile, grecv.at[seg, (far_slot, near_slot, 1)[kind]], e_s.at[step, kind], e_r.at[step, kind],
            {"segment": lax.rem(seg + step, segments), "space": (far, near, slab)[kind]},
        )

    ends = [(step, kind) for step in range(segments) for kind in range(3) if step or kind < 2]

    ptile[1] = jnp.zeros((A, C), F32)
    with scope("input"):
        for load in inputs[:8]:
            load.wait()
    for axis in range(3):
        for b in range(BATCHES):
            ptile[1, b * 3 + axis : b * 3 + axis + 1, 0:A] = places[axis, b : b + 1]
    ptile[1, 6:8, 0:A] = egrad[...]
    base = ptile[1]
    ptile[0] = base
    ptile[2] = pltpu.roll(base, 16, 1)
    own_tile = pltpu.roll(base, A, 1)

    def make_start(b):
        kind = jnp.sum(
            jnp.where(lane == row, jnp.broadcast_to(spec_tile[b : b + 1], (A, C)), 0.0), axis=1, keepdims=True
        )
        onehot = jnp.where(lane.astype(F32) == kind, 1.0, 0.0).astype(BF16)
        embed = dot(onehot[:, : table.shape[0]], table[...])
        for t in range(15):
            upper = node[b, UPPER[t]].astype(F32)
            if t == 0:
                upper = upper + embed
            if LOWER[t] is None:
                lower = jnp.zeros((A, C), F32)
            else:
                lower = node[b, LOWER[t]].astype(F32)
            ext[b, 1, :, t * C : (t + 1) * C] = jnp.concatenate([upper, lower], axis=0).astype(BF16)

    spec_tile = jnp.concatenate(
        [species[...].astype(F32), jnp.zeros((BATCHES, C - A), F32)], axis=1
    )

    with scope("start"):

        @pl.when(seg == 0)
        def _():
            for b in range(BATCHES):
                make_start(b)

    with scope("barrier"):
        pl.semaphore_wait(barrier, greeted)

    for kind in range(2):
        place_copy(kind).start()

    @pl.when(seg == 0)
    def _():
        for b in range(BATCHES):
            for k in range(3):
                first_copy(b, k).start()
                near_copy(b, k).start()

    lane3 = lax.broadcasted_iota(jnp.int32, (NEIGH, A, C), 2)
    lane_local = (lane3 >> 4) * A + (lane3 & 7)
    lane_part = (lane3 >> 3) & 1

    def make_index(b):
        index = sources[b]
        window = (index >> 3) - slab + 1
        window = jnp.where(window < 0, window + slabs, window)
        window = jnp.where(window >= slabs, window - slabs, window)
        local = window * A + (index & 7)
        local = jnp.concatenate([jnp.broadcast_to(local[:, j : j + 1], (A, C))[None] for j in range(NEIGH)], axis=0)
        mask[b] = jnp.where(local == lane3, 1.0, 0.0).astype(F32)
        same = local == lane_local
        picks = jnp.concatenate(
            [
                jnp.where(same & (lane_part == 0), 1.0, 0.0).astype(F32),
                jnp.where(same & (lane_part == 1), 1.0, 0.0).astype(F32),
            ],
            axis=1,
        ).reshape(2 * NEIGH * A, C)
        gmat[b] = picks[:, :48].astype(BF16)
        gtr[b] = picks.T[:48].astype(BF16)

    with scope("index"):
        for b in range(BATCHES):
            make_index(b)

    with scope("places"):
        for kind in range(2):
            place_copy(kind).wait_recv()
    around = precv[0] + own_tile + precv[2]
    elevation = jnp.where(lane < A, -SLAB_DEPTH, jnp.where(lane < 2 * A, 0.0, SLAB_DEPTH)).astype(F32)[0:1]
    rate_row = rate[...]

    def make_geometry(b):
        picks = mask[b]
        offsets = []
        for axis in range(3):
            line = around[b * 3 + axis : b * 3 + axis + 1]
            raised = line + elevation if axis == 2 else line
            there = jnp.sum(picks * raised[None], axis=2, keepdims=True)
            here = jnp.sum(ownmask * line, axis=1, keepdims=True)
            offsets.append(jnp.broadcast_to(there - here[None], (NEIGH, A, C)))
        ox, oy, oz = offsets
        length = jnp.sqrt(ox * ox + oy * oy + oz * oz + 1.0)
        planar = jnp.sqrt(ox * ox + oy * oy + 1.0)
        c1 = ox / planar
        s1 = oy / planar
        geo[b, RAD] = jnp.exp(-rate_row[None] * length)
        geo[b, C1] = c1
        geo[b, S1] = s1
        geo[b, C2] = c1 * c1 - s1 * s1
        geo[b, S2] = 2.0 * c1 * s1
        geo[b, LX] = ox / length
        geo[b, LY] = oy / length
        geo[b, LZ] = oz / length
        geo[b, PLANAR] = planar

    with scope("geometry"):
        for b in range(BATCHES):
            make_geometry(b)

    weights = (None, w1, w2)

    def relay(b, group, where):
        @pl.when(where)
        def _():
            for k in group:
                up_copy(b, k).wait_recv()
                pl.when(inner)(first_copy(b, k).start)
                near_copy(b, k).start()

    def gather(b, k):
        c0, n = CHUNKS[k]
        with scope(f"fwait{b}{k}"):
            near_copy(b, k).wait_recv()
            far_copy(b, k).wait_recv()
        picked = dot(gmat[b], ext[b, :, :, c0 : c0 + n].reshape(48, n))
        radial = geo[b, RAD]
        radial = jnp.concatenate([radial, radial], axis=1)
        if k:
            cos, sin = geo[b, (C1, C2)[k - 1]], geo[b, (S1, S2)[k - 1]]
        sums = []
        for t in range(n // C):
            part = picked[:, t * C : (t + 1) * C].reshape(NEIGH, 16, C)
            rounded = (part * radial).astype(BF16)
            scaled[b, :, c0 + t * C : c0 + (t + 1) * C] = rounded.reshape(NEIGH * 16, C)
            part = rounded.astype(F32)
            if k:
                re, im = part[:, :A], part[:, A:]
                sums.append(
                    jnp.concatenate(
                        [jnp.sum(cos * re - sin * im, axis=0), jnp.sum(sin * re + cos * im, axis=0)], axis=0
                    )
                )
            else:
                sums.append(jnp.sum(part, axis=0))
        return sums

    def mix(b, k, sums):
        c0, n = CHUNKS[k]
        if k:
            both = halves(jnp.concatenate(sums, axis=1))
            p = dot(both, weights[k][0])
            q = dot(both, weights[k][1])
            p = p[:16] + p[16:]
            q = q[:16] + q[16:]
            pooled[b, 0:8, c0 : c0 + n] = (p[:8] - q[8:]) * factor
            pooled[b, 8:16, c0 : c0 + n] = (p[8:] + q[:8]) * factor
        else:
            whole = jnp.concatenate([x[:8] for x in sums] + [x[8:] for x in sums[:3]], axis=1)
            z = dot(halves(whole), wz[...])
            z = (z[:8] + z[8:]) * factor
            pooled[b, 0:8, 0:512] = z[:, :512]
            pooled[b, 8:16, 0:384] = z[:, 512:]
            pooled[b, 8:16, 384:512] = jnp.zeros((A, C), F32)

    def forward_end(b):
        total = jnp.zeros((16, C), F32)
        for t in range(4, 15):
            value = pooled[b, :, t * C : (t + 1) * C]
            total = total + value * value
        sig = pooled[b, 0:8, 0:C] + total[:8] + total[8:]
        signal[b] = sig
        gate = jax.nn.sigmoid(sig)
        silu = sig * gate
        gate2 = jnp.concatenate([gate, gate], axis=0)
        for t in range(15):
            own = ext[b, 1, :, t * C : (t + 1) * C].astype(F32)
            added = gate2 * pooled[b, :, t * C : (t + 1) * C]
            if t == 0:
                added = jnp.concatenate([silu, added[8:]], axis=0)
            new = own + added
            if t == 0:
                last_top[b] = new[:8]
            yout[b, :, t * C : (t + 1) * C] = new.astype(BF16)

        @pl.when(seg < last)
        def _():
            for k in range(3):
                pl.when(cross)(far_copy(b, k).start)
                up_copy(b, k).start()

    def forward(b):
        if b == 0:
            for load in loads:
                load.wait()
        with scope(f"f{b}0"):
            mix(b, 0, gather(b, 0))
        with scope(f"f{b}1"):
            sums = gather(b, 1)
        if b == 0:
            with scope("relay1"):
                relay(1, range(3), seg == 1)
                relay(1, EARLY, (seg > 1) & (seg < last))
        else:
            with scope("comb0"):

                @pl.when(seg == last)
                def _():
                    combine(0)

        with scope(f"f{b}2"):
            more = gather(b, 2)
            mix(b, 1, sums)
            mix(b, 2, more)
        with scope(f"fend{b}"):
            forward_end(b)

    read_row = read[...]

    def backward_head(b):
        @pl.when(seg == last)
        def _():
            top = last_top[b]
            gate = jax.nn.sigmoid(top)
            energy = jnp.sum(read_row * (top * gate), axis=1, keepdims=True)
            seed = jnp.sum(ownmask * own_tile[6 + b : 7 + b], axis=1, keepdims=True)
            ftile[6 + b : 7 + b, :] = jnp.sum(ownmask * energy, axis=0, keepdims=True)
            du[b] = jnp.zeros((16, WIDTH), F32)
            du[b, 0:8, 0:C] = seed * read_row * (gate * (1.0 + top * (1.0 - gate)))

        def take(group):
            for k in group:
                down_copy(b, k).wait_recv()
                du[b, :, cols(k)] = ct[b, :, cols(k)].astype(F32)

            for k in group:

                @pl.when(straight(k))
                def _():
                    back_far_copy(b, k).wait_recv()
                    du[b, :, cols(k)] += ctfar[b, :, cols(k)].astype(F32)

        @pl.when(seg < last)
        def _():
            ftile[6 + b : 7 + b, :] = jnp.zeros((1, C), F32)
            take((0,))

        sig = signal[b]
        gate = jax.nn.sigmoid(sig)
        rows = [gate * du[b, 0:8, t * C : (t + 1) * C] for t in range(1, 4)]
        rows += [gate * du[b, 8:16, t * C : (t + 1) * C] for t in range(3)]
        early = dot_t(halves(jnp.concatenate(rows, axis=1) * factor), wz[:, C:])
        early = early[:8] + early[8:]

        @pl.when(seg < last)
        def _():
            take((1, 2))

        total = jnp.zeros((16, C), F32)
        for t in range(15):
            value = du[b, :, t * C : (t + 1) * C] * pooled[b, :, t * C : (t + 1) * C]
            if t == 0:
                value = jnp.concatenate([jnp.zeros((A, C), F32), value[8:]], axis=0)
            total = total + value
        dgate = total[:8] + total[8:]
        dsig = du[b, 0:8, 0:C] * (gate * (1.0 + sig * (1.0 - gate))) + dgate * (gate * (1.0 - gate))
        return dsig, gate, early

    def mix_back(b, k, dsig, gate, early):
        c0, n = CHUNKS[k]
        gate2 = jnp.concatenate([gate, gate], axis=0)
        dsig2 = jnp.concatenate([dsig, dsig], axis=0)
        parts = []
        for t in range(n // C if k else 0):
            at = slice(c0 + t * C, c0 + (t + 1) * C)
            parts.append((gate2 * du[b, :, at] + 2.0 * pooled[b, :, at] * dsig2) * factor)
        if k:
            both = halves(jnp.concatenate(parts, axis=1))
            p = dot_t(both, weights[k][0])
            q = dot_t(both, weights[k][1])
            p = p[:16] + p[16:]
            q = q[:16] + q[16:]
            uv[b, 0:8, c0 : c0 + n] = p[:8] + q[8:]
            uv[b, 8:16, c0 : c0 + n] = p[8:] - q[:8]
        else:
            z = dot_t(halves(dsig * factor), wz[:, :C])
            z = early + (z[:8] + z[8:])
            uv[b, 0:8, 0:512] = z[:, :512]
            uv[b, 8:16, 0:384] = z[:, 512:]
            uv[b, 8:16, 384:512] = jnp.zeros((A, C), F32)

    def spread_back(b, k):
        c0, n = CHUNKS[k]
        radial = geo[b, RAD]
        if k:
            rc, rs = radial * geo[b, (C1, C2)[k - 1]], radial * geo[b, (S1, S2)[k - 1]]
        for t in range(n // C):
            at = slice(c0 + t * C, c0 + (t + 1) * C)
            u, v = uv[b, 0:8, at], uv[b, 8:16, at]
            if k:
                upper, lower = rc * u + rs * v, rc * v - rs * u
            else:
                upper, lower = radial * u, radial * v
            dmat[:, at] = jnp.concatenate([upper, lower], axis=1).reshape(NEIGH * 16, C).astype(BF16)
        spread = dot(gtr[b], dmat[:, c0 : c0 + n])
        hsend[b, 1 - core, :, c0 : c0 + n] = spread[0:16].astype(BF16)
        hsend[b, core, :, c0 : c0 + n] = spread[32:48].astype(BF16)
        ownsum[b, :, c0 : c0 + n] = spread[16:32] + du[b, :, c0 : c0 + n]
    def send_back(b, k):
        back_far_copy(b, k).start()
        back_near_copy(b, k).start()

    def combine(b):
        for k in range(3):
            back_near_copy(b, k).wait_recv()
            total = ownsum.at[b, :, cols(k)]
            total[...] += hrecv[b, :, cols(k)].astype(F32)
            if k < max(DIRECT_MIDDLE, DIRECT_END):

                @pl.when(jnp.logical_not(straight(k)))
                def _():
                    back_far_copy(b, k).wait_recv()
                    total[...] += ctfar[b, :, cols(k)].astype(F32)

            ysend[b, :, cols(k)] = total[...].astype(BF16)
            down_copy(b, k).start()

    def coordinates(b):
        edge = [jnp.zeros((NEIGH, A, C), F32) for _ in range(3)]
        turn = [None, jnp.zeros((NEIGH, A, C), F32), jnp.zeros((NEIGH, A, C), F32)]
        for k in range(3):
            c0, n = CHUNKS[k]
            for t in range(n // C):
                at = slice(c0 + t * C, c0 + (t + 1) * C)
                part = scaled[b, :, at].astype(F32).reshape(NEIGH, 16, C)
                re, im = part[:, :A], part[:, A:]
                u, v = uv[b, 0:8, at], uv[b, 8:16, at]
                edge[k] = edge[k] + (re * u + im * v)
                if k:
                    turn[k] = turn[k] + (re * v - im * u)
        c1, s1, c2, s2 = geo[b, C1], geo[b, S1], geo[b, C2], geo[b, S2]
        weighted = edge[0] + c1 * edge[1] + s1 * turn[1] + c2 * edge[2] + s2 * turn[2]
        dlength = -jnp.sum(rate_row[None] * weighted, axis=2, keepdims=True)
        dc2 = jnp.sum(edge[2], axis=2, keepdims=True)
        ds2 = jnp.sum(turn[2], axis=2, keepdims=True)
        dc1 = jnp.sum(edge[1], axis=2, keepdims=True) + 2.0 * (c1 * dc2 + s1 * ds2)
        ds1 = jnp.sum(turn[1], axis=2, keepdims=True) + 2.0 * (c1 * ds2 - s1 * dc2)
        along = dc1 * c1 + ds1 * s1
        planar = geo[b, PLANAR]
        grads = (
            (dc1 - along * c1) / planar + dlength * geo[b, LX],
            (ds1 - along * s1) / planar + dlength * geo[b, LY],
            dlength * geo[b, LZ],
        )
        where = mask[b] - ownmask[None]
        for axis in range(3):
            ftile[b * 3 + axis : b * 3 + axis + 1, :] = jnp.sum(
                jnp.sum(where * grads[axis], axis=0), axis=0, keepdims=True
            )

    def backward(b, spreads, ends=True):
        with scope(f"bhead{b}"):
            dsig, gate, early = backward_head(b)
        if spreads:
            with scope(f"b{b}0"):
                mix_back(b, 0, dsig, gate, early)
                mix_back(b, 1, dsig, gate, early)
                spread_back(b, 0)
            send_back(b, 0)
            if not ends:
                with scope("relay1m"):
                    relay(1, LATE, seg == last)
            with scope(f"b{b}1"):
                mix_back(b, 2, dsig, gate, early)
                spread_back(b, 1)
            send_back(b, 1)
            with scope(f"b{b}2"):
                spread_back(b, 2)
            send_back(b, 2)
        else:
            with scope(f"b{b}first"):
                for k in range(3):
                    mix_back(b, k, dsig, gate, early)
        with scope(f"coord{b}"):
            coordinates(b)
        if spreads and ends:
            with scope(f"comb{b}"):
                combine(b)

    with scope("relay0"):
        relay(0, range(3), seg > 0)
    forward(0)

    with scope("relay1l"):
        relay(1, LATE, (seg > 1) & (seg < last))
        relay(1, EARLY, seg == last)

    @pl.when(seg == last)
    def _():
        backward(0, True, False)

    forward(1)

    @pl.when((seg > 0) & (seg < last))
    def _():
        backward(0, True)

    @pl.when(seg == 0)
    def _():
        backward(0, False)
        backward(1, False)

    @pl.when(seg > 0)
    def _():
        backward(1, True)

    with scope("final"):
        for step, kind in ends:
            end_copy(step, kind).start()
        grecv[seg, 1] = ftile[...]
        for step, kind in ends:
            end_copy(step, kind).wait_recv()
    totals = []
    for slot in range(3):
        total = grecv[0, slot]
        for other in range(1, segments):
            total = total + grecv[other, slot]
        totals.append(total)
    result = totals[1] + jnp.where(row < 6, pltpu.roll(totals[0], C - A, 1) + pltpu.roll(totals[2], A, 1), 0.0)
    result = pltpu.roll(result, C - A, 1)
    for axis in range(3):
        for b in range(BATCHES):
            out_p[axis, b : b + 1] = result[b * 3 + axis : b * 3 + axis + 1, 0:A]
    out_e[...] = result[6:8, 0:A]

    with scope("drain"):
        for kind in range(2):
            place_copy(kind).wait_send()
        for step, kind in ends:
            end_copy(step, kind).wait_send()
        for b in range(BATCHES):
            for k in range(3):
                near_copy(b, k).wait_send()

        @pl.when((seg == 0) | inner)
        def _():
            for b in range(BATCHES):
                for k in range(3):
                    first_copy(b, k).wait_send()

        @pl.when(seg < last)
        def _():
            for b in range(BATCHES):
                for k in range(3):
                    up_copy(b, k).wait_send()
                    pl.when(cross)(far_copy(b, k).wait_send)

        @pl.when(seg > 0)
        def _():
            for b in range(BATCHES):
                for k in range(3):
                    down_copy(b, k).wait_send()
                    back_near_copy(b, k).wait_send()
                    back_far_copy(b, k).wait_send()


def solution(mesh):
    segments = mesh.shape["segment"]
    vmem = pl.BlockSpec(memory_space=pltpu.VMEM)
    hbm = pl.BlockSpec(memory_space=pltpu.HBM)
    dma = pltpu.SemaphoreType.DMA
    B = BATCHES

    def on_device(
        node_states, species, species_table, places, sources, radial_rate, zero_weight, one_weight, two_weight,
        read_weight, energy_grad,
    ):
        energies, grads = pl.pallas_call(
            kernel,
            out_shape=(
                jax.ShapeDtypeStruct((B, A), F32),
                jax.ShapeDtypeStruct((3, B, A), F32),
            ),
            in_specs=[hbm] * 11,
            out_specs=(vmem, vmem),
            scratch_shapes=[
                pltpu.VMEM((3, B, A), F32),
                pltpu.VMEM((B, A), F32),
                pltpu.VMEM((B, 29, A, C), BF16),
                pltpu.VMEM((B, A), jnp.int32),
                pltpu.VMEM(species_table.shape, BF16),
                pltpu.VMEM((B, A, NEIGH), jnp.int32),
                pltpu.VMEM((1, C), F32),
                pltpu.VMEM((1, C), F32),
                pltpu.VMEM((7 * C, 7 * C), BF16),
                pltpu.VMEM((2, 6 * C, 6 * C), BF16),
                pltpu.VMEM((2, 5 * C, 5 * C), BF16),
                pltpu.VMEM((B, 3, 16, WIDTH), BF16),
                pltpu.VMEM((B, 16, WIDTH), BF16),
                pltpu.VMEM((B, NEIGH * 16, WIDTH), BF16),
                pltpu.VMEM((B, 16, WIDTH), F32),
                pltpu.VMEM((B, A, C), F32),
                pltpu.VMEM((B, A, C), F32),
                pltpu.VMEM((B, NEIGH * 16, 48), BF16),
                pltpu.VMEM((B, 48, NEIGH * 16), BF16),
                pltpu.VMEM((B, NEIGH, A, C), F32),
                pltpu.VMEM((B, 9, NEIGH, A, C), F32),
                pltpu.VMEM((B, 16, WIDTH), BF16),
                pltpu.VMEM((B, 16, WIDTH), F32),
                pltpu.VMEM((B, 16, WIDTH), F32),
                pltpu.VMEM((NEIGH * 16, WIDTH), BF16),
                pltpu.VMEM((B, 16, WIDTH), F32),
                pltpu.VMEM((B, 2, 16, WIDTH), BF16),
                pltpu.VMEM((B, 16, WIDTH), BF16),
                pltpu.VMEM((B, 16, WIDTH), BF16),
                pltpu.VMEM((B, 16, WIDTH), BF16),
                pltpu.VMEM((3, A, C), F32),
                pltpu.VMEM((3, A, C), F32),
                pltpu.VMEM((A, C), F32),
                pltpu.VMEM((segments, 3, A, C), F32),
                dma((11,)),
                dma((2,)),
                dma((2,)),
                *[dma((B, 3))] * 13,
                dma((segments, 3)),
                dma((segments, 3)),
            ],
            compiler_params=pltpu.CompilerParams(
                collective_id=0, has_side_effects=True, vmem_limit_bytes=67043328
            ),
        )(
            places.transpose(1, 0, 2), energy_grad, node_states.transpose(0, 2, 1, 3), species, species_table, sources,
            radial_rate, read_weight.reshape(1, C), zero_weight, one_weight, two_weight,
        )
        return energies, grads.transpose(1, 0, 2)

    in_specs = (
        P(None, "space", None, None),
        P(None, "space"),
        P(),
        P(None, None, "space"),
        P(None, "space", None),
        P("segment", None),
        P("segment", None, None),
        P("segment", None, None, None),
        P("segment", None, None, None),
        P(),
        P(None, "space"),
    )
    out_specs = (P(None, "space"), P(None, None, "space"))
    return jax.shard_map(on_device, mesh=mesh, in_specs=in_specs, out_specs=out_specs, check_vma=False)
```

```python
import contextlib
import jax
import jax.numpy as jnp
from jax import lax
from jax.experimental import pallas as pl
from jax.experimental.pallas import tpu as pltpu
from jax.sharding import PartitionSpec as P

A = 8
NEIGH = 8
C = 128
BATCHES = 2
SLAB_DEPTH = 2.0
ROW = 8
MESH = pl.DeviceIdType.MESH
F32 = jnp.float32
BF16 = jnp.bfloat16

CHUNKS = ((0, 512), (512, 768), (1280, 640))
WIDTH = 1920
UPPER = (0, 1, 2, 3, 7, 8, 9, 10, 11, 12, 19, 20, 21, 22, 23)
LOWER = (4, 5, 6, None, 13, 14, 15, 16, 17, 18, 24, 25, 26, 27, 28)
SCOPES = False
DIRECT_MIDDLE = 0
DIRECT_END = 0
EARLY, LATE = (0, 1), (2,)
RAD, C1, S1, C2, S2, LX, LY, LZ, PLANAR = range(9)


def dot(x, y):
    return lax.dot_general(x, y, (((1,), (0,)), ((), ())), preferred_element_type=F32)


def dot_t(x, y):
    return lax.dot_general(x, y, (((1,), (1,)), ((), ())), preferred_element_type=F32)


def scope(name):
    return jax.named_scope(name) if SCOPES else contextlib.nullcontext()


def halves(x):
    high = x.astype(BF16).astype(F32)
    return jnp.concatenate([high, x - high], axis=0).astype(BF16)


def kernel(
    places_hbm, egrad_hbm, node_hbm, species_hbm, table_hbm, sources_hbm, rate_hbm, read_hbm, wz_hbm, w1_hbm, w2_hbm,
    out_e, out_p,
    places, egrad, node, species, table, sources, rate, read, wz, w1, w2, ext, yout, scaled, pooled, signal, last_top, gmat, gtr, mask, geo, ct, du, uv, dmat,
    ownsum, hsend, hrecv, ctfar, ysend, ptile, precv, ftile, grecv,
    isem, psem_s, psem_r, f0_s, fn_s, fn_r, ff_s, ff_r, fy_s, fy_r, bn_s, bn_r, bf_s, bf_r, by_s, by_r, e_s, e_r,
):
    seg = lax.axis_index("segment")
    slab = lax.axis_index("space")
    segments = lax.axis_size("segment")
    slabs = lax.axis_size("space")
    core = lax.rem(slab, 2)
    near = slab + 1 - 2 * core
    far = lax.rem(slab + slabs + 2 * core - 1, slabs)
    near_slot = 2 * core
    far_slot = 2 - 2 * core
    row_of_slabs = min(ROW, slabs)
    place_in_row = lax.rem(slab, row_of_slabs)
    place_in_half = lax.rem(slab, max(slabs // 2, row_of_slabs))
    cross = (place_in_half == 0) | (place_in_half == max(slabs // 2, row_of_slabs) - 1)
    inner = jnp.logical_not(cross)
    last = segments - 1
    up = lax.rem(seg + 1, segments)
    down = lax.rem(seg + segments - 1, segments)
    factor = NEIGH ** (-0.5)
    lane = lax.broadcasted_iota(jnp.int32, (A, C), 1)
    row = lax.broadcasted_iota(jnp.int32, (A, C), 0)
    ownmask = jnp.where(lane == row + A, 1.0, 0.0).astype(F32)

    inputs = (
        (places_hbm, places), (egrad_hbm, egrad), (node_hbm, node), (species_hbm, species), (table_hbm, table),
        (sources_hbm, sources), (rate_hbm, rate), (read_hbm, read), (wz_hbm.at[0], wz), (w1_hbm.at[0], w1),
        (w2_hbm.at[0], w2),
    )
    inputs = [pltpu.make_async_copy(src, dst, isem.at[i]) for i, (src, dst) in enumerate(inputs)]
    loads = inputs[8:]
    for load in inputs:
        load.start()

    barrier = pltpu.get_barrier_semaphore()
    for target in (near, far):
        pl.semaphore_signal(barrier, inc=1, device_id={"space": target}, device_id_type=MESH)

    @pl.when(seg > 0)
    def _():
        pl.semaphore_signal(barrier, inc=1, device_id={"segment": down}, device_id_type=MESH)

    @pl.when(seg < last)
    def _():
        pl.semaphore_signal(barrier, inc=1, device_id={"segment": up}, device_id_type=MESH)

    greeted = 2 + jnp.minimum(seg, 1) + jnp.minimum(last - seg, 1)

    def remote(src, dst, send, recv, target):
        return pltpu.make_async_remote_copy(
            src_ref=src, dst_ref=dst, send_sem=send, recv_sem=recv, device_id=target, device_id_type=MESH
        )

    def cols(k):
        return pl.ds(CHUNKS[k][0], CHUNKS[k][1])

    def place_copy(kind):
        return remote(
            ptile.at[(far_slot, near_slot)[kind]], precv.at[(far_slot, near_slot)[kind]],
            psem_s.at[kind], psem_r.at[kind], {"space": (far, near)[kind]},
        )

    def near_copy(b, k):
        return remote(
            ext.at[b, 1, :, cols(k)], ext.at[b, near_slot, :, cols(k)], fn_s.at[b, k], fn_r.at[b, k], {"space": near}
        )

    def first_copy(b, k):
        return remote(
            ext.at[b, 1, :, cols(k)], ext.at[b, far_slot, :, cols(k)], f0_s.at[b, k], ff_r.at[b, k], {"space": far}
        )

    def far_copy(b, k):
        return remote(
            yout.at[b, :, cols(k)], ext.at[b, far_slot, :, cols(k)], ff_s.at[b, k], ff_r.at[b, k],
            {"segment": up, "space": far},
        )

    def up_copy(b, k):
        return remote(
            yout.at[b, :, cols(k)], ext.at[b, 1, :, cols(k)], fy_s.at[b, k], fy_r.at[b, k], {"segment": up}
        )

    def back_near_copy(b, k):
        return remote(
            hsend.at[b, 0, :, cols(k)], hrecv.at[b, :, cols(k)], bn_s.at[b, k], bn_r.at[b, k], {"space": near}
        )

    middle = (place_in_row == row_of_slabs // 2) | (place_in_row == row_of_slabs // 2 - 1)
    bound = jnp.where(cross, 0, jnp.where(middle, DIRECT_MIDDLE, DIRECT_END))

    def straight(k):
        return k >= bound

    def back_far_copy(b, k):
        return remote(
            hsend.at[b, 1, :, cols(k)], ctfar.at[b, :, cols(k)], bf_s.at[b, k], bf_r.at[b, k],
            {"segment": jnp.where(straight(k), down, seg), "space": far},
        )

    def down_copy(b, k):
        return remote(
            ysend.at[b, :, cols(k)], ct.at[b, :, cols(k)], by_s.at[b, k], by_r.at[b, k], {"segment": down}
        )

    def end_copy(step, kind):
        return remote(
            ftile, grecv.at[seg, (far_slot, near_slot, 1)[kind]], e_s.at[step, kind], e_r.at[step, kind],
            {"segment": lax.rem(seg + step, segments), "space": (far, near, slab)[kind]},
        )

    ends = [(step, kind) for step in range(segments) for kind in range(3) if step or kind < 2]

    ptile[1] = jnp.zeros((A, C), F32)
    with scope("input"):
        for load in inputs[:8]:
            load.wait()
    for axis in range(3):
        for b in range(BATCHES):
            ptile[1, b * 3 + axis : b * 3 + axis + 1, 0:A] = places[axis, b : b + 1]
    ptile[1, 6:8, 0:A] = egrad[...]
    base = ptile[1]
    ptile[0] = base
    ptile[2] = pltpu.roll(base, 16, 1)
    own_tile = pltpu.roll(base, A, 1)

    def make_start(b):
        kind = jnp.sum(
            jnp.where(lane == row, jnp.broadcast_to(spec_tile[b : b + 1], (A, C)), 0.0), axis=1, keepdims=True
        )
        onehot = jnp.where(lane.astype(F32) == kind, 1.0, 0.0).astype(BF16)
        embed = dot(onehot[:, : table.shape[0]], table[...])
        for t in range(15):
            upper = node[b, UPPER[t]].astype(F32)
            if t == 0:
                upper = upper + embed
            if LOWER[t] is None:
                lower = jnp.zeros((A, C), F32)
            else:
                lower = node[b, LOWER[t]].astype(F32)
            ext[b, 1, :, t * C : (t + 1) * C] = jnp.concatenate([upper, lower], axis=0).astype(BF16)

    spec_tile = jnp.concatenate(
        [species[...].astype(F32), jnp.zeros((BATCHES, C - A), F32)], axis=1
    )

    with scope("start"):

        @pl.when(seg == 0)
        def _():
            for b in range(BATCHES):
                make_start(b)

    with scope("barrier"):
        pl.semaphore_wait(barrier, greeted)

    for kind in range(2):
        place_copy(kind).start()

    @pl.when(seg == 0)
    def _():
        for b in range(BATCHES):
            for k in range(3):
                first_copy(b, k).start()
                near_copy(b, k).start()

    lane3 = lax.broadcasted_iota(jnp.int32, (NEIGH, A, C), 2)
    lane_local = (lane3 >> 4) * A + (lane3 & 7)
    lane_part = (lane3 >> 3) & 1

    def make_index(b):
        index = sources[b]
        window = (index >> 3) - slab + 1
        window = jnp.where(window < 0, window + slabs, window)
        window = jnp.where(window >= slabs, window - slabs, window)
        local = window * A + (index & 7)
        local = jnp.concatenate([jnp.broadcast_to(local[:, j : j + 1], (A, C))[None] for j in range(NEIGH)], axis=0)
        mask[b] = jnp.where(local == lane3, 1.0, 0.0).astype(F32)
        same = local == lane_local
        picks = jnp.concatenate(
            [
                jnp.where(same & (lane_part == 0), 1.0, 0.0).astype(F32),
                jnp.where(same & (lane_part == 1), 1.0, 0.0).astype(F32),
            ],
            axis=1,
        ).reshape(2 * NEIGH * A, C)
        gmat[b] = picks[:, :48].astype(BF16)
        gtr[b] = picks.T[:48].astype(BF16)

    with scope("index"):
        for b in range(BATCHES):
            make_index(b)

    with scope("places"):
        for kind in range(2):
            place_copy(kind).wait_recv()
    around = precv[0] + own_tile + precv[2]
    elevation = jnp.where(lane < A, -SLAB_DEPTH, jnp.where(lane < 2 * A, 0.0, SLAB_DEPTH)).astype(F32)[0:1]
    rate_row = rate[...]

    def make_geometry(b):
        picks = mask[b]
        offsets = []
        for axis in range(3):
            line = around[b * 3 + axis : b * 3 + axis + 1]
            raised = line + elevation if axis == 2 else line
            there = jnp.sum(picks * raised[None], axis=2, keepdims=True)
            here = jnp.sum(ownmask * line, axis=1, keepdims=True)
            offsets.append(jnp.broadcast_to(there - here[None], (NEIGH, A, C)))
        ox, oy, oz = offsets
        length = jnp.sqrt(ox * ox + oy * oy + oz * oz + 1.0)
        planar = jnp.sqrt(ox * ox + oy * oy + 1.0)
        c1 = ox / planar
        s1 = oy / planar
        geo[b, RAD] = jnp.exp(-rate_row[None] * length)
        geo[b, C1] = c1
        geo[b, S1] = s1
        geo[b, C2] = c1 * c1 - s1 * s1
        geo[b, S2] = 2.0 * c1 * s1
        geo[b, LX] = ox / length
        geo[b, LY] = oy / length
        geo[b, LZ] = oz / length
        geo[b, PLANAR] = planar

    with scope("geometry"):
        for b in range(BATCHES):
            make_geometry(b)

    weights = (None, w1, w2)

    def relay(b, group, where):
        @pl.when(where)
        def _():
            for k in group:
                up_copy(b, k).wait_recv()
                pl.when(inner)(first_copy(b, k).start)
                near_copy(b, k).start()

    def gather(b, k):
        c0, n = CHUNKS[k]
        with scope(f"fwait{b}{k}"):
            near_copy(b, k).wait_recv()
            far_copy(b, k).wait_recv()
        picked = dot(gmat[b], ext[b, :, :, c0 : c0 + n].reshape(48, n))
        radial = geo[b, RAD]
        radial = jnp.concatenate([radial, radial], axis=1)
        if k:
            cos, sin = geo[b, (C1, C2)[k - 1]], geo[b, (S1, S2)[k - 1]]
        sums = []
        for t in range(n // C):
            part = picked[:, t * C : (t + 1) * C].reshape(NEIGH, 16, C)
            rounded = (part * radial).astype(BF16)
            scaled[b, :, c0 + t * C : c0 + (t + 1) * C] = rounded.reshape(NEIGH * 16, C)
            part = rounded.astype(F32)
            if k:
                re, im = part[:, :A], part[:, A:]
                sums.append(
                    jnp.concatenate(
                        [jnp.sum(cos * re - sin * im, axis=0), jnp.sum(sin * re + cos * im, axis=0)], axis=0
                    )
                )
            else:
                sums.append(jnp.sum(part, axis=0))
        return sums

    def mix(b, k, sums):
        c0, n = CHUNKS[k]
        if k:
            both = halves(jnp.concatenate(sums, axis=1))
            p = dot(both, weights[k][0])
            q = dot(both, weights[k][1])
            p = p[:16] + p[16:]
            q = q[:16] + q[16:]
            pooled[b, 0:8, c0 : c0 + n] = (p[:8] - q[8:]) * factor
            pooled[b, 8:16, c0 : c0 + n] = (p[8:] + q[:8]) * factor
        else:
            whole = jnp.concatenate([x[:8] for x in sums] + [x[8:] for x in sums[:3]], axis=1)
            z = dot(halves(whole), wz[...])
            z = (z[:8] + z[8:]) * factor
            pooled[b, 0:8, 0:512] = z[:, :512]
            pooled[b, 8:16, 0:384] = z[:, 512:]
            pooled[b, 8:16, 384:512] = jnp.zeros((A, C), F32)

    def forward_end(b):
        total = jnp.zeros((16, C), F32)
        for t in range(4, 15):
            value = pooled[b, :, t * C : (t + 1) * C]
            total = total + value * value
        sig = pooled[b, 0:8, 0:C] + total[:8] + total[8:]
        signal[b] = sig
        gate = jax.nn.sigmoid(sig)
        silu = sig * gate
        gate2 = jnp.concatenate([gate, gate], axis=0)
        for t in range(15):
            own = ext[b, 1, :, t * C : (t + 1) * C].astype(F32)
            added = gate2 * pooled[b, :, t * C : (t + 1) * C]
            if t == 0:
                added = jnp.concatenate([silu, added[8:]], axis=0)
            new = own + added
            if t == 0:
                last_top[b] = new[:8]
            yout[b, :, t * C : (t + 1) * C] = new.astype(BF16)

        @pl.when(seg < last)
        def _():
            for k in range(3):
                pl.when(cross)(far_copy(b, k).start)
                up_copy(b, k).start()

    def forward(b):
        if b == 0:
            for load in loads:
                load.wait()
        with scope(f"f{b}0"):
            mix(b, 0, gather(b, 0))
        with scope(f"f{b}1"):
            sums = gather(b, 1)
        if b == 0:
            with scope("relay1"):
                relay(1, range(3), seg == 1)
                relay(1, EARLY, (seg > 1) & (seg < last))
        else:
            with scope("comb0"):

                @pl.when(seg == last)
                def _():
                    combine(0)

        with scope(f"f{b}2"):
            more = gather(b, 2)
            mix(b, 1, sums)
            mix(b, 2, more)
        with scope(f"fend{b}"):
            forward_end(b)

    read_row = read[...]

    def backward_head(b):
        @pl.when(seg == last)
        def _():
            top = last_top[b]
            gate = jax.nn.sigmoid(top)
            energy = jnp.sum(read_row * (top * gate), axis=1, keepdims=True)
            seed = jnp.sum(ownmask * own_tile[6 + b : 7 + b], axis=1, keepdims=True)
            ftile[6 + b : 7 + b, :] = jnp.sum(ownmask * energy, axis=0, keepdims=True)
            du[b] = jnp.zeros((16, WIDTH), F32)
            du[b, 0:8, 0:C] = seed * read_row * (gate * (1.0 + top * (1.0 - gate)))

        def take(group):
            for k in group:
                down_copy(b, k).wait_recv()
                du[b, :, cols(k)] = ct[b, :, cols(k)].astype(F32)

            for k in group:

                @pl.when(straight(k))
                def _():
                    back_far_copy(b, k).wait_recv()
                    du[b, :, cols(k)] += ctfar[b, :, cols(k)].astype(F32)

        @pl.when(seg < last)
        def _():
            ftile[6 + b : 7 + b, :] = jnp.zeros((1, C), F32)
            take((0,))

        sig = signal[b]
        gate = jax.nn.sigmoid(sig)
        rows = [gate * du[b, 0:8, t * C : (t + 1) * C] for t in range(1, 4)]
        rows += [gate * du[b, 8:16, t * C : (t + 1) * C] for t in range(3)]
        early = dot_t(halves(jnp.concatenate(rows, axis=1) * factor), wz[:, C:])
        early = early[:8] + early[8:]

        @pl.when(seg < last)
        def _():
            take((1, 2))

        total = jnp.zeros((16, C), F32)
        for t in range(15):
            value = du[b, :, t * C : (t + 1) * C] * pooled[b, :, t * C : (t + 1) * C]
            if t == 0:
                value = jnp.concatenate([jnp.zeros((A, C), F32), value[8:]], axis=0)
            total = total + value
        dgate = total[:8] + total[8:]
        dsig = du[b, 0:8, 0:C] * (gate * (1.0 + sig * (1.0 - gate))) + dgate * (gate * (1.0 - gate))
        return dsig, gate, early

    def mix_back(b, k, dsig, gate, early):
        c0, n = CHUNKS[k]
        gate2 = jnp.concatenate([gate, gate], axis=0)
        dsig2 = jnp.concatenate([dsig, dsig], axis=0)
        parts = []
        for t in range(n // C if k else 0):
            at = slice(c0 + t * C, c0 + (t + 1) * C)
            parts.append((gate2 * du[b, :, at] + 2.0 * pooled[b, :, at] * dsig2) * factor)
        if k:
            both = halves(jnp.concatenate(parts, axis=1))
            p = dot_t(both, weights[k][0])
            q = dot_t(both, weights[k][1])
            p = p[:16] + p[16:]
            q = q[:16] + q[16:]
            uv[b, 0:8, c0 : c0 + n] = p[:8] + q[8:]
            uv[b, 8:16, c0 : c0 + n] = p[8:] - q[:8]
        else:
            z = dot_t(halves(dsig * factor), wz[:, :C])
            z = early + (z[:8] + z[8:])
            uv[b, 0:8, 0:512] = z[:, :512]
            uv[b, 8:16, 0:384] = z[:, 512:]
            uv[b, 8:16, 384:512] = jnp.zeros((A, C), F32)

    def spread_back(b, k):
        c0, n = CHUNKS[k]
        radial = geo[b, RAD]
        if k:
            rc, rs = radial * geo[b, (C1, C2)[k - 1]], radial * geo[b, (S1, S2)[k - 1]]
        for t in range(n // C):
            at = slice(c0 + t * C, c0 + (t + 1) * C)
            u, v = uv[b, 0:8, at], uv[b, 8:16, at]
            if k:
                upper, lower = rc * u + rs * v, rc * v - rs * u
            else:
                upper, lower = radial * u, radial * v
            dmat[:, at] = jnp.concatenate([upper, lower], axis=1).reshape(NEIGH * 16, C).astype(BF16)
        spread = dot(gtr[b], dmat[:, c0 : c0 + n])
        hsend[b, 1 - core, :, c0 : c0 + n] = spread[0:16].astype(BF16)
        hsend[b, core, :, c0 : c0 + n] = spread[32:48].astype(BF16)
        ownsum[b, :, c0 : c0 + n] = spread[16:32] + du[b, :, c0 : c0 + n]
    def send_back(b, k):
        back_far_copy(b, k).start()
        back_near_copy(b, k).start()

    def combine(b):
        for k in range(3):
            back_near_copy(b, k).wait_recv()
            total = ownsum.at[b, :, cols(k)]
            total[...] += hrecv[b, :, cols(k)].astype(F32)
            if k < max(DIRECT_MIDDLE, DIRECT_END):

                @pl.when(jnp.logical_not(straight(k)))
                def _():
                    back_far_copy(b, k).wait_recv()
                    total[...] += ctfar[b, :, cols(k)].astype(F32)

            ysend[b, :, cols(k)] = total[...].astype(BF16)
            down_copy(b, k).start()

    def coordinates(b):
        edge = [jnp.zeros((NEIGH, A, C), F32) for _ in range(3)]
        turn = [None, jnp.zeros((NEIGH, A, C), F32), jnp.zeros((NEIGH, A, C), F32)]
        for k in range(3):
            c0, n = CHUNKS[k]
            for t in range(n // C):
                at = slice(c0 + t * C, c0 + (t + 1) * C)
                part = scaled[b, :, at].astype(F32).reshape(NEIGH, 16, C)
                re, im = part[:, :A], part[:, A:]
                u, v = uv[b, 0:8, at], uv[b, 8:16, at]
                edge[k] = edge[k] + (re * u + im * v)
                if k:
                    turn[k] = turn[k] + (re * v - im * u)
        c1, s1, c2, s2 = geo[b, C1], geo[b, S1], geo[b, C2], geo[b, S2]
        weighted = edge[0] + c1 * edge[1] + s1 * turn[1] + c2 * edge[2] + s2 * turn[2]
        dlength = -jnp.sum(rate_row[None] * weighted, axis=2, keepdims=True)
        dc2 = jnp.sum(edge[2], axis=2, keepdims=True)
        ds2 = jnp.sum(turn[2], axis=2, keepdims=True)
        dc1 = jnp.sum(edge[1], axis=2, keepdims=True) + 2.0 * (c1 * dc2 + s1 * ds2)
        ds1 = jnp.sum(turn[1], axis=2, keepdims=True) + 2.0 * (c1 * ds2 - s1 * dc2)
        along = dc1 * c1 + ds1 * s1
        planar = geo[b, PLANAR]
        grads = (
            (dc1 - along * c1) / planar + dlength * geo[b, LX],
            (ds1 - along * s1) / planar + dlength * geo[b, LY],
            dlength * geo[b, LZ],
        )
        where = mask[b] - ownmask[None]
        for axis in range(3):
            ftile[b * 3 + axis : b * 3 + axis + 1, :] = jnp.sum(
                jnp.sum(where * grads[axis], axis=0), axis=0, keepdims=True
            )

    def backward(b, spreads, ends=True):
        with scope(f"bhead{b}"):
            dsig, gate, early = backward_head(b)
        if spreads:
            with scope(f"b{b}0"):
                mix_back(b, 0, dsig, gate, early)
                mix_back(b, 1, dsig, gate, early)
                spread_back(b, 0)
            send_back(b, 0)
            if not ends:
                with scope("relay1m"):
                    relay(1, LATE, seg == last)
            with scope(f"b{b}1"):
                mix_back(b, 2, dsig, gate, early)
                spread_back(b, 1)
            send_back(b, 1)
            with scope(f"b{b}2"):
                spread_back(b, 2)
            send_back(b, 2)
        else:
            with scope(f"b{b}first"):
                for k in range(3):
                    mix_back(b, k, dsig, gate, early)
        with scope(f"coord{b}"):
            coordinates(b)
        if spreads and ends:
            with scope(f"comb{b}"):
                combine(b)

    with scope("relay0"):
        relay(0, range(3), seg > 0)
    forward(0)

    with scope("relay1l"):
        relay(1, LATE, (seg > 1) & (seg < last))
        relay(1, EARLY, seg == last)

    @pl.when(seg == last)
    def _():
        backward(0, True, False)

    forward(1)

    @pl.when((seg > 0) & (seg < last))
    def _():
        backward(0, True)

    @pl.when(seg == 0)
    def _():
        backward(0, False)
        backward(1, False)

    @pl.when(seg > 0)
    def _():
        backward(1, True)

    with scope("final"):
        for step, kind in ends:
            end_copy(step, kind).start()
        grecv[seg, 1] = ftile[...]
        for step, kind in ends:
            end_copy(step, kind).wait_recv()
    totals = []
    for slot in range(3):
        total = grecv[0, slot]
        for other in range(1, segments):
            total = total + grecv[other, slot]
        totals.append(total)
    result = totals[1] + jnp.where(row < 6, pltpu.roll(totals[0], C - A, 1) + pltpu.roll(totals[2], A, 1), 0.0)
    result = pltpu.roll(result, C - A, 1)
    for axis in range(3):
        for b in range(BATCHES):
            out_p[axis, b : b + 1] = result[b * 3 + axis : b * 3 + axis + 1, 0:A]
    out_e[...] = result[6:8, 0:A]

    with scope("drain"):
        for kind in range(2):
            place_copy(kind).wait_send()
        for step, kind in ends:
            end_copy(step, kind).wait_send()
        for b in range(BATCHES):
            for k in range(3):
                near_copy(b, k).wait_send()

        @pl.when((seg == 0) | inner)
        def _():
            for b in range(BATCHES):
                for k in range(3):
                    first_copy(b, k).wait_send()

        @pl.when(seg < last)
        def _():
            for b in range(BATCHES):
                for k in range(3):
                    up_copy(b, k).wait_send()
                    pl.when(cross)(far_copy(b, k).wait_send)

        @pl.when(seg > 0)
        def _():
            for b in range(BATCHES):
                for k in range(3):
                    down_copy(b, k).wait_send()
                    back_near_copy(b, k).wait_send()
                    back_far_copy(b, k).wait_send()


def solution(mesh):
    segments = mesh.shape["segment"]
    vmem = pl.BlockSpec(memory_space=pltpu.VMEM)
    hbm = pl.BlockSpec(memory_space=pltpu.HBM)
    dma = pltpu.SemaphoreType.DMA
    B = BATCHES

    def on_device(
        node_states, species, species_table, places, sources, radial_rate, zero_weight, one_weight, two_weight,
        read_weight, energy_grad,
    ):
        energies, grads = pl.pallas_call(
            kernel,
            out_shape=(
                jax.ShapeDtypeStruct((B, A), F32),
                jax.ShapeDtypeStruct((3, B, A), F32),
            ),
            in_specs=[hbm] * 11,
            out_specs=(vmem, vmem),
            scratch_shapes=[
                pltpu.VMEM((3, B, A), F32),
                pltpu.VMEM((B, A), F32),
                pltpu.VMEM((B, 29, A, C), BF16),
                pltpu.VMEM((B, A), jnp.int32),
                pltpu.VMEM(species_table.shape, BF16),
                pltpu.VMEM((B, A, NEIGH), jnp.int32),
                pltpu.VMEM((1, C), F32),
                pltpu.VMEM((1, C), F32),
                pltpu.VMEM((7 * C, 7 * C), BF16),
                pltpu.VMEM((2, 6 * C, 6 * C), BF16),
                pltpu.VMEM((2, 5 * C, 5 * C), BF16),
                pltpu.VMEM((B, 3, 16, WIDTH), BF16),
                pltpu.VMEM((B, 16, WIDTH), BF16),
                pltpu.VMEM((B, NEIGH * 16, WIDTH), BF16),
                pltpu.VMEM((B, 16, WIDTH), F32),
                pltpu.VMEM((B, A, C), F32),
                pltpu.VMEM((B, A, C), F32),
                pltpu.VMEM((B, NEIGH * 16, 48), BF16),
                pltpu.VMEM((B, 48, NEIGH * 16), BF16),
                pltpu.VMEM((B, NEIGH, A, C), F32),
                pltpu.VMEM((B, 9, NEIGH, A, C), F32),
                pltpu.VMEM((B, 16, WIDTH), BF16),
                pltpu.VMEM((B, 16, WIDTH), F32),
                pltpu.VMEM((B, 16, WIDTH), F32),
                pltpu.VMEM((NEIGH * 16, WIDTH), BF16),
                pltpu.VMEM((B, 16, WIDTH), F32),
                pltpu.VMEM((B, 2, 16, WIDTH), BF16),
                pltpu.VMEM((B, 16, WIDTH), BF16),
                pltpu.VMEM((B, 16, WIDTH), BF16),
                pltpu.VMEM((B, 16, WIDTH), BF16),
                pltpu.VMEM((3, A, C), F32),
                pltpu.VMEM((3, A, C), F32),
                pltpu.VMEM((A, C), F32),
                pltpu.VMEM((segments, 3, A, C), F32),
                dma((11,)),
                dma((2,)),
                dma((2,)),
                *[dma((B, 3))] * 13,
                dma((segments, 3)),
                dma((segments, 3)),
            ],
            compiler_params=pltpu.CompilerParams(
                collective_id=0, has_side_effects=True, vmem_limit_bytes=67043328
            ),
        )(
            places.transpose(1, 0, 2), energy_grad, node_states.transpose(0, 2, 1, 3), species, species_table, sources,
            radial_rate, read_weight.reshape(1, C), zero_weight, one_weight, two_weight,
        )
        return energies, grads.transpose(1, 0, 2)

    in_specs = (
        P(None, "space", None, None),
        P(None, "space"),
        P(),
        P(None, None, "space"),
        P(None, "space", None),
        P("segment", None),
        P("segment", None, None),
        P("segment", None, None, None),
        P("segment", None, None, None),
        P(),
        P(None, "space"),
    )
    out_specs = (P(None, "space"), P(None, None, "space"))
    return jax.shard_map(on_device, mesh=mesh, in_specs=in_specs, out_specs=out_specs, check_vma=False)
```
